32 devices in a mesh: rows: 32 (over z, y, x, core).
Axes of the slice: x: 2, y: 2, z: 4, core: 2. Of those that a mesh axis runs over, the one named last changes fastest.
Arguments:
- inputs: bfloat16 [32768, 768], P('rows'), may hold values from -6 to 6
- context_count: int32 [32], P('rows'), may hold values from 64 to 768, as said below
- query_count: int32 [32], P('rows'), may hold values from 1 to 256, as said below
- row_mask: int32 [32768], P('rows'), may hold values 0 or 1
- ln1_gain: float32 [768], replicated, may hold values from 0.25 to 1.75
- ln1_bias: float32 [768], replicated, may hold values from -3 to 3
- w_qkv: bfloat16 [768, 2304], replicated, may hold values from -0.21875 to 0.21875
- w_out: bfloat16 [768, 768], replicated, may hold values from -2 to 2
- ln2_gain: float32 [768], replicated, may hold values from 0.25 to 1.75
- ln2_bias: float32 [768], replicated, may hold values from -3 to 3
- w_up: bfloat16 [768, 3072], replicated, may hold values from -0.21875 to 0.21875
- w_down: bfloat16 [3072, 768], replicated, may hold values from -0.109375 to 0.109375
- cotangent: bfloat16 [32768, 768], P('rows'), may hold values from -6 to 6
Outputs:
- layer_out: bfloat16 [32768, 768], P('rows')
- grad_inputs: float32 [32768, 768], P('rows')
- grad_ln1_gain: float32 [768], replicated
- grad_ln1_bias: float32 [768], replicated
- grad_qkv: float32 [768, 2304], replicated
- grad_out: float32 [768, 768], replicated
- grad_ln2_gain: float32 [768], replicated
- grad_ln2_bias: float32 [768], replicated
- grad_up: float32 [768, 3072], P(None, 'rows')
- grad_down: float32 [3072, 768], P('rows')
The draws below stay inside these ranges and needn't reach their ends.
Inputs may be any that keep to these rules, and one draw needn't show every extreme that they name: `context_count`: context rows of each table; in every draw some table has exactly 768 and some exactly 64. `query_count`: query rows of each table; in every draw some table has exactly 256.
All inputs are finite; a program needn't handle non-finite values. No bound on the sum of `row_mask` on one device may be relied on, other than what follows from the above.
Results may differ from the reference program's by a relative error of at most 0.0096.
Values sent between devices are 32-bit elements; how exact they have to be, the bound alone decides.
No kernel may reach another device: no remote copies, remote signals or barrier semaphores. Data moves between devices by JAX's collectives and lax.ppermute only.
A program may use at most 256 MiB of HBM per device.

```python
import math
from functools import partial
import jax
import jax.numpy as jnp
from jax import lax

D = 768
HEADS = 12
HEAD = 64
FF = 3072
SLOT = 1024
CTX_LEAST = 64
KEYS = 768
QUERY_MOST = 256
TABLES = 32
ROWS_ALL = 32768


def draw_context_count(key, part):
    counts = jax.random.randint(jax.random.fold_in(key, 11), (TABLES,), CTX_LEAST, KEYS + 1)
    order = jax.random.permutation(jax.random.fold_in(key, 12), TABLES)
    counts = counts.at[order[0]].set(KEYS)
    counts = counts.at[order[1]].set(CTX_LEAST)
    return counts.astype(jnp.int32)


def draw_query_count(key, part):
    counts = jax.random.randint(jax.random.fold_in(key, 21), (TABLES,), 1, QUERY_MOST + 1)
    order = jax.random.permutation(jax.random.fold_in(key, 22), TABLES)
    counts = counts.at[order[0]].set(QUERY_MOST)
    return counts.astype(jnp.int32)


def plant(drawn, own_key, least, high):
    shape = drawn.shape
    index_at = [jax.random.randint(jax.random.fold_in(own_key, axis), (), 0, shape[axis]) for axis in range(len(shape))]
    drawn = drawn.at[tuple(index_at)].set(least)
    longest = shape.index(max(shape))
    index_at[longest] = (index_at[longest] + 1) % shape[longest]
    return drawn.at[tuple(index_at)].set(high)


def levels(key, extent, pieces, smallest, top_value):
    loudness = 1.0
    for position, blocks in pieces:
        heights = jax.random.uniform(jax.random.fold_in(jax.random.fold_in(key, 6), position), (blocks,), jnp.float32, smallest / len(pieces), top_value / len(pieces))
        loudness = loudness * jnp.repeat(jnp.exp(heights), extent[position] // blocks).reshape((-1,) + (1,) * (len(extent) - 1 - position))
    return loudness


def gaussian(key, extent, deviation, bound, cuts=(), kind=jnp.bfloat16):
    array = jax.random.normal(key, extent, jnp.float32) * deviation
    if len(cuts) > 0:
        array = levels(key, extent, cuts, -0.22, 0.18) * array
    return jnp.clip(array, min=-bound, max=bound).astype(kind)


def setup_inputs(seed: int = 0) -> dict:
    arg_keys = jax.random.split(jax.random.key(seed), 14)
    inputs = gaussian(arg_keys[0], (ROWS_ALL, D), 1.0, 6.0, ((0, 32),))
    context_count = draw_context_count(jax.random.fold_in(arg_keys[13], 71), 0)
    query_count = draw_query_count(jax.random.fold_in(arg_keys[13], 71), 0)
    row_mask = plant((jax.random.randint(arg_keys[3], (ROWS_ALL,), 0, 8) < 7).astype(jnp.int32), jax.random.fold_in(arg_keys[3], 1), 0, 1)
    ln1_gain = jnp.clip(1.0 + 0.15 * jax.random.normal(arg_keys[4], (D,), jnp.float32), 0.25, 1.75)
    ln1_bias = gaussian(arg_keys[5], (D,), 0.3, 3.0, (), jnp.float32)
    w_qkv = gaussian(arg_keys[6], (D, 3 * D), D ** -0.5, 0.21875)
    w_out = gaussian(arg_keys[7], (D, D), (max(D // 96, 1)) ** -0.5, 2.0)
    ln2_gain = jnp.clip(1.0 + 0.15 * jax.random.normal(arg_keys[8], (D,), jnp.float32), 0.25, 1.75)
    ln2_bias = gaussian(arg_keys[9], (D,), 0.3, 3.0, (), jnp.float32)
    w_up = gaussian(arg_keys[10], (D, FF), D ** -0.5, 0.21875)
    w_down = gaussian(arg_keys[11], (FF, D), FF ** -0.5, 0.109375)
    cotangent = gaussian(arg_keys[12], (ROWS_ALL, D), 1.0, 6.0, ((0, 32),))
    return {"inputs": inputs, "context_count": context_count, "query_count": query_count, "row_mask": row_mask, "ln1_gain": ln1_gain, "ln1_bias": ln1_bias, "w_qkv": w_qkv, "w_out": w_out, "ln2_gain": ln2_gain, "ln2_bias": ln2_bias, "w_up": w_up, "w_down": w_down, "cotangent": cotangent}


@jax.custom_vjp
def low(v):
    return lax.optimization_barrier(v.astype(jnp.bfloat16)).astype(jnp.float32)

@jax.custom_vjp
def low_back(v):
    return v

def low_keep(v):
    return (low(v), None)

def low_pass(kept, grad):
    return (grad,)

def back_keep(v):
    return (v, None)

def back_low(kept, grad):
    return (low(grad),)
low.defvjp(low_keep, low_pass)
low_back.defvjp(back_keep, back_low)
epsilon = 1e-05
masked_score = -1000000000.0
highest = lax.Precision.HIGHEST

def normalize(values, norm_gain, norm_bias):
    centre = lax.optimization_barrier(jnp.mean(values, axis=-1, keepdims=True))
    centred = values - centre
    spread = lax.optimization_barrier(jnp.mean(centred * centred, axis=-1, keepdims=True))
    return centred * lax.rsqrt(spread + epsilon) * norm_gain + norm_bias

def table_layer(params, table_data):
    ln1_gain, ln1_bias, w_qkv, w_out, ln2_gain, ln2_bias, w_up, w_down = params
    table_rows, row_live, key_live = table_data
    width = table_rows.shape[1]
    score_factor = 1.0 / math.sqrt(HEAD)
    normed = low(normalize(table_rows, ln1_gain, ln1_bias))
    packed = low(low_back(jnp.dot(normed, w_qkv, precision=highest)))
    query_rows = packed[:, :width].reshape(SLOT, HEADS, HEAD)
    key_rows = packed[:KEYS, width:2 * width].reshape(KEYS, HEADS, HEAD)
    value_rows = packed[:KEYS, 2 * width:].reshape(KEYS, HEADS, HEAD)
    scores = low_back(jnp.einsum('qhe,khe->hqk', query_rows, key_rows, precision=highest) * score_factor)
    scores = jnp.where(key_live[None, None, :], scores, masked_score)
    row_max = lax.optimization_barrier(jnp.max(scores, axis=-1, keepdims=True))
    exponent = jnp.exp(scores - row_max)
    attn_probs = low(exponent / lax.optimization_barrier(jnp.sum(exponent, axis=-1, keepdims=True)))
    attended = jnp.einsum('hqk,khe->qhe', attn_probs, value_rows, precision=highest).reshape(SLOT, width)
    attended = low(low_back(jnp.where(row_live[:, None], attended, 0.0)))
    hidden_rows = table_rows + low_back(jnp.dot(attended, w_out, precision=highest))
    normed_two = low(normalize(hidden_rows, ln2_gain, ln2_bias))
    pre_act = low_back(jnp.dot(normed_two, w_up, precision=highest))
    activated = low(jax.nn.gelu(pre_act, approximate=False))
    return hidden_rows + low_back(jnp.dot(activated, w_down, precision=highest))

def whole_layer(row_live, key_live, params, all_rows):
    tables = all_rows.reshape(TABLES, SLOT, D)
    per_table = jax.checkpoint(partial(table_layer, params))
    outputs = lax.map(per_table, (tables, row_live, key_live))
    return outputs.reshape(TABLES * SLOT, D)

def reference(inputs, context_count, query_count, row_mask, ln1_gain, ln1_bias, w_qkv, w_out, ln2_gain, ln2_bias, w_up, w_down, cotangent):
    positions = jnp.arange(SLOT, dtype=jnp.int32)[None, :]
    present = (row_mask.reshape(TABLES, SLOT) == 1) | (positions == 0)
    row_live = present & (positions < (context_count + query_count)[:, None])
    key_live = (present & (positions < context_count[:, None]))[:, :KEYS]
    is_query = (row_live & (positions >= context_count[:, None])).reshape(TABLES * SLOT, 1)
    query_sum = jnp.sum(query_count.astype(jnp.float32))
    loss_factor = math.sqrt(TABLES) * QUERY_MOST / query_sum
    params = (ln1_gain.astype(jnp.float32), ln1_bias.astype(jnp.float32), w_qkv.astype(jnp.float32), w_out.astype(jnp.float32), ln2_gain.astype(jnp.float32), ln2_bias.astype(jnp.float32), w_up.astype(jnp.float32), w_down.astype(jnp.float32))
    layer_out, pull_back = jax.vjp(partial(whole_layer, row_live, key_live), params, inputs.astype(jnp.float32))
    upstream = cotangent.astype(jnp.float32) * jnp.where(is_query, loss_factor, 0.0)
    grad_params, grad_inputs = pull_back(upstream)
    return (layer_out.astype(jnp.bfloat16), grad_inputs, grad_params[0], grad_params[1], grad_params[2], grad_params[3], grad_params[4], grad_params[5], grad_params[6], grad_params[7])
```

```python
from functools import partial
import math

import jax
import jax.numpy as jnp
from jax import lax
from jax.experimental import pallas as pl
from jax.experimental.pallas import tpu as pltpu
from jax.sharding import PartitionSpec as P

HEADS = 12
HEAD = 64
WINDOW = 256

epsilon = 1e-05
masked_score = -1000000000.0
root_half = math.sqrt(0.5)
root_two_pi = math.sqrt(2.0 / math.pi) * 0.5


def normalize(values, gain, bias):
    centre = jnp.mean(values, axis=-1, keepdims=True)
    centred = values - centre
    spread = jnp.mean(centred * centred, axis=-1, keepdims=True)
    inverse = lax.rsqrt(spread + epsilon)
    unit_rows = centred * inverse
    return (unit_rows * gain + bias, unit_rows, inverse)


def norm_back(grad_norm, unit_rows, inverse, gain):
    grad_unit = grad_norm * gain
    grad_mean = jnp.mean(grad_unit, axis=-1, keepdims=True)
    grad_proj = jnp.mean(grad_unit * unit_rows, axis=-1, keepdims=True)
    grad_values = inverse * (grad_unit - grad_mean - unit_rows * grad_proj)
    return (grad_values, jnp.sum(grad_norm * unit_rows, axis=0), jnp.sum(grad_norm, axis=0))


def dot(left, right, left_dim=1, right_dim=0):
    return lax.dot_general(
        left, right, (((left_dim,), (right_dim,)), ((), ())), preferred_element_type=jnp.float32
    )


def lane_masks(width):
    lanes = lax.broadcasted_iota(jnp.int32, (1, width), 1)
    return (lanes < HEAD, lanes >= HEAD)


def head_scores(query, key_rows, live, lanes):
    only = jnp.where(lanes, query, jnp.zeros_like(query)) * jnp.bfloat16(1.0 / math.sqrt(HEAD))
    return jnp.where(live, dot(only, key_rows, 1, 1), masked_score)


def attend_kernel(query_ref, key_ref, value_ref, live_ref, out_ref):
    live = live_ref[...] > 0
    query, key_rows, value_rows = query_ref[...], key_ref[...], value_ref[...]
    parts = []
    for lanes in lane_masks(2 * HEAD):
        scores = head_scores(query, key_rows, live, lanes)
        exponent = jnp.exp(scores - jnp.max(scores, axis=-1, keepdims=True))
        inverse = 1.0 / jnp.sum(exponent, axis=-1, keepdims=True)
        parts.append(dot((exponent * inverse).astype(jnp.bfloat16), value_rows))
    out_ref[...] = jnp.where(lane_masks(2 * HEAD)[0], parts[0], parts[1]).astype(jnp.bfloat16)


def attend(query_rows, packed_keys, key_live, block):
    slots, width = query_rows.shape
    keys_len = packed_keys.shape[0]
    pairs = width // (2 * HEAD)
    return pl.pallas_call(
        attend_kernel,
        grid=(pairs, slots // block),
        in_specs=[
            pl.BlockSpec((block, 2 * HEAD), lambda p, r: (r, p)),
            pl.BlockSpec((keys_len, 2 * HEAD), lambda p, r: (0, p)),
            pl.BlockSpec((keys_len, 2 * HEAD), lambda p, r: (0, pairs + p)),
            pl.BlockSpec((1, keys_len), lambda p, r: (0, 0)),
        ],
        out_specs=pl.BlockSpec((block, 2 * HEAD), lambda p, r: (r, p)),
        out_shape=jax.ShapeDtypeStruct((slots, width), jnp.bfloat16),
    )(query_rows, packed_keys, packed_keys, key_live)


def attend_back_kernel(query_ref, key_ref, value_ref, grad_ref, live_ref, dq_ref, dk_ref, dv_ref):
    live = live_ref[...] > 0
    query, key_rows, value_rows = query_ref[...], key_ref[...], value_ref[...]
    grad = grad_ref[...]
    factor = 1.0 / math.sqrt(HEAD)
    parts = []
    for lanes in lane_masks(2 * HEAD):
        scores = head_scores(query, key_rows, live, lanes)
        exponent = jnp.exp(scores - jnp.max(scores, axis=-1, keepdims=True))
        probs = exponent * (1.0 / jnp.sum(exponent, axis=-1, keepdims=True))
        grad_probs = dot(jnp.where(lanes, grad, jnp.zeros_like(grad)), value_rows, 1, 1)
        inner = jnp.sum(grad_probs * probs, axis=-1, keepdims=True)
        grad_scores = (probs * (grad_probs - inner)).astype(jnp.bfloat16)
        parts.append(
            (
                dot(grad_scores, key_rows),
                dot(grad_scores, query, 0, 0),
                dot(probs.astype(jnp.bfloat16), grad, 0, 0),
            )
        )
    first = lane_masks(2 * HEAD)[0]
    dq_ref[...] = (jnp.where(first, parts[0][0], parts[1][0]) * factor).astype(jnp.bfloat16)
    dk_ref[...] = (jnp.where(first, parts[0][1], parts[1][1]) * factor).astype(jnp.bfloat16)
    dv_ref[...] = jnp.where(first, parts[0][2], parts[1][2]).astype(jnp.bfloat16)


def attend_back(query_rows, packed_keys, grad_rows, key_live):
    width = query_rows.shape[1]
    slots = grad_rows.shape[0]
    keys_len = packed_keys.shape[0]
    pairs = width // (2 * HEAD)
    rows_spec = pl.BlockSpec((slots, 2 * HEAD), lambda p: (0, p))
    keys_spec = pl.BlockSpec((keys_len, 2 * HEAD), lambda p: (0, p))
    return pl.pallas_call(
        attend_back_kernel,
        grid=(pairs,),
        in_specs=[
            rows_spec,
            keys_spec,
            pl.BlockSpec((keys_len, 2 * HEAD), lambda p: (0, pairs + p)),
            rows_spec,
            pl.BlockSpec((1, keys_len), lambda p: (0, 0)),
        ],
        out_specs=(rows_spec, keys_spec, keys_spec),
        out_shape=(
            jax.ShapeDtypeStruct((slots, width), jnp.bfloat16),
            jax.ShapeDtypeStruct((keys_len, width), jnp.bfloat16),
            jax.ShapeDtypeStruct((keys_len, width), jnp.bfloat16),
        ),
    )(query_rows, packed_keys, packed_keys, grad_rows, key_live)


def gelu_parts(values):
    share = 0.5 * (1.0 + lax.erf(values * root_half))
    return share


def local(
    devices,
    inputs,
    context_count,
    query_count,
    row_mask,
    ln1_gain,
    ln1_bias,
    w_qkv,
    w_out,
    ln2_gain,
    ln2_bias,
    w_up,
    w_down,
    cotangent,
):
    slots, width = inputs.shape
    hidden = w_up.shape[1]
    half = hidden // 2
    me = lax.axis_index("rows")
    core = me & 1

    def bit_of(bit):
        return ((me & bit) != 0).astype(jnp.int32)

    def swap(value, bit):
        return lax.ppermute(value, "rows", [(i, i ^ bit) for i in range(devices)])

    def pick(value, axis, index):
        return lax.dynamic_index_in_dim(value, index, axis, keepdims=False)

    bits = []
    bit = 2
    while bit < devices:
        bits.append(bit)
        bit *= 2
    top = bits[-1]

    def order_of(list_of_bits, flip):
        if flip and len(list_of_bits) > 1:
            return [list_of_bits[1], list_of_bits[0]] + list_of_bits[2:]
        return list_of_bits

    context = context_count[0]
    queries = query_count[0]
    place = (jnp.arange(slots, dtype=jnp.int32) + context) & (slots - 1)
    mask_rolled = lax.dynamic_slice(jnp.concatenate([row_mask, row_mask]), (context,), (slots,))
    rows_rolled = lax.dynamic_slice(
        jnp.concatenate([inputs, inputs], axis=0), (context, 0), (slots, width)
    )
    present = (mask_rolled == 1) | (place == 0)
    row_live = present & (place < context + queries)
    key_live = (present & (place < context))[WINDOW:].astype(jnp.float32)[None, :]
    is_query = (row_live & (place >= context))[:WINDOW]
    upstream_low = lax.dynamic_slice(cotangent, (context, 0), (WINDOW, width))
    upstream = upstream_low.astype(jnp.float32) * is_query.astype(jnp.float32)[:, None]
    upstream_got = 2.0 * swap(upstream * 0.5, 1)
    upstream_both = jnp.concatenate([upstream, upstream_got], axis=0).astype(jnp.bfloat16)

    rows_wide = rows_rolled.astype(jnp.float32)
    normed, unit_one, inverse_one = normalize(rows_wide, ln1_gain, ln1_bias)
    normed_low = normed.astype(jnp.bfloat16)
    w_keys = w_qkv[:, width:]
    w_query = w_qkv[:, :width]
    packed_keys = dot(normed_low[WINDOW:], w_keys).astype(jnp.bfloat16)
    query_rows = dot(normed_low, w_query).astype(jnp.bfloat16)
    attended_q = attend(query_rows[:WINDOW], packed_keys, key_live, WINDOW)
    attended_q = jnp.where(row_live[:WINDOW, None], attended_q, jnp.bfloat16(0))
    hidden_q = rows_wide[:WINDOW] + dot(attended_q, w_out)
    _, unit_two, inverse_two = normalize(hidden_q, ln2_gain, ln2_bias)
    unit_both = jnp.concatenate([unit_two, swap(unit_two, 1)], axis=0)
    normed_two_both = (unit_both * ln2_gain + ln2_bias).astype(jnp.bfloat16)
    up_half = lax.dynamic_slice(w_up, (0, core * half), (width, half))
    down_half = lax.dynamic_slice(w_down, (core * half, 0), (half, width))
    pre_act = dot(normed_two_both, up_half)
    share = gelu_parts(pre_act)
    activated = (pre_act * share).astype(jnp.bfloat16)
    slope = share + pre_act * (root_two_pi * jnp.exp(-0.5 * pre_act * pre_act))
    grad_act = dot(upstream_both, down_half, 1, 1)
    grad_pre = (grad_act * slope).astype(jnp.bfloat16)
    grad_down = dot(activated, upstream_both, 0, 0)
    grad_up = dot(grad_pre, normed_two_both, 0, 0)

    grad_two_parts = dot(grad_pre, up_half, 1, 1)
    down_parts = dot(activated, down_half)
    grad_normed_two = grad_two_parts[:WINDOW] + swap(grad_two_parts[WINDOW:], 1)
    out_q = hidden_q + down_parts[:WINDOW] + swap(down_parts[WINDOW:], 1)

    def scatter_ff(value, flip):
        remaining = bits[:-1][::-1] + [1]
        value = value.reshape([2] * len(remaining) + [half // (2 ** len(remaining)), width])
        for bit in order_of(bits[:-1], flip):
            axis = remaining.index(bit)
            mine = bit_of(bit)
            got = swap(pick(value, axis, 1 - mine), bit)
            value = pick(value, axis, mine) + got
            remaining.remove(bit)
        pairs = [(i, i ^ top) for i in range(devices) if ((i & top) != 0) != ((i & 1) != 0)]
        value = value + lax.ppermute(value, "rows", pairs)
        other = swap(pick(value, 0, 1 - core), 1)
        return jnp.where(bit_of(top) == core, pick(value, 0, core), other)

    down_share = scatter_ff(grad_down, False)
    up_share = scatter_ff(grad_up, True)

    grad_hidden_norm, gain_two, bias_two = norm_back(
        grad_normed_two, unit_two, inverse_two, ln2_gain
    )
    grad_hidden = upstream + grad_hidden_norm
    grad_hidden_low = grad_hidden.astype(jnp.bfloat16)
    grad_wout = dot(attended_q, grad_hidden_low, 0, 0)
    grad_attended = dot(grad_hidden_low, w_out, 1, 1)
    grad_attended = jnp.where(row_live[:WINDOW, None], grad_attended, 0.0).astype(jnp.bfloat16)
    grad_query, grad_key, grad_value = attend_back(
        query_rows, packed_keys, grad_attended, key_live
    )
    grad_wq = dot(normed_low[:WINDOW], grad_query, 0, 0)
    grad_wk = dot(normed_low[WINDOW:], grad_key, 0, 0)
    grad_wv = dot(normed_low[WINDOW:], grad_value, 0, 0)
    is_odd = core == 1
    keep = [jnp.where(is_odd, grad_wk, grad_wq), jnp.where(is_odd, grad_wv, grad_wout)]
    give = [jnp.where(is_odd, grad_wq, grad_wk), jnp.where(is_odd, grad_wout, grad_wv)]

    grad_normed = jnp.concatenate(
        [
            dot(grad_query, w_query, 1, 1),
            dot(grad_key, w_keys[:, :width], 1, 1) + dot(grad_value, w_keys[:, width:], 1, 1),
        ],
        axis=0,
    )
    grad_rows, gain_one, bias_one = norm_back(grad_normed, unit_one, inverse_one, ln1_gain)
    small = jnp.concatenate(
        [
            gain_one[None],
            bias_one[None],
            gain_two[None],
            bias_two[None],
            jnp.full((4, width), queries, jnp.float32),
        ],
        axis=0,
    )
    small, keep[0] = lax.optimization_barrier((small, keep[0]))
    for bit in [1] + bits:
        small = small + swap(small, bit)
    loss_factor = math.sqrt(devices) * (slots // 4) / small[4, 0]

    def reduce_all(own, give, flip):
        value = own + swap(give, 1)
        remaining = bits[::-1]
        value = value.reshape([2] * len(remaining) + [width // (2 ** len(remaining)), width])
        order = order_of(bits, flip)
        for bit in order:
            axis = remaining.index(bit)
            mine = bit_of(bit)
            got = swap(pick(value, axis, 1 - mine), bit)
            value = pick(value, axis, mine) + got
            remaining.remove(bit)
        value = value * loss_factor
        for bit in order[::-1]:
            axis = sum(1 for b in remaining if b > bit)
            got = swap(value, bit)
            high = bit_of(bit) == 1
            value = jnp.stack([jnp.where(high, got, value), jnp.where(high, value, got)], axis=axis)
            remaining.append(bit)
        value = value.reshape(width, width)
        return (value, swap(value, 1))

    first_own, first_got = reduce_all(keep[0], give[0], False)
    second_own, second_got = reduce_all(keep[1], give[1], True)
    grad_qkv = jnp.concatenate(
        [
            jnp.where(is_odd, first_got, first_own),
            jnp.where(is_odd, first_own, first_got),
            jnp.where(is_odd, second_own, second_got),
        ],
        axis=1,
    )
    grad_out = jnp.where(is_odd, second_got, second_own)

    normed_low_c, _ = lax.optimization_barrier((query_rows, grad_up))
    context_queries = normed_low_c[WINDOW:]
    attended_c = attend(context_queries, packed_keys, key_live, WINDOW)
    attended_c = jnp.where(row_live[WINDOW:, None], attended_c, jnp.bfloat16(0))
    hidden_c = rows_wide[WINDOW:] + dot(attended_c, w_out)
    normed_two_c = normalize(hidden_c, ln2_gain, ln2_bias)[0].astype(jnp.bfloat16)
    pre_c = dot(normed_two_c, w_up)
    activated_c = (pre_c * gelu_parts(pre_c)).astype(jnp.bfloat16)
    out_c = hidden_c + dot(activated_c, w_down)

    layer_rolled = jnp.concatenate([out_q, out_c], axis=0).astype(jnp.bfloat16)
    grad_rolled = loss_factor * jnp.concatenate(
        [grad_hidden + grad_rows[:WINDOW], grad_rows[WINDOW:]], axis=0
    )

    def unroll(value):
        return lax.dynamic_slice(
            jnp.concatenate([value, value], axis=0), (slots - context, 0), (slots, width)
        )

    return (
        unroll(layer_rolled),
        unroll(grad_rolled),
        small[0] * loss_factor,
        small[1] * loss_factor,
        grad_qkv,
        grad_out,
        small[2] * loss_factor,
        small[3] * loss_factor,
        (up_share * loss_factor).T,
        down_share * loss_factor,
    )


def solution(mesh):
    placed = (
        P("rows", None),
        P("rows"),
        P("rows"),
        P("rows"),
        P(),
        P(),
        P(),
        P(),
        P(),
        P(),
        P(),
        P(),
        P("rows", None),
    )
    return jax.shard_map(
        partial(local, mesh.shape["rows"]),
        mesh=mesh,
        in_specs=placed,
        out_specs=(
            P("rows", None),
            P("rows", None),
            P(),
            P(),
            P(),
            P(),
            P(),
            P(),
            P(None, "rows"),
            P("rows", None),
        ),
        check_vma=False,
    )
```

```python
from functools import partial
import math

import jax
import jax.numpy as jnp
from jax import lax
from jax.experimental import pallas as pl
from jax.experimental.pallas import tpu as pltpu
from jax.sharding import PartitionSpec as P

HEADS = 12
HEAD = 64
WINDOW = 256
SHARE = 64
PIECE = 512

epsilon = 1e-05
score_factor = 1.0 / math.sqrt(HEAD)
masked_score = -3e38
root_half = math.sqrt(0.5)
root_two_pi = math.sqrt(2.0 / math.pi) * 0.5


def dot(left, right, left_dim=1, right_dim=0):
    return lax.dot_general(
        left, right, (((left_dim,), (right_dim,)), ((), ())), preferred_element_type=jnp.float32
    )


def cost(flops, transcendentals, bytes_accessed):
    return pl.CostEstimate(
        flops=flops // SHARE,
        transcendentals=transcendentals // SHARE,
        bytes_accessed=bytes_accessed // SHARE,
    )


def lane_masks(width):
    lanes = lax.broadcasted_iota(jnp.int32, (1, width), 1)
    return (lanes < HEAD, lanes >= HEAD)


def both_heads(rows):
    none = jnp.zeros_like(rows)
    return jnp.concatenate([jnp.where(lanes, rows, none) for lanes in lane_masks(2 * HEAD)], axis=0)


def one_head(rows):
    size = rows.shape[0] // 2
    return jnp.where(lane_masks(2 * HEAD)[0], rows[:size], rows[size:])


def columns(values):
    rows = values[0].shape[0]
    lanes = lax.broadcasted_iota(jnp.int32, (rows, 2 * HEAD), 1)
    block = jnp.zeros((rows, 2 * HEAD), jnp.float32)
    for lane, value in enumerate(values):
        block = jnp.where(lanes == lane, value, block)
    return block.astype(jnp.bfloat16)


def ones_block(rows):
    return jnp.ones((rows, 2 * HEAD), jnp.bfloat16)


def norm_rows(values):
    centre = jnp.mean(values, axis=-1, keepdims=True)
    centred = values - centre
    inverse = lax.rsqrt(jnp.mean(centred * centred, axis=-1, keepdims=True) + epsilon)
    return (centred * inverse, inverse)


def norm_rows_back(grad_norm, unit_rows, inverse, gain):
    grad_unit = grad_norm * gain
    grad_mean = jnp.mean(grad_unit, axis=-1, keepdims=True)
    grad_proj = jnp.mean(grad_unit * unit_rows, axis=-1, keepdims=True)
    return inverse * (grad_unit - grad_mean - unit_rows * grad_proj)


def column_sums(grad_norm, unit_rows):
    return jnp.concatenate(
        [
            jnp.sum(grad_norm * unit_rows, axis=0, keepdims=True),
            jnp.sum(grad_norm, axis=0, keepdims=True),
        ],
        axis=0,
    )


def project_kernel(
    at_ref, rows_ref, norms_ref, weight_ref, rolled_ref, norm_ref, query_ref, packed_ref, twice
):
    step = pl.program_id(0)
    slots, width = rows_ref.shape

    @pl.when(step == 0)
    def _():
        twice[:slots] = rows_ref[...]
        twice[slots:] = rows_ref[...]
        start = pl.multiple_of(at_ref[0] // 16 * 16, 16)
        taken = lax.broadcasted_iota(jnp.int32, (WINDOW, WINDOW + 16), 1)
        given = lax.broadcasted_iota(jnp.int32, (WINDOW, WINDOW + 16), 0) + (at_ref[0] - start)
        shifted = jnp.where(taken == given, 1.0, 0.0).astype(jnp.bfloat16)
        for first in range(0, slots, WINDOW):
            rows = dot(shifted, twice[pl.ds(start + first, WINDOW + 16), :])
            rolled_ref[first : first + WINDOW] = rows.astype(jnp.bfloat16)
            unit_rows = norm_rows(rows)[0]
            norm_ref[first : first + WINDOW] = (
                unit_rows * norms_ref[0:1] + norms_ref[1:2]
            ).astype(jnp.bfloat16)
        query_ref[...] = dot(norm_ref[:WINDOW], weight_ref[...]).astype(jnp.bfloat16)

    @pl.when(step > 0)
    def _():
        packed_ref[...] = dot(norm_ref[WINDOW:], weight_ref[...]).astype(jnp.bfloat16)


def project(context, inputs, norms, w_qkv):
    slots, width = inputs.shape
    whole = pl.BlockSpec((slots, width), lambda j, at: (0, 0))
    return pl.pallas_call(
        project_kernel,
        grid_spec=pltpu.PrefetchScalarGridSpec(
            num_scalar_prefetch=1,
            grid=(3,),
            in_specs=[
                whole,
                pl.BlockSpec(norms.shape, lambda j, at: (0, 0)),
                pl.BlockSpec((width, width), lambda j, at: (0, j)),
            ],
            out_specs=(
                whole,
                whole,
                pl.BlockSpec((WINDOW, width), lambda j, at: (0, 0)),
                pl.BlockSpec((slots - WINDOW, width), lambda j, at: (0, jnp.maximum(j - 1, 0))),
            ),
            scratch_shapes=[pltpu.VMEM((2 * slots, width), jnp.bfloat16)],
        ),
        out_shape=(
            jax.ShapeDtypeStruct((slots, width), jnp.bfloat16),
            jax.ShapeDtypeStruct((slots, width), jnp.bfloat16),
            jax.ShapeDtypeStruct((WINDOW, width), jnp.bfloat16),
            jax.ShapeDtypeStruct((slots - WINDOW, 2 * width), jnp.bfloat16),
        ),
        cost_estimate=cost(
            flops=2 * slots * width * 2 * width,
            transcendentals=slots,
            bytes_accessed=14 * slots * width,
        ),
    )(context.reshape(1), inputs, norms, w_qkv)


def attend_kernel(
    query_ref, key_ref, value_ref, dead_ref, row_ref, rows_ref, wout_ref, attended_ref, hidden_ref, unit_ref, inverse_ref, attended
):
    step = pl.program_id(1)
    block = query_ref.shape[0]
    first_lane = columns([jnp.ones((2 * block, 1), jnp.float32)])
    queries = both_heads(query_ref[...] * jnp.bfloat16(score_factor))
    queries = jnp.concatenate([queries, first_lane], axis=1)
    keys = jnp.concatenate([key_ref[...], dead_ref[...]], axis=1)
    values = jnp.concatenate([value_ref[...], ones_block(key_ref.shape[0])], axis=1)
    parts = []
    for first in range(0, 2 * block, PIECE):
        scores = dot(queries[first : first + PIECE], keys, 1, 1)
        exponent = jnp.exp(scores - jnp.max(scores, axis=-1, keepdims=True)).astype(jnp.bfloat16)
        summed = dot(exponent, values)
        parts.append(summed[:, : 2 * HEAD] / summed[:, 2 * HEAD :])
    both = one_head(jnp.concatenate(parts, axis=0))
    both = jnp.where(row_ref[...] > 0, both, 0.0).astype(jnp.bfloat16)
    attended_ref[...] = both
    attended[:, pl.ds(pl.multiple_of(step * 2 * HEAD, 2 * HEAD), 2 * HEAD)] = both

    @pl.when(step == pl.num_programs(1) - 1)
    def _():
        hidden = rows_ref[...].astype(jnp.float32) + dot(attended[...], wout_ref[...])
        hidden_ref[...] = hidden
        unit_ref[...], inverse_ref[...] = norm_rows(hidden)


def attend(query_rows, packed_keys, key_dead, row_live, rows, w_out, from_query, from_row):
    slots, block, width = WINDOW, WINDOW, query_rows.shape[1]
    keys_len = packed_keys.shape[0]
    pairs = width // (2 * HEAD)
    whole = pl.BlockSpec((block, width), lambda r, p: (r, 0))
    return pl.pallas_call(
        attend_kernel,
        grid=(slots // block, pairs),
        in_specs=[
            pl.BlockSpec((block, 2 * HEAD), lambda r, p: (from_query, p)),
            pl.BlockSpec((keys_len, 2 * HEAD), lambda r, p: (0, p)),
            pl.BlockSpec((keys_len, 2 * HEAD), lambda r, p: (0, pairs + p)),
            pl.BlockSpec((keys_len, 2 * HEAD), lambda r, p: (0, 0)),
            pl.BlockSpec((block, 1), lambda r, p: (from_row, 0)),
            pl.BlockSpec((block, width), lambda r, p: (from_row, 0)),
            pl.BlockSpec((width, width), lambda r, p: (0, 0)),
        ],
        out_specs=(
            pl.BlockSpec((block, 2 * HEAD), lambda r, p: (r, p)),
            whole,
            whole,
            pl.BlockSpec((block, 1), lambda r, p: (r, 0)),
        ),
        scratch_shapes=[pltpu.VMEM((block, width), jnp.bfloat16)],
        out_shape=(
            jax.ShapeDtypeStruct((slots, width), jnp.bfloat16),
            jax.ShapeDtypeStruct((slots, width), jnp.float32),
            jax.ShapeDtypeStruct((slots, width), jnp.float32),
            jax.ShapeDtypeStruct((slots, 1), jnp.float32),
        ),
        cost_estimate=cost(
            flops=4 * slots * keys_len * width * 4,
            transcendentals=slots * keys_len * HEADS,
            bytes_accessed=12 * slots * width + 4 * keys_len * width,
        ),
    )(query_rows, packed_keys, packed_keys, key_dead, row_live, rows, w_out)


def units_kernel(
    at_ref, own_ref, got_ref, norms_ref, grad_ref, grad_got_ref, up_ref, down_ref, *outs
):
    keep_refs, act_ref, pre_ref, normed, upstream = outs[:8], outs[8], outs[9], outs[10], outs[11]
    width = own_ref.shape[1]
    cut = width // 2

    @pl.when(pl.program_id(0) == 0)
    def _():
        for first, part, grad in ((0, own_ref, grad_ref), (WINDOW, got_ref, grad_got_ref)):
            rows = part[...] * norms_ref[2:3] + norms_ref[3:4]
            normed[first : first + WINDOW] = rows.astype(jnp.bfloat16)
            upstream[first : first + WINDOW] = grad[...].astype(jnp.bfloat16)

    pre_act = dot(normed[...], up_ref[...])
    share = gelu_parts(pre_act)
    activated = (pre_act * share).astype(jnp.bfloat16)
    slope = share + pre_act * (root_two_pi * jnp.exp(-0.5 * pre_act * pre_act))
    grad_pre = (dot(upstream[...], down_ref[...], 1, 1) * slope).astype(jnp.bfloat16)
    act_ref[...] = activated
    pre_ref[...] = grad_pre
    for index, (left, right) in enumerate(((activated, upstream), (grad_pre, normed))):
        product = dot(left, right[...], 0, 0)
        mine = at_ref[1 + index] == 1
        rows = keep_refs[4 * index].shape[1]
        product = product.reshape(-1, 2, rows, width)
        keep = jnp.where(mine, product[:, 1], product[:, 0])
        give = jnp.where(mine, product[:, 0], product[:, 1])
        for place, (low, high) in enumerate(((0, cut), (cut, width))):
            keep_refs[4 * index + 2 * place][...] = keep[:, :, low:high]
            keep_refs[4 * index + 2 * place + 1][...] = give[:, :, low:high]


def units(core, bits_mine, rows, unit_own, unit_got, norms, upstream, upstream_got, w_up, w_down):
    width, hidden = w_up.shape
    half = hidden // 2
    tile = 8 * rows if 8 * rows >= 384 else 384
    tiles = half // tile
    whole = pl.BlockSpec((WINDOW, width), lambda j, at: (0, 0))
    pieces, shapes = [], []
    for index in range(2):
        size = 2 * rows * (index + 1)
        for _ in range(4):
            pieces.append(
                pl.BlockSpec((tile // (2 * size), size, width // 2), lambda j, at: (j, 0, 0))
            )
            shapes.append(
                jax.ShapeDtypeStruct((half // (2 * size), size, width // 2), jnp.float32)
            )
    acts = pl.BlockSpec((2 * WINDOW, tile), lambda j, at: (0, j))
    return pl.pallas_call(
        units_kernel,
        grid_spec=pltpu.PrefetchScalarGridSpec(
            num_scalar_prefetch=1,
            grid=(tiles,),
            in_specs=[
                whole,
                whole,
                pl.BlockSpec(norms.shape, lambda j, at: (0, 0)),
                whole,
                whole,
                pl.BlockSpec((width, tile), lambda j, at: (0, at[0] * tiles + j)),
                pl.BlockSpec((tile, width), lambda j, at: (at[0] * tiles + j, 0)),
            ],
            out_specs=(*pieces, acts, acts),
            scratch_shapes=[
                pltpu.VMEM((2 * WINDOW, width), jnp.bfloat16),
                pltpu.VMEM((2 * WINDOW, width), jnp.bfloat16),
            ],
        ),
        out_shape=(
            *shapes,
            jax.ShapeDtypeStruct((2 * WINDOW, half), jnp.bfloat16),
            jax.ShapeDtypeStruct((2 * WINDOW, half), jnp.bfloat16),
        ),
        cost_estimate=cost(
            flops=16 * WINDOW * width * half,
            transcendentals=4 * WINDOW * half,
            bytes_accessed=12 * width * half,
        ),
    )(
        jnp.stack([core, *bits_mine]),
        unit_own,
        unit_got,
        norms,
        upstream,
        upstream_got,
        w_up,
        w_down,
    )


def halves_kernel(right_dim, at_ref, left_ref, right_ref, own_ref, give_ref):
    product = dot(left_ref[...], right_ref[...], 1, right_dim)
    own_ref[...], give_ref[...] = product[:WINDOW], product[WINDOW:]


def halves(core, left, right, right_dim):
    rows, half = left.shape
    width = right.shape[1 - right_dim]
    tile = 256
    if right_dim == 1:
        spec = pl.BlockSpec((tile, half), lambda j, at: (j, at[0]))
    else:
        spec = pl.BlockSpec((half, tile), lambda j, at: (at[0], j))
    out = pl.BlockSpec((WINDOW, tile), lambda j, at: (0, j))
    return pl.pallas_call(
        partial(halves_kernel, right_dim),
        grid_spec=pltpu.PrefetchScalarGridSpec(
            num_scalar_prefetch=1,
            grid=(width // tile,),
            in_specs=[pl.BlockSpec((rows, half), lambda j, at: (0, 0)), spec],
            out_specs=(out, out),
        ),
        out_shape=(jax.ShapeDtypeStruct((WINDOW, width), jnp.float32),) * 2,
        cost_estimate=cost(
            flops=2 * rows * width * half, transcendentals=0, bytes_accessed=4 * width * half
        ),
    )(core.reshape(1), left, right)


def attend_back_kernel(
    query_ref,
    key_ref,
    value_ref,
    dead_ref,
    row_ref,
    own_ref,
    got_ref,
    unit_ref,
    inverse_ref,
    norms_ref,
    upstream_ref,
    wout_ref,
    dq_ref,
    dk_ref,
    dv_ref,
    grad_hidden_ref,
    low_ref,
    sums_ref,
):
    @pl.when(pl.program_id(0) == 0)
    def _():
        grad_norm = own_ref[...] + got_ref[...]
        unit_rows = unit_ref[...]
        sums_ref[...] = column_sums(grad_norm, unit_rows)
        grad_rows = norm_rows_back(grad_norm, unit_rows, inverse_ref[...], norms_ref[2:3])
        grad_hidden = upstream_ref[...] + grad_rows
        grad_hidden_ref[...] = grad_hidden
        low_ref[...] = grad_hidden.astype(jnp.bfloat16)

    key_rows = key_ref[...]
    grad = dot(low_ref[...], wout_ref[...], 1, 1)
    grads = both_heads(jnp.where(row_ref[...] > 0, grad, 0.0).astype(jnp.bfloat16))
    block = query_ref.shape[0]
    first_lane = columns([jnp.ones((2 * block, 1), jnp.float32)])
    queries = both_heads(query_ref[...] * jnp.bfloat16(score_factor))
    keys = jnp.concatenate([key_rows, dead_ref[...]], axis=1)
    scores = dot(jnp.concatenate([queries, first_lane], axis=1), keys, 1, 1)
    exponent = jnp.exp(scores - jnp.max(scores, axis=-1, keepdims=True))
    probs = exponent * (1.0 / jnp.sum(exponent, axis=-1, keepdims=True))
    grad_probs = dot(grads, value_ref[...], 1, 1)
    inner = jnp.sum(grad_probs * probs, axis=-1, keepdims=True)
    grad_scores = (probs * (grad_probs - inner)).astype(jnp.bfloat16)
    dq_ref[...] = (one_head(dot(grad_scores, key_rows)) * score_factor).astype(jnp.bfloat16)
    dk_ref[...] = dot(grad_scores, queries, 0, 0).astype(jnp.bfloat16)
    dv_ref[...] = dot(probs.astype(jnp.bfloat16), grads, 0, 0).astype(jnp.bfloat16)


def attend_back(
    query_rows, packed_keys, key_dead, row_live, own, got, unit, inverse, norms, upstream, w_out
):
    slots, width = query_rows.shape
    keys_len = packed_keys.shape[0]
    pairs = width // (2 * HEAD)
    rows_spec = pl.BlockSpec((slots, 2 * HEAD), lambda p: (0, p))
    keys_spec = pl.BlockSpec((keys_len, 2 * HEAD), lambda p: (0, p))
    whole = pl.BlockSpec((slots, width), lambda p: (0, 0))
    column = pl.BlockSpec((slots, 1), lambda p: (0, 0))
    return pl.pallas_call(
        attend_back_kernel,
        grid=(pairs,),
        in_specs=[
            rows_spec,
            keys_spec,
            pl.BlockSpec((keys_len, 2 * HEAD), lambda p: (0, pairs + p)),
            pl.BlockSpec((keys_len, 2 * HEAD), lambda p: (0, 0)),
            column,
            whole,
            whole,
            whole,
            column,
            pl.BlockSpec(norms.shape, lambda p: (0, 0)),
            whole,
            pl.BlockSpec((2 * HEAD, width), lambda p: (p, 0)),
        ],
        out_specs=(
            rows_spec,
            keys_spec,
            keys_spec,
            whole,
            whole,
            pl.BlockSpec((2, width), lambda p: (0, 0)),
        ),
        out_shape=(
            jax.ShapeDtypeStruct((slots, width), jnp.bfloat16),
            jax.ShapeDtypeStruct((keys_len, width), jnp.bfloat16),
            jax.ShapeDtypeStruct((keys_len, width), jnp.bfloat16),
            jax.ShapeDtypeStruct((slots, width), jnp.float32),
            jax.ShapeDtypeStruct((slots, width), jnp.bfloat16),
            jax.ShapeDtypeStruct((2, width), jnp.float32),
        ),
        cost_estimate=cost(
            flops=10 * slots * keys_len * width * 4,
            transcendentals=slots * keys_len * HEADS,
            bytes_accessed=6 * slots * width + 8 * keys_len * width,
        ),
    )(
        query_rows,
        packed_keys,
        packed_keys,
        key_dead,
        row_live,
        own,
        got,
        unit,
        inverse,
        norms,
        upstream,
        w_out,
    )


def weights_kernel(
    at_ref, factor_ref, norm_ref, attended_ref, dq_ref, dk_ref, dv_ref, low_ref, keep_a, keep_b, give_a, give_b
):
    for odd, (even_a, even_b, odd_a, odd_b) in (
        (0, (keep_a, keep_b, give_a, give_b)),
        (1, (give_a, give_b, keep_a, keep_b)),
    ):

        @pl.when(at_ref[0] == odd)
        def _(even_a=even_a, even_b=even_b, odd_a=odd_a, odd_b=odd_b):
            even_a[...] = dot(norm_ref[:WINDOW], dq_ref[...], 0, 0) * factor_ref[0, 0]
            odd_a[...] = dot(norm_ref[WINDOW:], dk_ref[...], 0, 0) * factor_ref[0, 0]
            odd_b[...] = dot(norm_ref[WINDOW:], dv_ref[...], 0, 0) * factor_ref[0, 0]
            even_b[...] = dot(attended_ref[...], low_ref[...], 0, 0) * factor_ref[0, 0]


def weights(core, factor, normed, attended, dq, dk, dv, low):
    slots, width = normed.shape
    tile = 256

    def full(value):
        return pl.BlockSpec(value.shape, lambda j, at: (0, 0))

    out = pl.BlockSpec((tile, width), lambda j, at: (j, 0))
    return pl.pallas_call(
        weights_kernel,
        grid_spec=pltpu.PrefetchScalarGridSpec(
            num_scalar_prefetch=1,
            grid=(width // tile,),
            in_specs=[
                pl.BlockSpec(memory_space=pltpu.SMEM),
                pl.BlockSpec((slots, tile), lambda j, at: (0, j)),
                pl.BlockSpec((WINDOW, tile), lambda j, at: (0, j)),
                full(dq),
                full(dk),
                full(dv),
                full(low),
            ],
            out_specs=(out,) * 4,
        ),
        out_shape=(jax.ShapeDtypeStruct((width, width), jnp.float32),) * 4,
        cost_estimate=cost(
            flops=4 * slots * width * width, transcendentals=0, bytes_accessed=20 * width * width
        ),
    )(core.reshape(1), factor, normed, attended, dq, dk, dv, low)


def rows_back_kernel(factor_ref, dq_ref, dk_ref, dv_ref, rows_ref, hidden_ref, norms_ref, wq, wk, wv, out_ref, sums_ref):
    step = pl.program_id(0)
    unit_rows, inverse = norm_rows(rows_ref[...].astype(jnp.float32))

    def finish(grad_norm):
        sums = column_sums(grad_norm, unit_rows)
        return (norm_rows_back(grad_norm, unit_rows, inverse, norms_ref[0:1]), sums * factor_ref[0, 0])

    @pl.when(step == 0)
    def _():
        grad_rows, sums = finish(dot(dq_ref[...], wq[...], 1, 1))
        out_ref[...] = (grad_rows + hidden_ref[...]) * factor_ref[0, 0]
        sums_ref[...] = sums

    @pl.when(step > 0)
    def _():
        grad_rows, sums = finish(dot(dk_ref[...], wk[...], 1, 1) + dot(dv_ref[...], wv[...], 1, 1))
        out_ref[...] = grad_rows * factor_ref[0, 0]
        sums_ref[...] += sums


def rows_back(factor, dq, dk, dv, rows, grad_hidden, norms, w_qkv):
    slots, width = rows.shape
    fixed = pl.BlockSpec((WINDOW, width), lambda r: (0, 0))
    keys = pl.BlockSpec((WINDOW, width), lambda r: (jnp.maximum(r - 1, 0), 0))
    tile = pl.BlockSpec((WINDOW, width), lambda r: (r, 0))
    return pl.pallas_call(
        rows_back_kernel,
        grid=(slots // WINDOW,),
        in_specs=[
            pl.BlockSpec(memory_space=pltpu.SMEM),
            fixed,
            keys,
            keys,
            tile,
            fixed,
            pl.BlockSpec(norms.shape, lambda r: (0, 0)),
            pl.BlockSpec((width, width), lambda r: (0, 0)),
            pl.BlockSpec((width, width), lambda r: (0, 1)),
            pl.BlockSpec((width, width), lambda r: (0, 2)),
        ],
        out_specs=(tile, pl.BlockSpec((2, width), lambda r: (0, 0))),
        out_shape=(
            jax.ShapeDtypeStruct((slots, width), jnp.float32),
            jax.ShapeDtypeStruct((2, width), jnp.float32),
        ),
        cost_estimate=cost(
            flops=4 * slots * width * width, transcendentals=slots, bytes_accessed=12 * slots * width
        ),
    )(factor, dq, dk, dv, rows, grad_hidden, norms, w_qkv, w_qkv, w_qkv)


def place_kernel(at_ref, own_a, own_b, got_a, got_b, *refs):
    qkv_ref, out_ref = refs[-2:]
    step = pl.program_id(0)
    odd = at_ref[0] == 1

    @pl.when(step == 0)
    def _():
        qkv_ref[...] = jnp.where(odd, got_a[...], own_a[...])
        out_ref[...] = jnp.where(odd, got_b[...], own_b[...])

    @pl.when(step == 1)
    def _():
        qkv_ref[...] = jnp.where(odd, own_a[...], got_a[...])

    @pl.when(step == 2)
    def _():
        qkv_ref[...] = jnp.where(odd, own_b[...], got_b[...])


def put(at, pieces, held):
    size, width = pieces[0].shape
    operands = [*pieces, *(held or ())]
    return pl.pallas_call(
        place_kernel,
        grid_spec=pltpu.PrefetchScalarGridSpec(
            num_scalar_prefetch=1,
            grid=(3,),
            in_specs=[pl.BlockSpec((size, width), lambda j, at: (0, 0))] * 4
            + [pl.BlockSpec(memory_space=pl.ANY)] * (2 if held else 0),
            out_specs=(
                pl.BlockSpec((size, width), lambda j, at: (jnp.where(j < 2, at[1], at[2]), j)),
                pl.BlockSpec((size, width), lambda j, at: (at[2], 0)),
            ),
        ),
        out_shape=(
            jax.ShapeDtypeStruct((2 * size, 3 * width), jnp.float32),
            jax.ShapeDtypeStruct((2 * size, width), jnp.float32),
        ),
        input_output_aliases={5: 0, 6: 1} if held else {},
        cost_estimate=cost(flops=0, transcendentals=0, bytes_accessed=16 * width * width),
    )(at, *operands)


def gelu_parts(values):
    share = 0.5 * (1.0 + lax.erf(values * root_half))
    return share


def local(
    devices,
    inputs,
    context_count,
    query_count,
    row_mask,
    ln1_gain,
    ln1_bias,
    w_qkv,
    w_out,
    ln2_gain,
    ln2_bias,
    w_up,
    w_down,
    cotangent,
):
    slots, width = inputs.shape
    hidden = w_up.shape[1]
    half = hidden // 2
    me = lax.axis_index("rows")
    core = me & 1

    def bit_of(bit):
        return ((me & bit) != 0).astype(jnp.int32)

    def swap(value, bit):
        return lax.ppermute(value, "rows", [(i, i ^ bit) for i in range(devices)])

    def pick(value, axis, index):
        return lax.dynamic_index_in_dim(value, index, axis, keepdims=False)

    bits = []
    bit = 2
    while bit < devices:
        bits.append(bit)
        bit *= 2
    top = bits[-1]

    def order_of(list_of_bits, flip):
        if flip and len(list_of_bits) > 1:
            return [list_of_bits[1], list_of_bits[0]] + list_of_bits[2:]
        return list_of_bits

    context = context_count[0]
    queries = query_count[0]
    norms = jnp.stack([ln1_gain, ln1_bias, ln2_gain, ln2_bias])
    place = (jnp.arange(slots, dtype=jnp.int32) + context) & (slots - 1)
    mask_rolled = lax.dynamic_slice(jnp.concatenate([row_mask, row_mask]), (context,), (slots,))
    present = (mask_rolled == 1) | (place == 0)
    row_live = present & (place < context + queries)
    key_live = (present & (place < context))[WINDOW:]
    key_dead = jnp.where(
        key_live[:, None] | (jnp.arange(2 * HEAD) > 0)[None, :], 0.0, masked_score
    ).astype(jnp.bfloat16)
    row_column = row_live.astype(jnp.float32)[:, None]
    is_query = (row_live & (place >= context))[:WINDOW]
    upstream_low = lax.dynamic_slice(cotangent, (context, 0), (WINDOW, width))
    upstream = upstream_low.astype(jnp.float32) * is_query.astype(jnp.float32)[:, None]
    upstream_got = 2.0 * swap(upstream * 0.5, 1)

    tie = lax.optimization_barrier
    total = jnp.full((8, 128), queries, jnp.float32)
    steps = [1] + bits
    total_got = swap(total, steps.pop(0))
    rows, normed_low, query_window, packed_keys = project(context, inputs, norms, w_qkv)
    query_window, total_got = tie((query_window, total_got))
    total = total + total_got
    total_got = swap(total, steps.pop(0))
    attended_q, hidden_q, unit_two, inverse_two = attend(
        query_window, packed_keys, key_dead, row_column, rows, w_out, 0, 0
    )
    unit_two, total_got = tie((unit_two, total_got))
    total = total + total_got
    ff_rows = half // (devices // 2)
    ff_bits = bits[:-1]
    total_got = swap(total, steps.pop(0))
    pieces = units(
        core,
        (bit_of(bits[0]), bit_of(bits[1])),
        ff_rows,
        unit_two,
        swap(unit_two, 1),
        norms,
        upstream,
        upstream_got,
        w_up,
        w_down,
    )
    pieces, total_got = tie((pieces, total_got))
    total = total + total_got
    activated, grad_pre = pieces[8:]
    first_bits, second_bits = order_of(bits, False), order_of(bits, True)

    class Halving:
        def __init__(self, terms, axes):
            self.terms, self.axes = terms, list(axes)

        def split(self, bit):
            axis = self.axes.index(bit)
            mine = bit_of(bit)
            self.axes.remove(bit)
            self.kept = sum(pick(term, axis, mine) for term in self.terms)
            self.sent = sum(pick(term, axis, 1 - mine) for term in self.terms)

        def go(self, bit):
            self.terms = [self.kept, swap(self.sent, bit)]

        def send(self, bit):
            self.split(bit)
            self.go(bit)

    def got_of(chains):
        return tuple(chain.terms[1] for chain in chains)

    def set_got(chains, values):
        for chain, value in zip(chains, values):
            chain.terms[1] = value

    def feed_forward(index, place):
        keep, give = pieces[4 * index + 2 * place : 4 * index + 2 * place + 2]
        axes = ff_bits[::-1] + [1]
        axes.remove(ff_order[index][0])
        shape = [2] * len(axes) + [ff_rows, width // 2]
        got = swap(give, ff_order[index][0])
        return Halving([keep.reshape(shape), got.reshape(shape)], axes)

    def to_top(chain):
        pairs = [(i, i ^ top) for i in range(devices) if ((i & top) != 0) != ((i & 1) != 0)]
        value = chain.terms[0] + chain.terms[1]
        chain.terms = [value, lax.ppermute(value, "rows", pairs)]

    def hand_over(chain):
        mine = sum(pick(term, 1, core) for term in chain.terms)
        other = swap(sum(pick(term, 1, 1 - core) for term in chain.terms), 1)
        return jnp.where(bit_of(top) == core, mine, other)

    ff_order = (order_of(ff_bits, False), order_of(ff_bits, True))

    down_one = feed_forward(0, 0)
    up_one = feed_forward(1, 0)
    ones = (down_one, up_one)

    total_got = swap(total, steps.pop(0))
    grad_own, grad_give = halves(core, grad_pre, w_up, 1)
    grad_own, total_got = tie((grad_own, total_got))
    total = total + total_got
    while len(steps) > 1:
        total = total + swap(total, steps.pop(0))
    total_got = swap(total, steps.pop(0))
    grad_query, grad_key, grad_value, grad_hidden, grad_low, sums_two = attend_back(
        query_window,
        packed_keys,
        key_dead,
        row_column,
        grad_own,
        swap(grad_give, 1),
        unit_two,
        inverse_two,
        norms,
        upstream,
        w_out,
    )
    grad_query, grad_key, grad_value, ones_got, total_got = tie(
        (grad_query, grad_key, grad_value, got_of(ones), total_got)
    )
    set_got(ones, ones_got)
    total = total + total_got
    loss_factor = math.sqrt(devices) * (slots // 4) / total[0, 0]
    factor = loss_factor.reshape(1, 1)
    for chain, order in zip(ones, ff_order):
        chain.split(order[1])
    grad_query, ones[0].sent, ones[1].sent = tie((grad_query, ones[0].sent, ones[1].sent))
    for chain, order in zip(ones, ff_order):
        chain.go(order[1])
    keep_first, keep_second, *give = weights(
        core, factor, normed_low, attended_q, grad_query, grad_key, grad_value, grad_low
    )

    def unroll(value):
        return lax.dynamic_slice(
            jnp.concatenate([value, value], axis=0), (slots - context, 0), (slots, width)
        )

    def joined(chains):
        terms = [jnp.stack([c.terms[k] for c in chains]) for k in range(2)]
        return Halving(terms, [None] + chains[0].axes)

    give_first, give_second = swap(give[0], 1), swap(give[1], 1)
    shape = [2] * len(bits) + [width // (2 ** len(bits)), width]
    first = Halving([keep_first.reshape(shape), give_first.reshape(shape)], first_bits)
    second = Halving([keep_second.reshape(shape), give_second.reshape(shape)], second_bits)
    both = (first, second)

    first.send(first_bits[0])
    second.send(second_bits[0])
    grad_query, grad_key, grad_value, ones_got, _ = tie(
        (grad_query, grad_key, grad_value, got_of(ones), give_first)
    )
    set_got(ones, ones_got)
    ones = joined(ones)
    for bit in ff_bits[2:]:
        ones.send(bit)
    grad_rows, sums_one = rows_back(
        factor, grad_query, grad_key, grad_value, rows, grad_hidden, norms, w_qkv
    )
    context_norms, _ = tie((normed_low[WINDOW:], grad_rows))
    context_queries = dot(context_norms, w_qkv[:, :width]).astype(jnp.bfloat16)

    def context_part(index, queries):
        return attend(
            queries, packed_keys, key_dead, row_column, rows, w_out, index, index + 1
        )[1:3]

    both_got, ones_got, context_queries, sums_one = tie(
        (got_of(both), ones.terms[1], context_queries, sums_one)
    )
    set_got(both, both_got)
    ones.terms[1] = ones_got

    first.send(first_bits[1])
    second.send(second_bits[1])
    small = jnp.concatenate(
        [sums_one, sums_two * loss_factor, jnp.zeros((4, width), jnp.float32)], axis=0
    )
    small_got = swap(small, 1)
    to_top(ones)
    part_one = context_part(0, context_queries)
    both_got, ones_got, part_one, pieces, small_got, context_queries = tie(
        (got_of(both), ones.terms[1], part_one, pieces, small_got, context_queries)
    )
    set_got(both, both_got)
    ones.terms[1] = ones_got
    small = small + small_got

    down_two = feed_forward(0, 1)
    up_two = feed_forward(1, 1)
    twos = (down_two, up_two)
    both = joined(both)
    for bit in bits[2:-1]:
        both.send(bit)
    ones = hand_over(ones)
    small_got = swap(small, bits[0])
    part_two = context_part(1, context_queries)
    both_got, part_two, small_got, context_queries = tie(
        (both.terms[1], part_two, small_got, context_queries)
    )
    both.terms[1] = both_got
    small = small + small_got

    value = both.terms[0] + both.terms[1]
    value_got = swap(value, top)
    small_got = swap(small, bits[1])
    part_three = context_part(2, context_queries)
    hidden_c, unit_c = (
        jnp.concatenate(p, axis=0) for p in zip(part_one, part_two, part_three)
    )
    normed_two_c = (unit_c * ln2_gain + ln2_bias).astype(jnp.bfloat16)
    twos_got, normed_two_c = tie((got_of(twos), normed_two_c))
    set_got(twos, twos_got)
    for chain, order in zip(twos, ff_order):
        chain.split(order[1])
    twos[0].sent, twos[1].sent, value_got, normed_two_c, small_got, activated, ones = tie(
        (twos[0].sent, twos[1].sent, value_got, normed_two_c, small_got, activated, ones)
    )
    value = value + value_got
    small = small + small_got

    def widen(value, bit, axis):
        got = swap(value, bit)
        high = bit_of(bit) == 1
        return jnp.stack(
            [jnp.where(high, got, value), jnp.where(high, value, got)], axis=axis
        )

    for bit in bits[2:-1][::-1]:
        value = widen(value, bit, 1)
    for chain, order in zip(twos, ff_order):
        chain.go(order[1])
    out_own, out_give = halves(core, activated, w_down, 0)
    out_give = swap(out_give, 1)
    for bit in bits[2:-1]:
        small = small + swap(small, bit)
    twos_got, value, out_own, out_give, small = tie(
        (got_of(twos), value, out_own, out_give, small)
    )
    set_got(twos, twos_got)
    twos = joined(twos)

    first_value = widen(value[0], first_bits[1], 0)
    second_value = widen(value[1], second_bits[1], 0)
    for bit in ff_bits[2:]:
        twos.send(bit)
    pre_c = dot(normed_two_c, w_up)
    activated_c = (pre_c * gelu_parts(pre_c)).astype(jnp.bfloat16)
    out_c = hidden_c + dot(activated_c, w_down)
    out_q = hidden_q + out_own + out_give
    first_value, second_value, twos_got, out_c, small = tie(
        (first_value, second_value, twos.terms[1], out_c, small)
    )
    twos.terms[1] = twos_got

    first_value, second_value = first_value.reshape(-1, width), second_value.reshape(-1, width)
    first_far = swap(first_value, first_bits[0])
    second_far = swap(second_value, second_bits[0])
    first_near = swap(first_value, 1)
    second_near = swap(second_value, 1)
    to_top(twos)
    small = small + swap(small, top)
    layer_out = unroll(jnp.concatenate([out_q, out_c], axis=0).astype(jnp.bfloat16))
    grad_inputs = unroll(grad_rows)
    one, two = bit_of(first_bits[0]), bit_of(second_bits[0])
    held = put(
        jnp.stack([core, one, two]), (first_value, second_value, first_near, second_near), None
    )
    first_far, second_far, twos_got, small, layer_out, grad_inputs, held = tie(
        (first_far, second_far, twos.terms[1], small, layer_out, grad_inputs, held)
    )
    twos.terms[1] = twos_got

    first_got = swap(first_far, 1)
    second_got = swap(second_far, 1)
    twos = hand_over(twos)
    grad_qkv, grad_out = put(
        jnp.stack([core, 1 - one, 1 - two]), (first_far, second_far, first_got, second_got), held
    )
    down_one, up_one = ones[0], ones[1]
    down_two, up_two = twos[0], twos[1]
    down_share = jnp.concatenate([down_one, down_two], axis=1)
    up_share = jnp.concatenate([up_one, up_two], axis=1)
    return (
        layer_out,
        grad_inputs,
        small[0],
        small[1],
        grad_qkv,
        grad_out,
        small[2],
        small[3],
        (up_share * loss_factor).T,
        down_share * loss_factor,
    )


def solution(mesh):
    placed = (
        P("rows", None),
        P("rows"),
        P("rows"),
        P("rows"),
        P(),
        P(),
        P(),
        P(),
        P(),
        P(),
        P(),
        P(),
        P("rows", None),
    )
    return jax.shard_map(
        partial(local, mesh.shape["rows"]),
        mesh=mesh,
        in_specs=placed,
        out_specs=(
            P("rows", None),
            P("rows", None),
            P(),
            P(),
            P(),
            P(),
            P(),
            P(),
            P(None, "rows"),
            P("rows", None),
        ),
        check_vma=False,
    )
```

```python
from functools import partial
import math

import jax
import jax.numpy as jnp
from jax import lax
from jax.experimental import pallas as pl
from jax.experimental.pallas import tpu as pltpu
from jax.sharding import PartitionSpec as P

HEADS = 12
HEAD = 64
WINDOW = 256
SHARE = 64
PIECE = 256

epsilon = 1e-05
score_factor = 1.0 / math.sqrt(HEAD)
masked_score = -3e38
root_half = math.sqrt(0.5)
root_two_pi = math.sqrt(2.0 / math.pi) * 0.5


def dot(left, right, left_dim=1, right_dim=0):
    return lax.dot_general(
        left, right, (((left_dim,), (right_dim,)), ((), ())), preferred_element_type=jnp.float32
    )


def cost(flops, transcendentals, bytes_accessed):
    return pl.CostEstimate(
        flops=flops // SHARE,
        transcendentals=transcendentals // SHARE,
        bytes_accessed=bytes_accessed // SHARE,
    )


def lane_masks(width):
    lanes = lax.broadcasted_iota(jnp.int32, (1, width), 1)
    return (lanes < HEAD, lanes >= HEAD)


def both_heads(rows):
    none = jnp.zeros_like(rows)
    return jnp.concatenate([jnp.where(lanes, rows, none) for lanes in lane_masks(2 * HEAD)], axis=0)


def one_head(rows):
    size = rows.shape[0] // 2
    return jnp.where(lane_masks(2 * HEAD)[0], rows[:size], rows[size:])


def columns(values):
    rows = values[0].shape[0]
    lanes = lax.broadcasted_iota(jnp.int32, (rows, 2 * HEAD), 1)
    block = jnp.zeros((rows, 2 * HEAD), jnp.float32)
    for lane, value in enumerate(values):
        block = jnp.where(lanes == lane, value, block)
    return block.astype(jnp.bfloat16)


def ones_block(rows):
    return jnp.ones((rows, 2 * HEAD), jnp.bfloat16)


def norm_rows(values):
    centre = jnp.mean(values, axis=-1, keepdims=True)
    centred = values - centre
    inverse = lax.rsqrt(jnp.mean(centred * centred, axis=-1, keepdims=True) + epsilon)
    return (centred * inverse, inverse)


def norm_rows_back(grad_norm, unit_rows, inverse, gain):
    grad_unit = grad_norm * gain
    grad_mean = jnp.mean(grad_unit, axis=-1, keepdims=True)
    grad_proj = jnp.mean(grad_unit * unit_rows, axis=-1, keepdims=True)
    return inverse * (grad_unit - grad_mean - unit_rows * grad_proj)


def column_sums(grad_norm, unit_rows):
    return jnp.concatenate(
        [
            jnp.sum(grad_norm * unit_rows, axis=0, keepdims=True),
            jnp.sum(grad_norm, axis=0, keepdims=True),
        ],
        axis=0,
    )


def shift_rows(count):
    taken = lax.broadcasted_iota(jnp.int32, (WINDOW, WINDOW + 16), 1)
    given = lax.broadcasted_iota(jnp.int32, (WINDOW, WINDOW + 16), 0) + count
    return jnp.where(taken == given, 1.0, 0.0).astype(jnp.bfloat16)


def project_kernel(
    context_ref,
    queries_ref,
    rows_ref,
    mask_ref,
    cotangent_ref,
    norms_ref,
    weight_ref,
    rolled_ref,
    norm_ref,
    query_ref,
    packed_ref,
    live_ref,
    dead_ref,
    upstream_ref,
    twice,
    present,
):
    step = pl.program_id(0)
    slots, width = rows_ref.shape

    @pl.when(step == 0)
    def _():
        context, queries = context_ref[0], queries_ref[0]
        start = pl.multiple_of(context // 16 * 16, 16)
        shifted = shift_rows(context - start)
        for half in (slice(0, slots), slice(slots, 2 * slots)):
            twice[half] = rows_ref[...]
        across = lax.broadcasted_iota(jnp.int32, (128, 128), 1)
        down = lax.broadcasted_iota(jnp.int32, (128, 128), 0)
        for group in range(slots // 128):
            kept = (across == down) & (mask_ref[group : group + 1] == 1)
            if group == 0:
                kept = kept | ((across == 0) & (down == 0))
            kept = jnp.where(kept, 1.0, 0.0).astype(jnp.bfloat16)
            marks = dot(kept, jnp.ones((128, 128), jnp.bfloat16)).astype(jnp.bfloat16)
            for first in (0, slots):
                present[first + group * 128 : first + (group + 1) * 128] = marks
        for first in range(0, slots, WINDOW):
            rows = dot(shifted, twice[pl.ds(start + first, WINDOW + 16), :])
            rolled_ref[first : first + WINDOW] = rows.astype(jnp.bfloat16)
            unit_rows = norm_rows(rows)[0]
            norm_ref[first : first + WINDOW] = (
                unit_rows * norms_ref[0:1] + norms_ref[1:2]
            ).astype(jnp.bfloat16)
            here = dot(shifted, present[pl.ds(start + first, WINDOW + 16), :])
            place = lax.broadcasted_iota(jnp.int32, here.shape, 0) + (first + context)
            place = jnp.where(place >= slots, place - slots, place)
            live_ref[first : first + WINDOW] = jnp.where(place < context + queries, here, 0.0)[:, 0:1]
            lanes = lax.broadcasted_iota(jnp.int32, here.shape, 1)
            if first > 0:
                known = (here > 0) & (place < context)
                split = lanes & (HEAD - 1)
                ones = jnp.where((split >= 1) & (split <= 3), 1.0, 0.0)
                dead = jnp.where((lanes == 0) & jnp.logical_not(known), masked_score, ones)
                dead_ref[first - WINDOW : first] = dead.astype(jnp.bfloat16)
            else:
                asked = jnp.where(place < context + queries, here, 0.0)[:, 0:1]
        twice[:slots] = cotangent_ref[...]
        near = jnp.minimum(start, slots - WINDOW - 16)
        near = pl.multiple_of(near, 16)
        upstream_ref[...] = dot(shift_rows(context - near), twice[pl.ds(near, WINDOW + 16), :]) * asked
        query_ref[...] = dot(norm_ref[:WINDOW], weight_ref[...]).astype(jnp.bfloat16)

    @pl.when(step > 0)
    def _():
        packed_ref[...] = dot(norm_ref[WINDOW:], weight_ref[...]).astype(jnp.bfloat16)


def project(context, queries, inputs, row_mask, cotangent, norms, w_qkv):
    slots, width = inputs.shape

    def fixed(shape):
        return pl.BlockSpec(shape, lambda j, at, more: (0, 0))

    whole = fixed((slots, width))
    outs = (
        ((slots, width), jnp.bfloat16),
        ((slots, width), jnp.bfloat16),
        ((WINDOW, width), jnp.bfloat16),
        ((slots - WINDOW, 2 * width), jnp.bfloat16),
        ((slots, 1), jnp.float32),
        ((slots - WINDOW, 128), jnp.bfloat16),
        ((WINDOW, width), jnp.float32),
    )
    specs = [fixed(shape) for shape, _ in outs]
    specs[3] = pl.BlockSpec((slots - WINDOW, width), lambda j, at, more: (0, jnp.maximum(j - 1, 0)))
    return pl.pallas_call(
        project_kernel,
        grid_spec=pltpu.PrefetchScalarGridSpec(
            num_scalar_prefetch=2,
            grid=(3,),
            in_specs=[
                whole,
                fixed((slots // 128, 128)),
                whole,
                fixed(norms.shape),
                pl.BlockSpec((width, width), lambda j, at, more: (0, j)),
            ],
            out_specs=specs,
            scratch_shapes=[
                pltpu.VMEM((2 * slots, width), jnp.bfloat16),
                pltpu.VMEM((2 * slots, 128), jnp.bfloat16),
            ],
        ),
        out_shape=[jax.ShapeDtypeStruct(shape, dtype) for shape, dtype in outs],
        cost_estimate=cost(
            flops=2 * slots * width * 2 * width,
            transcendentals=slots,
            bytes_accessed=14 * slots * width,
        ),
    )(context, queries, inputs, row_mask.reshape(slots // 128, 128), cotangent, norms, w_qkv)


def attend_kernel(
    keep_logs, query_ref, key_ref, value_ref, dead_ref, row_ref, rows_ref, wout_ref, *outs
):
    attended_ref, hidden_ref, unit_ref, inverse_ref = outs[:4]
    log_ref, attended = outs[-2:]
    step = pl.program_id(1)
    block = query_ref.shape[0]
    first_lane = columns([jnp.ones((2 * block, 1), jnp.float32)])
    queries = both_heads(query_ref[...] * jnp.bfloat16(score_factor))
    queries = jnp.concatenate([queries, first_lane], axis=1)
    keys = jnp.concatenate([key_ref[...], dead_ref[...]], axis=1)
    values = jnp.concatenate([value_ref[...], ones_block(key_ref.shape[0])], axis=1)
    scores = [dot(queries[k : k + PIECE], keys, 1, 1) for k in range(0, 2 * block, PIECE)]
    exponents = [
        jnp.exp(part - jnp.max(part, axis=-1, keepdims=True)).astype(jnp.bfloat16) for part in scores
    ]
    parts, totals = [], []
    for exponent in exponents:
        summed = dot(exponent, values)
        totals.append(summed[:, 2 * HEAD :])
        parts.append(summed[:, : 2 * HEAD] / summed[:, 2 * HEAD :])
    if keep_logs:
        logs = [
            jnp.max(part, axis=-1, keepdims=True) + jnp.log(total) for part, total in zip(scores, totals)
        ]
        log_ref[...] = one_head(jnp.concatenate(logs, axis=0))
    both = one_head(jnp.concatenate(parts, axis=0))
    both = jnp.where(row_ref[...] > 0, both, 0.0).astype(jnp.bfloat16)
    attended_ref[...] = both
    attended[:, pl.ds(pl.multiple_of(step * 2 * HEAD, 2 * HEAD), 2 * HEAD)] = both

    @pl.when(step == pl.num_programs(1) - 1)
    def _():
        hidden = rows_ref[...].astype(jnp.float32) + dot(attended[...], wout_ref[...])
        hidden_ref[...] = hidden
        unit_ref[...], inverse_ref[...] = norm_rows(hidden)


def attend(query_rows, packed_keys, key_dead, row_live, rows, w_out, from_query, from_row, keep_logs):
    slots, block, width = WINDOW, WINDOW, query_rows.shape[1]
    keys_len = packed_keys.shape[0]
    pairs = width // (2 * HEAD)
    whole = pl.BlockSpec((block, width), lambda r, p: (r, 0))
    return pl.pallas_call(
        partial(attend_kernel, keep_logs),
        grid=(slots // block, pairs),
        in_specs=[
            pl.BlockSpec((block, 2 * HEAD), lambda r, p: (from_query, p)),
            pl.BlockSpec((keys_len, 2 * HEAD), lambda r, p: (0, p)),
            pl.BlockSpec((keys_len, 2 * HEAD), lambda r, p: (0, pairs + p)),
            pl.BlockSpec((keys_len, 2 * HEAD), lambda r, p: (0, 0)),
            pl.BlockSpec((block, 1), lambda r, p: (from_row, 0)),
            pl.BlockSpec((block, width), lambda r, p: (from_row, 0)),
            pl.BlockSpec((width, width), lambda r, p: (0, 0)),
        ],
        out_specs=(
            pl.BlockSpec((block, 2 * HEAD), lambda r, p: (r, p)),
            whole,
            whole,
            pl.BlockSpec((block, 1), lambda r, p: (r, 0)),
            *([pl.BlockSpec((block, 2 * HEAD), lambda r, p: (r, p))] if keep_logs else ()),
        ),
        scratch_shapes=[pltpu.VMEM((block, width), jnp.bfloat16)],
        out_shape=(
            jax.ShapeDtypeStruct((slots, width), jnp.bfloat16),
            jax.ShapeDtypeStruct((slots, width), jnp.float32),
            jax.ShapeDtypeStruct((slots, width), jnp.float32),
            jax.ShapeDtypeStruct((slots, 1), jnp.float32),
            *([jax.ShapeDtypeStruct((slots, width), jnp.float32)] if keep_logs else ()),
        ),
        cost_estimate=cost(
            flops=4 * slots * keys_len * width * 4,
            transcendentals=slots * keys_len * HEADS,
            bytes_accessed=12 * slots * width + 4 * keys_len * width,
        ),
    )(query_rows, packed_keys, packed_keys, key_dead, row_live, rows, w_out)


def units_kernel(
    bits, at_ref, own_ref, got_ref, norms_ref, grad_ref, grad_got_ref, up_ref, down_ref, *outs
):
    keep_refs, act_ref, (own_grad, give_grad), (normed, upstream) = outs[:8], outs[8], outs[9:11], outs[11:]
    width = own_ref.shape[1]
    cut = width // 2

    @pl.when(pl.program_id(0) == 0)
    def _():
        for first, part, grad in ((0, own_ref, grad_ref), (WINDOW, got_ref, grad_got_ref)):
            rows = part[...] * norms_ref[2:3] + norms_ref[3:4]
            normed[first : first + WINDOW] = rows.astype(jnp.bfloat16)
            upstream[first : first + WINDOW] = grad[...].astype(jnp.bfloat16)

    pre_act = dot(normed[...], up_ref[...])
    share = gelu_parts(pre_act)
    activated = (pre_act * share).astype(jnp.bfloat16)
    slope = share + pre_act * (root_two_pi * jnp.exp(-0.5 * pre_act * pre_act))
    grad_pre = (dot(upstream[...], down_ref[...], 1, 1) * slope).astype(jnp.bfloat16)
    act_ref[...] = activated
    part = dot(grad_pre, up_ref[...], 1, 1)

    @pl.when(pl.program_id(0) == 0)
    def _():
        own_grad[...], give_grad[...] = part[:WINDOW], part[WINDOW:]

    @pl.when(pl.program_id(0) > 0)
    def _():
        own_grad[...] += part[:WINDOW]
        give_grad[...] += part[WINDOW:]

    for index, (left, right) in enumerate(((activated, upstream), (grad_pre, normed))):
        product = dot(left, right[...], 0, 0)
        mine = (at_ref[0] & bits[index]) != 0
        rows = keep_refs[4 * index].shape[1]
        product = product.reshape(-1, 2, rows, width)
        keep = jnp.where(mine, product[:, 1], product[:, 0])
        give = jnp.where(mine, product[:, 0], product[:, 1])
        for place, (low, high) in enumerate(((0, cut), (cut, width))):
            keep_refs[4 * index + 2 * place][...] = keep[:, :, low:high]
            keep_refs[4 * index + 2 * place + 1][...] = give[:, :, low:high]


def units(me, bits, rows, unit_own, unit_got, norms, upstream, upstream_got, w_up, w_down):
    width, hidden = w_up.shape
    half = hidden // 2
    tile = 8 * rows if 8 * rows >= 384 else 384
    tiles = half // tile
    whole = pl.BlockSpec((WINDOW, width), lambda j, at: (0, 0))
    pieces, shapes = [], []
    for index in range(2):
        size = 2 * rows * (index + 1)
        for _ in range(4):
            pieces.append(
                pl.BlockSpec((tile // (2 * size), size, width // 2), lambda j, at: (j, 0, 0))
            )
            shapes.append(
                jax.ShapeDtypeStruct((half // (2 * size), size, width // 2), jnp.float32)
            )
    acts = pl.BlockSpec((2 * WINDOW, tile), lambda j, at: (0, j))
    return pl.pallas_call(
        partial(units_kernel, bits),
        grid_spec=pltpu.PrefetchScalarGridSpec(
            num_scalar_prefetch=1,
            grid=(tiles,),
            in_specs=[
                whole,
                whole,
                pl.BlockSpec(norms.shape, lambda j, at: (0, 0)),
                whole,
                whole,
                pl.BlockSpec((width, tile), lambda j, at: (0, (at[0] & 1) * tiles + j)),
                pl.BlockSpec((tile, width), lambda j, at: ((at[0] & 1) * tiles + j, 0)),
            ],
            out_specs=(*pieces, acts, whole, whole),
            scratch_shapes=[
                pltpu.VMEM((2 * WINDOW, width), jnp.bfloat16),
                pltpu.VMEM((2 * WINDOW, width), jnp.bfloat16),
            ],
        ),
        out_shape=(
            *shapes,
            jax.ShapeDtypeStruct((2 * WINDOW, half), jnp.bfloat16),
            jax.ShapeDtypeStruct((WINDOW, width), jnp.float32),
            jax.ShapeDtypeStruct((WINDOW, width), jnp.float32),
        ),
        cost_estimate=cost(
            flops=16 * WINDOW * width * half,
            transcendentals=4 * WINDOW * half,
            bytes_accessed=12 * width * half,
        ),
    )(
        me.reshape(1),
        unit_own,
        unit_got,
        norms,
        upstream,
        upstream_got,
        w_up,
        w_down,
    )


def halves_kernel(right_dim, at_ref, left_ref, right_ref, own_ref, give_ref):
    product = dot(left_ref[...], right_ref[...], 1, right_dim)
    own_ref[...], give_ref[...] = product[:WINDOW], product[WINDOW:]


def halves(me, left, right, right_dim):
    rows, half = left.shape
    width = right.shape[1 - right_dim]
    tile = 256
    if right_dim == 1:
        spec = pl.BlockSpec((tile, half), lambda j, at: (j, at[0] & 1))
    else:
        spec = pl.BlockSpec((half, tile), lambda j, at: (at[0] & 1, j))
    out = pl.BlockSpec((WINDOW, tile), lambda j, at: (0, j))
    return pl.pallas_call(
        partial(halves_kernel, right_dim),
        grid_spec=pltpu.PrefetchScalarGridSpec(
            num_scalar_prefetch=1,
            grid=(width // tile,),
            in_specs=[pl.BlockSpec((rows, half), lambda j, at: (0, 0)), spec],
            out_specs=(out, out),
        ),
        out_shape=(jax.ShapeDtypeStruct((WINDOW, width), jnp.float32),) * 2,
        cost_estimate=cost(
            flops=2 * rows * width * half, transcendentals=0, bytes_accessed=4 * width * half
        ),
    )(me.reshape(1), left, right)


def attend_back_kernel(
    query_ref,
    key_ref,
    value_ref,
    dead_ref,
    row_ref,
    attended_ref,
    log_ref,
    own_ref,
    got_ref,
    unit_ref,
    inverse_ref,
    norms_ref,
    upstream_ref,
    wout_ref,
    dq_ref,
    dk_ref,
    dv_ref,
    grad_hidden_ref,
    low_ref,
    sums_ref,
):
    @pl.when(pl.program_id(0) == 0)
    def _():
        grad_norm = own_ref[...] + got_ref[...]
        unit_rows = unit_ref[...]
        sums_ref[...] = column_sums(grad_norm, unit_rows)
        grad_rows = norm_rows_back(grad_norm, unit_rows, inverse_ref[...], norms_ref[2:3])
        grad_hidden = upstream_ref[...] + grad_rows
        grad_hidden_ref[...] = grad_hidden
        low_ref[...] = grad_hidden.astype(jnp.bfloat16)

    block = query_ref.shape[0]
    key_rows = key_ref[...]
    grad = dot(low_ref[...], wout_ref[...], 1, 1)
    grad = jnp.where(row_ref[...] > 0, grad, 0.0).astype(jnp.bfloat16)
    product = grad.astype(jnp.float32) * attended_ref[...].astype(jnp.float32)
    grads = both_heads(grad)
    grads_wide = jnp.concatenate([grads, both_heads((-product).astype(jnp.bfloat16))], axis=1)
    values_wide = jnp.concatenate([value_ref[...], ones_block(key_rows.shape[0])], axis=1)
    lanes = lax.broadcasted_iota(jnp.int32, (block, 2 * HEAD), 1)
    rest = -log_ref[...]
    extra = jnp.zeros((block, 2 * HEAD), jnp.float32)
    for lane in range(1, 4):
        part = rest.astype(jnp.bfloat16).astype(jnp.float32)
        rest = rest - part
        extra = jnp.where((lanes & (HEAD - 1)) == lane, part, extra)
    extra = both_heads(extra)
    wide_lanes = lax.broadcasted_iota(jnp.int32, (2 * block, 2 * HEAD), 1)
    extra = jnp.where(wide_lanes == 0, 1.0, extra).astype(jnp.bfloat16)
    queries = both_heads(query_ref[...] * jnp.bfloat16(score_factor))
    queries_wide = jnp.concatenate([queries, extra], axis=1)
    keys_wide = jnp.concatenate([key_rows, dead_ref[...]], axis=1)
    pieces = [slice(k, k + PIECE) for k in range(0, 2 * block, PIECE)]
    probs = [jnp.exp(dot(queries_wide[piece], keys_wide, 1, 1)) for piece in pieces]
    grad_scores = [
        (prob * dot(grads_wide[piece], values_wide, 1, 1)).astype(jnp.bfloat16)
        for prob, piece in zip(probs, pieces)
    ]
    probs = jnp.concatenate([prob.astype(jnp.bfloat16) for prob in probs], axis=0)
    grad_scores = jnp.concatenate(grad_scores, axis=0)
    dq_ref[...] = (one_head(dot(grad_scores, key_rows)) * score_factor).astype(jnp.bfloat16)
    dk_ref[...] = dot(grad_scores, queries, 0, 0).astype(jnp.bfloat16)
    dv_ref[...] = dot(probs, grads, 0, 0).astype(jnp.bfloat16)


def attend_back(
    query_rows, packed_keys, key_dead, row_live, attended, logs, own, got, unit, inverse, norms, upstream, w_out
):
    slots, width = query_rows.shape
    keys_len = packed_keys.shape[0]
    pairs = width // (2 * HEAD)
    rows_spec = pl.BlockSpec((slots, 2 * HEAD), lambda p: (0, p))
    keys_spec = pl.BlockSpec((keys_len, 2 * HEAD), lambda p: (0, p))
    whole = pl.BlockSpec((slots, width), lambda p: (0, 0))
    column = pl.BlockSpec((slots, 1), lambda p: (0, 0))
    return pl.pallas_call(
        attend_back_kernel,
        grid=(pairs,),
        in_specs=[
            rows_spec,
            keys_spec,
            pl.BlockSpec((keys_len, 2 * HEAD), lambda p: (0, pairs + p)),
            pl.BlockSpec((keys_len, 2 * HEAD), lambda p: (0, 0)),
            column,
            rows_spec,
            rows_spec,
            whole,
            whole,
            whole,
            column,
            pl.BlockSpec(norms.shape, lambda p: (0, 0)),
            whole,
            pl.BlockSpec((2 * HEAD, width), lambda p: (p, 0)),
        ],
        out_specs=(
            rows_spec,
            keys_spec,
            keys_spec,
            whole,
            whole,
            pl.BlockSpec((2, width), lambda p: (0, 0)),
        ),
        out_shape=(
            jax.ShapeDtypeStruct((slots, width), jnp.bfloat16),
            jax.ShapeDtypeStruct((keys_len, width), jnp.bfloat16),
            jax.ShapeDtypeStruct((keys_len, width), jnp.bfloat16),
            jax.ShapeDtypeStruct((slots, width), jnp.float32),
            jax.ShapeDtypeStruct((slots, width), jnp.bfloat16),
            jax.ShapeDtypeStruct((2, width), jnp.float32),
        ),
        cost_estimate=cost(
            flops=10 * slots * keys_len * width * 4,
            transcendentals=slots * keys_len * HEADS,
            bytes_accessed=6 * slots * width + 8 * keys_len * width,
        ),
    )(
        query_rows,
        packed_keys,
        packed_keys,
        key_dead,
        row_live,
        attended,
        logs,
        own,
        got,
        unit,
        inverse,
        norms,
        upstream,
        w_out,
    )


def weights_kernel(
    at_ref, norm_ref, attended_ref, dq_ref, dk_ref, dv_ref, low_ref, keep_a, keep_b, give_a, give_b
):
    for odd, (even_a, even_b, odd_a, odd_b) in (
        (0, (keep_a, keep_b, give_a, give_b)),
        (1, (give_a, give_b, keep_a, keep_b)),
    ):

        @pl.when((at_ref[0] & 1) == odd)
        def _(even_a=even_a, even_b=even_b, odd_a=odd_a, odd_b=odd_b):
            even_a[...] = dot(norm_ref[:WINDOW], dq_ref[...], 0, 0)
            odd_a[...] = dot(norm_ref[WINDOW:], dk_ref[...], 0, 0)
            odd_b[...] = dot(norm_ref[WINDOW:], dv_ref[...], 0, 0)
            even_b[...] = dot(attended_ref[...], low_ref[...], 0, 0)


def weights(me, normed, attended, dq, dk, dv, low):
    slots, width = normed.shape
    tile = 256

    def full(value):
        return pl.BlockSpec(value.shape, lambda j, at: (0, 0))

    out = pl.BlockSpec((tile, width), lambda j, at: (j, 0))
    return pl.pallas_call(
        weights_kernel,
        grid_spec=pltpu.PrefetchScalarGridSpec(
            num_scalar_prefetch=1,
            grid=(width // tile,),
            in_specs=[
                pl.BlockSpec((slots, tile), lambda j, at: (0, j)),
                pl.BlockSpec((WINDOW, tile), lambda j, at: (0, j)),
                full(dq),
                full(dk),
                full(dv),
                full(low),
            ],
            out_specs=(out,) * 4,
        ),
        out_shape=(jax.ShapeDtypeStruct((width, width), jnp.float32),) * 4,
        cost_estimate=cost(
            flops=4 * slots * width * width, transcendentals=0, bytes_accessed=20 * width * width
        ),
    )(me.reshape(1), normed, attended, dq, dk, dv, low)


def rows_back_kernel(dq_ref, dk_ref, dv_ref, rows_ref, hidden_ref, norms_ref, wq, wk, wv, out_ref, sums_ref):
    step = pl.program_id(0)
    unit_rows, inverse = norm_rows(rows_ref[...].astype(jnp.float32))

    def finish(grad_norm):
        sums = column_sums(grad_norm, unit_rows)
        return (norm_rows_back(grad_norm, unit_rows, inverse, norms_ref[0:1]), sums)

    @pl.when(step == 0)
    def _():
        grad_rows, sums = finish(dot(dq_ref[...], wq[...], 1, 1))
        out_ref[...] = grad_rows + hidden_ref[...]
        sums_ref[...] = sums

    @pl.when(step > 0)
    def _():
        grad_rows, sums = finish(dot(dk_ref[...], wk[...], 1, 1) + dot(dv_ref[...], wv[...], 1, 1))
        out_ref[...] = grad_rows
        sums_ref[...] += sums


def rows_back(dq, dk, dv, rows, grad_hidden, norms, w_qkv):
    slots, width = rows.shape
    fixed = pl.BlockSpec((WINDOW, width), lambda r: (0, 0))
    keys = pl.BlockSpec((WINDOW, width), lambda r: (jnp.maximum(r - 1, 0), 0))
    tile = pl.BlockSpec((WINDOW, width), lambda r: (r, 0))
    return pl.pallas_call(
        rows_back_kernel,
        grid=(slots // WINDOW,),
        in_specs=[
            fixed,
            keys,
            keys,
            tile,
            fixed,
            pl.BlockSpec(norms.shape, lambda r: (0, 0)),
            pl.BlockSpec((width, width), lambda r: (0, 0)),
            pl.BlockSpec((width, width), lambda r: (0, 1)),
            pl.BlockSpec((width, width), lambda r: (0, 2)),
        ],
        out_specs=(tile, pl.BlockSpec((2, width), lambda r: (0, 0))),
        out_shape=(
            jax.ShapeDtypeStruct((slots, width), jnp.float32),
            jax.ShapeDtypeStruct((2, width), jnp.float32),
        ),
        cost_estimate=cost(
            flops=4 * slots * width * width, transcendentals=slots, bytes_accessed=12 * slots * width
        ),
    )(dq, dk, dv, rows, grad_hidden, norms, w_qkv, w_qkv, w_qkv)


def place_kernel(bits, far, got, me_ref, factor_ref, a_ref, b_ref, *refs):
    qkv_ref, out_ref, a_wide, b_wide, semaphores = refs[-5:]
    size, width = a_ref.shape
    me = me_ref[0]
    a_wide[...] = a_ref[...] * factor_ref[0, 0]
    b_wide[...] = b_ref[...] * factor_ref[0, 0]
    odd = (me & 1) != 0
    rows = []
    for bit in bits:
        high = (me & bit) != 0
        rows.append(jnp.where(high, 0 if far else size, size if far else 0))
    rows_a, rows_b = (pl.ds(pl.multiple_of(row, size), size) for row in rows)

    def place(targets):
        copies = [
            pltpu.make_async_copy(source, target, semaphores.at[index])
            for index, (source, target) in enumerate(zip((a_wide, b_wide), targets))
        ]
        for copy in copies:
            copy.start()
        for copy in copies:
            copy.wait()

    @pl.when(odd == got)
    def _():
        place((qkv_ref.at[rows_a, pl.ds(0, width)], out_ref.at[rows_b]))

    @pl.when(odd != got)
    def _():
        place((qkv_ref.at[rows_a, pl.ds(width, width)], qkv_ref.at[rows_b, pl.ds(2 * width, width)]))


def put(me, bits, far, got, factor, pieces, held):
    size, width = pieces[0].shape
    scalar = pl.BlockSpec(memory_space=pltpu.SMEM)
    anywhere = pl.BlockSpec(memory_space=pl.ANY)
    vmem = pl.BlockSpec(memory_space=pltpu.VMEM)
    operands = [*pieces, *(held or ())]
    return pl.pallas_call(
        partial(place_kernel, bits, far, got),
        in_specs=[scalar, scalar, vmem, vmem] + [anywhere] * (2 if held else 0),
        out_specs=(anywhere, anywhere),
        out_shape=(
            jax.ShapeDtypeStruct((2 * size, 3 * width), jnp.float32),
            jax.ShapeDtypeStruct((2 * size, width), jnp.float32),
        ),
        scratch_shapes=[
            pltpu.VMEM((size, width), jnp.float32),
            pltpu.VMEM((size, width), jnp.float32),
            pltpu.SemaphoreType.DMA((2,)),
        ],
        input_output_aliases={4: 0, 5: 1} if held else {},
        cost_estimate=cost(flops=0, transcendentals=0, bytes_accessed=8 * width * width),
    )(me.reshape(1), factor, *operands)


def output_kernel(
    at_ref, *refs
):
    units, hiddens, (own_ref, got_ref, base_ref, norms_ref, up_ref, down_ref) = refs[:3], refs[3:6], refs[6:12]
    out_ref, normed, total, twice = refs[12:]
    step = pl.program_id(0)
    slots, width = out_ref.shape

    @pl.when(step == 0)
    def _():
        for index in range(3):
            rows = slice(index * WINDOW, (index + 1) * WINDOW)
            normed[rows] = (units[index][...] * norms_ref[2:3] + norms_ref[3:4]).astype(jnp.bfloat16)
            total[rows] = hiddens[index][...]

    pre_act = dot(normed[...], up_ref[...])
    total[...] += dot((pre_act * gelu_parts(pre_act)).astype(jnp.bfloat16), down_ref[...])

    @pl.when(step == pl.num_programs(0) - 1)
    def _():
        window = (base_ref[...] + (own_ref[...] + got_ref[...])).astype(jnp.bfloat16)
        rest = total[...].astype(jnp.bfloat16)
        for first in (0, slots):
            twice[first : first + WINDOW] = window
            twice[first + WINDOW : first + slots] = rest
        begin = slots - at_ref[0]
        start = pl.multiple_of(begin // 16 * 16, 16)
        shifted = shift_rows(begin - start)
        for first in range(0, slots, WINDOW):
            rows = dot(shifted, twice[pl.ds(start + first, WINDOW + 16), :])
            out_ref[first : first + WINDOW] = rows.astype(jnp.bfloat16)


def output(context, units, hiddens, own, got, base, norms, w_up, w_down):
    width, hidden = w_up.shape
    slots = 4 * WINDOW
    tile = 512
    part = pl.BlockSpec((WINDOW, width), lambda j, at: (0, 0))
    return pl.pallas_call(
        output_kernel,
        grid_spec=pltpu.PrefetchScalarGridSpec(
            num_scalar_prefetch=1,
            grid=(hidden // tile,),
            in_specs=[part] * 9
            + [
                pl.BlockSpec(norms.shape, lambda j, at: (0, 0)),
                pl.BlockSpec((width, tile), lambda j, at: (0, j)),
                pl.BlockSpec((tile, width), lambda j, at: (j, 0)),
            ],
            out_specs=pl.BlockSpec((slots, width), lambda j, at: (0, 0)),
            scratch_shapes=[
                pltpu.VMEM((slots - WINDOW, width), jnp.bfloat16),
                pltpu.VMEM((slots - WINDOW, width), jnp.float32),
                pltpu.VMEM((2 * slots + 16, width), jnp.bfloat16),
            ],
        ),
        out_shape=jax.ShapeDtypeStruct((slots, width), jnp.bfloat16),
        cost_estimate=pl.CostEstimate(
            flops=12 * WINDOW * width * hidden,
            transcendentals=3 * WINDOW * hidden,
            bytes_accessed=8 * width * hidden,
        ),
    )(context, *units, *hiddens, own, got, base, norms, w_up, w_down)


def gelu_parts(values):
    share = 0.5 * (1.0 + lax.erf(values * root_half))
    return share


def local(
    devices,
    inputs,
    context_count,
    query_count,
    row_mask,
    ln1_gain,
    ln1_bias,
    w_qkv,
    w_out,
    ln2_gain,
    ln2_bias,
    w_up,
    w_down,
    cotangent,
):
    slots, width = inputs.shape
    hidden = w_up.shape[1]
    half = hidden // 2
    me = lax.axis_index("rows")
    core = me & 1

    def bit_of(bit):
        return ((me & bit) != 0).astype(jnp.int32)

    def swap(value, bit):
        return lax.ppermute(value, "rows", [(i, i ^ bit) for i in range(devices)])

    def pick(value, axis, index):
        return lax.dynamic_index_in_dim(value, index, axis, keepdims=False)

    bits = []
    bit = 2
    while bit < devices:
        bits.append(bit)
        bit *= 2
    top = bits[-1]

    def order_of(list_of_bits, flip):
        if flip and len(list_of_bits) > 1:
            return [list_of_bits[1], list_of_bits[0]] + list_of_bits[2:]
        return list_of_bits

    context = context_count[0]
    queries = query_count[0]
    norms = jnp.concatenate([ln1_gain, ln1_bias, ln2_gain, ln2_bias]).reshape(4, width)
    tie = lax.optimization_barrier
    rows, normed_low, query_window, packed_keys, row_column, key_dead, upstream = project(
        context_count, query_count, inputs, row_mask, cotangent, norms, w_qkv
    )
    upstream_got = swap(upstream, 1)
    attended_q, hidden_q, unit_two, inverse_two, log_sums = attend(
        query_window, packed_keys, key_dead, row_column, rows, w_out, 0, 0, True
    )
    ff_rows = half // (devices // 2)
    ff_bits = bits[:-1]
    pieces = units(
        me,
        bits[:2],
        ff_rows,
        unit_two,
        swap(unit_two, 1),
        norms,
        upstream,
        upstream_got,
        w_up,
        w_down,
    )
    activated, grad_own, grad_give = pieces[8:]
    pieces = pieces[:8]
    first_bits, second_bits = order_of(bits, False), order_of(bits, True)

    class Halving:
        def __init__(self, terms, axes):
            self.terms, self.axes = terms, list(axes)

        def split(self, bit):
            axis = self.axes.index(bit)
            mine = bit_of(bit)
            self.axes.remove(bit)
            self.kept = sum(pick(term, axis, mine) for term in self.terms)
            self.sent = sum(pick(term, axis, 1 - mine) for term in self.terms)

        def go(self, bit):
            self.terms = [self.kept, swap(self.sent, bit)]

        def send(self, bit):
            self.split(bit)
            self.go(bit)

    def got_of(chains):
        return tuple(chain.terms[1] for chain in chains)

    def set_got(chains, values):
        for chain, value in zip(chains, values):
            chain.terms[1] = value

    def feed_forward(index, place):
        keep, give = pieces[4 * index + 2 * place : 4 * index + 2 * place + 2]
        axes = ff_bits[::-1] + [1]
        axes.remove(ff_order[index][0])
        shape = [2] * len(axes) + [ff_rows, width // 2]
        got = swap(give, ff_order[index][0])
        return Halving([keep.reshape(shape), got.reshape(shape)], axes)

    def to_top(chain):
        pairs = [(i, i ^ top) for i in range(devices) if ((i & top) != 0) != ((i & 1) != 0)]
        value = chain.terms[0] + chain.terms[1]
        chain.terms = [value, lax.ppermute(value, "rows", pairs)]

    def hand_over(chain):
        mine = sum(pick(term, 1, core) for term in chain.terms)
        other = swap(sum(pick(term, 1, 1 - core) for term in chain.terms), 1)
        return jnp.where(bit_of(top) == core, mine, other)

    ff_order = (order_of(ff_bits, False), order_of(ff_bits, True))

    down_one = feed_forward(0, 0)
    up_one = feed_forward(1, 0)
    ones = (down_one, up_one)

    grad_query, grad_key, grad_value, grad_hidden, grad_low, sums_two = attend_back(
        query_window,
        packed_keys,
        key_dead,
        row_column,
        attended_q,
        log_sums,
        grad_own,
        swap(grad_give, 1),
        unit_two,
        inverse_two,
        norms,
        upstream,
        w_out,
    )
    keep_first, keep_second, *give = weights(
        me, normed_low, attended_q, grad_query, grad_key, grad_value, grad_low
    )

    def unroll(value):
        return lax.dynamic_slice(
            jnp.concatenate([value, value], axis=0), (slots - context, 0), (slots, width)
        )

    def joined(chains):
        terms = [jnp.stack([c.terms[k] for c in chains]) for k in range(2)]
        return Halving(terms, [None] + chains[0].axes)

    ones_got, give = tie((got_of(ones), give))
    set_got(ones, ones_got)
    for chain, order in zip(ones, ff_order):
        chain.send(order[1])
    give_first, give_second = swap(give[0], 1), swap(give[1], 1)
    shape = [2] * len(bits) + [width // (2 ** len(bits)), width]
    first = Halving([keep_first.reshape(shape), give_first.reshape(shape)], first_bits)
    second = Halving([keep_second.reshape(shape), give_second.reshape(shape)], second_bits)
    both = (first, second)

    first.send(first_bits[0])
    second.send(second_bits[0])
    grad_query, grad_key, grad_value, ones_got, _ = tie(
        (grad_query, grad_key, grad_value, got_of(ones), give_first)
    )
    set_got(ones, ones_got)
    ones = joined(ones)
    for bit in ff_bits[2:]:
        ones.send(bit)
    grad_rows, sums_one = rows_back(
        grad_query, grad_key, grad_value, rows, grad_hidden, norms, w_qkv
    )
    context_norms, _ = tie((normed_low[WINDOW:], grad_rows))
    context_queries = dot(context_norms, w_qkv[:, :width]).astype(jnp.bfloat16)

    def context_part(index, queries):
        return attend(
            queries, packed_keys, key_dead, row_column, rows, w_out, index, index + 1, False
        )[1:3]

    both_got, ones_got, context_queries, sums_one = tie(
        (got_of(both), ones.terms[1], context_queries, sums_one)
    )
    set_got(both, both_got)
    ones.terms[1] = ones_got

    first.split(first_bits[1])
    second.split(second_bits[1])
    first.sent, second.sent, ones.terms = tie((first.sent, second.sent, ones.terms))
    first.go(first_bits[1])
    second.go(second_bits[1])
    small = jnp.concatenate(
        [sums_one, sums_two, jnp.full((4, width), queries, jnp.float32)], axis=0
    )
    small = small + swap(small, 1)
    small_got = swap(small, top)
    to_top(ones)
    out_own, out_give = halves(me, activated, w_down, 0)
    out_give = swap(out_give, 1)
    both_got, ones_got, pieces, small_got, context_queries, out_own, out_give = tie(
        (got_of(both), ones.terms[1], pieces, small_got, context_queries, out_own, out_give)
    )
    set_got(both, both_got)
    ones.terms[1] = ones_got
    small = small + small_got

    for bit in bits[:2]:
        small = small + swap(small, bit)
    small, pieces = tie((small, pieces))
    down_two = feed_forward(0, 1)
    up_two = feed_forward(1, 1)
    twos = (down_two, up_two)
    both = joined(both)
    for bit in bits[2:-1]:
        both.send(bit)
    for bit in bits[2:-1]:
        small = small + swap(small, bit)
    part_one = context_part(0, context_queries)
    both_got, part_one, small, context_queries = tie(
        (both.terms[1], part_one, small, context_queries)
    )
    both.terms[1] = both_got

    value = both.terms[0] + both.terms[1]
    value_got = swap(value, top)
    part_two = context_part(1, context_queries)
    part_three = context_part(2, context_queries)
    twos_got, part_three = tie((got_of(twos), part_three))
    set_got(twos, twos_got)
    for chain, order in zip(twos, ff_order):
        chain.send(order[1])
    value_got, part_two, part_three, ones.terms = tie(
        (value_got, part_two, part_three, ones.terms)
    )
    value = value + value_got

    def widen(value, bit, axis):
        got = swap(value, bit)
        high = bit_of(bit) == 1
        return jnp.stack(
            [jnp.where(high, got, value), jnp.where(high, value, got)], axis=axis
        )

    for bit in bits[2:-1][::-1]:
        value = widen(value, bit, 1)
    ones = hand_over(ones)
    hiddens, units_c = zip(part_one, part_two, part_three)
    layer_out = output(
        context_count, units_c, hiddens, out_own, out_give, hidden_q, norms, w_up, w_down
    )
    twos_got, value, layer_out, ones = tie((got_of(twos), value, layer_out, ones))
    set_got(twos, twos_got)
    twos = joined(twos)

    first_value = widen(value[0], first_bits[1], 0)
    second_value = widen(value[1], second_bits[1], 0)
    for bit in ff_bits[2:]:
        twos.send(bit)
    grad_rows = unroll(grad_rows)
    first_value, second_value, twos_got, grad_rows, small = tie(
        (first_value, second_value, twos.terms[1], grad_rows, small)
    )
    twos.terms[1] = twos_got
    loss_factor = math.sqrt(devices) * (slots // 4) / small[4, 0]
    factor = loss_factor.reshape(1, 1)

    first_value, second_value = first_value.reshape(-1, width), second_value.reshape(-1, width)
    first_far = swap(first_value, first_bits[0])
    second_far = swap(second_value, second_bits[0])
    first_near = swap(first_value, 1)
    second_near = swap(second_value, 1)
    to_top(twos)
    twos = hand_over(twos)
    small = small * loss_factor
    grad_inputs = grad_rows * loss_factor
    ends = (first_bits[0], second_bits[0])
    held = put(me, ends, False, False, factor, (first_value, second_value), None)
    held = put(me, ends, False, True, factor, (first_near, second_near), held)
    down_share = loss_factor * jnp.concatenate([ones[0], twos[0]], axis=1)
    up_share = loss_factor * jnp.concatenate([ones[1], twos[1]], axis=1).T
    first_far, second_far, down_share, up_share, small, grad_inputs, held = tie(
        (first_far, second_far, down_share, up_share, small, grad_inputs, held)
    )

    first_got = swap(first_far, 1)
    second_got = swap(second_far, 1)
    held = put(me, ends, True, False, factor, (first_far, second_far), held)
    grad_qkv, grad_out = put(me, ends, True, True, factor, (first_got, second_got), held)
    return (
        layer_out,
        grad_inputs,
        small[0],
        small[1],
        grad_qkv,
        grad_out,
        small[2],
        small[3],
        up_share,
        down_share,
    )


def solution(mesh):
    placed = (
        P("rows", None),
        P("rows"),
        P("rows"),
        P("rows"),
        P(),
        P(),
        P(),
        P(),
        P(),
        P(),
        P(),
        P(),
        P("rows", None),
    )
    return jax.shard_map(
        partial(local, mesh.shape["rows"]),
        mesh=mesh,
        in_specs=placed,
        out_specs=(
            P("rows", None),
            P("rows", None),
            P(),
            P(),
            P(),
            P(),
            P(),
            P(),
            P(None, "rows"),
            P("rows", None),
        ),
        check_vma=False,
    )
```

```python
from functools import partial
import math

import jax
import jax.numpy as jnp
from jax import lax
from jax.experimental import pallas as pl
from jax.experimental.pallas import tpu as pltpu
from jax.sharding import PartitionSpec as P

HEADS = 12
HEAD = 64
WINDOW = 256
SHARE = 64
PIECE = 256
STRIP = 768
OUTPUT_TILE = 1024
FIRST_PART = 256

epsilon = 1e-05
score_factor = 1.0 / math.sqrt(HEAD)
masked_score = -3e38
root_half = math.sqrt(0.5)
root_two_pi = math.sqrt(2.0 / math.pi) * 0.5


def dot(left, right, left_dim=1, right_dim=0):
    return lax.dot_general(
        left, right, (((left_dim,), (right_dim,)), ((), ())), preferred_element_type=jnp.float32
    )


def cost(flops, transcendentals, bytes_accessed):
    return pl.CostEstimate(
        flops=flops // SHARE,
        transcendentals=transcendentals // SHARE,
        bytes_accessed=bytes_accessed // SHARE,
    )


def lane_masks(width):
    lanes = lax.broadcasted_iota(jnp.int32, (1, width), 1)
    return (lanes < HEAD, lanes >= HEAD)


def both_heads(rows):
    none = jnp.zeros_like(rows)
    return jnp.concatenate([jnp.where(lanes, rows, none) for lanes in lane_masks(2 * HEAD)], axis=0)


def one_head(rows):
    size = rows.shape[0] // 2
    return jnp.where(lane_masks(2 * HEAD)[0], rows[:size], rows[size:])


def columns(values):
    rows = values[0].shape[0]
    lanes = lax.broadcasted_iota(jnp.int32, (rows, 2 * HEAD), 1)
    block = jnp.zeros((rows, 2 * HEAD), jnp.float32)
    for lane, value in enumerate(values):
        block = jnp.where(lanes == lane, value, block)
    return block.astype(jnp.bfloat16)


def ones_block(rows):
    return jnp.ones((rows, 2 * HEAD), jnp.bfloat16)


def norm_rows(values):
    centre = jnp.mean(values, axis=-1, keepdims=True)
    centred = values - centre
    inverse = lax.rsqrt(jnp.mean(centred * centred, axis=-1, keepdims=True) + epsilon)
    return (centred * inverse, inverse)


def norm_rows_back(grad_norm, unit_rows, inverse, gain):
    grad_unit = grad_norm * gain
    grad_mean = jnp.mean(grad_unit, axis=-1, keepdims=True)
    grad_proj = jnp.mean(grad_unit * unit_rows, axis=-1, keepdims=True)
    return inverse * (grad_unit - grad_mean - unit_rows * grad_proj)


def column_sums(grad_norm, unit_rows):
    return jnp.concatenate(
        [
            jnp.sum(grad_norm * unit_rows, axis=0, keepdims=True),
            jnp.sum(grad_norm, axis=0, keepdims=True),
        ],
        axis=0,
    )


def shift_rows(count):
    taken = lax.broadcasted_iota(jnp.int32, (WINDOW, WINDOW + 16), 1)
    given = lax.broadcasted_iota(jnp.int32, (WINDOW, WINDOW + 16), 0) + count
    return jnp.where(taken == given, 1.0, 0.0).astype(jnp.bfloat16)


def project_kernel(
    context_ref,
    queries_ref,
    rows_ref,
    mask_ref,
    cotangent_ref,
    norms_ref,
    weight_ref,
    rolled_ref,
    norm_ref,
    query_ref,
    packed_ref,
    live_ref,
    dead_ref,
    upstream_ref,
    twice,
    present,
):
    step = pl.program_id(0)
    slots, width = rows_ref.shape

    @pl.when(step == 0)
    def _():
        context, queries = context_ref[0], queries_ref[0]
        start = pl.multiple_of(context // 16 * 16, 16)
        shifted = shift_rows(context - start)
        for half in (slice(0, slots), slice(slots, 2 * slots)):
            twice[half] = rows_ref[...]
        across = lax.broadcasted_iota(jnp.int32, (128, 128), 1)
        down = lax.broadcasted_iota(jnp.int32, (128, 128), 0)
        for group in range(slots // 128):
            kept = (across == down) & (mask_ref[group : group + 1] == 1)
            if group == 0:
                kept = kept | ((across == 0) & (down == 0))
            kept = jnp.where(kept, 1.0, 0.0).astype(jnp.bfloat16)
            marks = dot(kept, jnp.ones((128, 128), jnp.bfloat16)).astype(jnp.bfloat16)
            for first in (0, slots):
                present[first + group * 128 : first + (group + 1) * 128] = marks
        for first in range(0, slots, WINDOW):
            rows = dot(shifted, twice[pl.ds(start + first, WINDOW + 16), :])
            rolled_ref[first : first + WINDOW] = rows.astype(jnp.bfloat16)
            unit_rows = norm_rows(rows)[0]
            norm_ref[first : first + WINDOW] = (
                unit_rows * norms_ref[0:1] + norms_ref[1:2]
            ).astype(jnp.bfloat16)
            here = dot(shifted, present[pl.ds(start + first, WINDOW + 16), :])
            place = lax.broadcasted_iota(jnp.int32, here.shape, 0) + (first + context)
            place = jnp.where(place >= slots, place - slots, place)
            live_ref[first : first + WINDOW] = jnp.where(place < context + queries, here, 0.0)[:, 0:1]
            lanes = lax.broadcasted_iota(jnp.int32, here.shape, 1)
            if first > 0:
                known = (here > 0) & (place < context)
                split = lanes & (HEAD - 1)
                ones = jnp.where((split >= 1) & (split <= 3), 1.0, 0.0)
                dead = jnp.where((lanes == 0) & jnp.logical_not(known), masked_score, ones)
                dead_ref[first - WINDOW : first] = dead.astype(jnp.bfloat16)
            else:
                asked = jnp.where(place < context + queries, here, 0.0)[:, 0:1]
        twice[:slots] = cotangent_ref[...]
        near = jnp.minimum(start, slots - WINDOW - 16)
        near = pl.multiple_of(near, 16)
        upstream_ref[...] = dot(shift_rows(context - near), twice[pl.ds(near, WINDOW + 16), :]) * asked
        query_ref[...] = dot(norm_ref[:WINDOW], weight_ref[...]).astype(jnp.bfloat16)

    @pl.when(step > 0)
    def _():
        packed_ref[...] = dot(norm_ref[WINDOW:], weight_ref[...]).astype(jnp.bfloat16)


def project(context, queries, inputs, row_mask, cotangent, norms, w_qkv):
    slots, width = inputs.shape

    def fixed(shape):
        return pl.BlockSpec(shape, lambda j, at, more: (0, 0))

    whole = fixed((slots, width))
    outs = (
        ((slots, width), jnp.bfloat16),
        ((slots, width), jnp.bfloat16),
        ((WINDOW, width), jnp.bfloat16),
        ((slots - WINDOW, 2 * width), jnp.bfloat16),
        ((slots, 1), jnp.float32),
        ((slots - WINDOW, 128), jnp.bfloat16),
        ((WINDOW, width), jnp.float32),
    )
    specs = [fixed(shape) for shape, _ in outs]
    specs[3] = pl.BlockSpec((slots - WINDOW, width), lambda j, at, more: (0, jnp.maximum(j - 1, 0)))
    return pl.pallas_call(
        project_kernel,
        grid_spec=pltpu.PrefetchScalarGridSpec(
            num_scalar_prefetch=2,
            grid=(3,),
            in_specs=[
                whole,
                fixed((slots // 128, 128)),
                whole,
                fixed(norms.shape),
                pl.BlockSpec((width, width), lambda j, at, more: (0, j)),
            ],
            out_specs=specs,
            scratch_shapes=[
                pltpu.VMEM((2 * slots, width), jnp.bfloat16),
                pltpu.VMEM((2 * slots, 128), jnp.bfloat16),
            ],
        ),
        out_shape=[jax.ShapeDtypeStruct(shape, dtype) for shape, dtype in outs],
        cost_estimate=cost(
            flops=2 * slots * width * 2 * width,
            transcendentals=slots,
            bytes_accessed=14 * slots * width,
        ),
    )(context, queries, inputs, row_mask.reshape(slots // 128, 128), cotangent, norms, w_qkv)


def attend_kernel(
    keep_logs, query_ref, key_ref, value_ref, dead_ref, row_ref, rows_ref, wout_ref, *outs
):
    attended_ref, hidden_ref, unit_ref, inverse_ref = outs[:4]
    log_ref, attended = outs[-2:]
    step = pl.program_id(1)
    block = query_ref.shape[0]
    first_lane = columns([jnp.ones((2 * block, 1), jnp.float32)])
    queries = both_heads(query_ref[...] * jnp.bfloat16(score_factor))
    queries = jnp.concatenate([queries, first_lane], axis=1)
    keys = jnp.concatenate([key_ref[...], dead_ref[...]], axis=1)
    values = jnp.concatenate([value_ref[...], ones_block(key_ref.shape[0])], axis=1)
    scores = [dot(queries[k : k + PIECE], keys, 1, 1) for k in range(0, 2 * block, PIECE)]
    exponents = [
        jnp.exp(part - jnp.max(part, axis=-1, keepdims=True)).astype(jnp.bfloat16) for part in scores
    ]
    parts, totals = [], []
    for exponent in exponents:
        summed = dot(exponent, values)
        totals.append(summed[:, 2 * HEAD :])
        parts.append(summed[:, : 2 * HEAD] / summed[:, 2 * HEAD :])
    if keep_logs:
        logs = [
            jnp.max(part, axis=-1, keepdims=True) + jnp.log(total) for part, total in zip(scores, totals)
        ]
        log_ref[...] = one_head(jnp.concatenate(logs, axis=0))
    both = one_head(jnp.concatenate(parts, axis=0))
    both = jnp.where(row_ref[...] > 0, both, 0.0).astype(jnp.bfloat16)
    attended_ref[...] = both
    attended[:, pl.ds(pl.multiple_of(step * 2 * HEAD, 2 * HEAD), 2 * HEAD)] = both

    @pl.when(step == pl.num_programs(1) - 1)
    def _():
        hidden = rows_ref[...].astype(jnp.float32) + dot(attended[...], wout_ref[...])
        hidden_ref[...] = hidden
        unit_ref[...], inverse_ref[...] = norm_rows(hidden)


def attend(query_rows, packed_keys, key_dead, row_live, rows, w_out, from_query, from_row, keep_logs):
    slots, block, width = WINDOW, WINDOW, query_rows.shape[1]
    keys_len = packed_keys.shape[0]
    pairs = width // (2 * HEAD)
    whole = pl.BlockSpec((block, width), lambda r, p: (r, 0))
    return pl.pallas_call(
        partial(attend_kernel, keep_logs),
        grid=(slots // block, pairs),
        in_specs=[
            pl.BlockSpec((block, 2 * HEAD), lambda r, p: (from_query, p)),
            pl.BlockSpec((keys_len, 2 * HEAD), lambda r, p: (0, p)),
            pl.BlockSpec((keys_len, 2 * HEAD), lambda r, p: (0, pairs + p)),
            pl.BlockSpec((keys_len, 2 * HEAD), lambda r, p: (0, 0)),
            pl.BlockSpec((block, 1), lambda r, p: (from_row, 0)),
            pl.BlockSpec((block, width), lambda r, p: (from_row, 0)),
            pl.BlockSpec((width, width), lambda r, p: (0, 0)),
        ],
        out_specs=(
            pl.BlockSpec((block, 2 * HEAD), lambda r, p: (r, p)),
            whole,
            whole,
            pl.BlockSpec((block, 1), lambda r, p: (r, 0)),
            *([pl.BlockSpec((block, 2 * HEAD), lambda r, p: (r, p))] if keep_logs else ()),
        ),
        scratch_shapes=[pltpu.VMEM((block, width), jnp.bfloat16)],
        out_shape=(
            jax.ShapeDtypeStruct((slots, width), jnp.bfloat16),
            jax.ShapeDtypeStruct((slots, width), jnp.float32),
            jax.ShapeDtypeStruct((slots, width), jnp.float32),
            jax.ShapeDtypeStruct((slots, 1), jnp.float32),
            *([jax.ShapeDtypeStruct((slots, width), jnp.float32)] if keep_logs else ()),
        ),
        cost_estimate=cost(
            flops=4 * slots * keys_len * width * 4,
            transcendentals=slots * keys_len * HEADS,
            bytes_accessed=12 * slots * width + 4 * keys_len * width,
        ),
    )(query_rows, packed_keys, packed_keys, key_dead, row_live, rows, w_out)


def units_kernel(
    bits, at_ref, own_ref, got_ref, norms_ref, grad_ref, grad_got_ref, up_ref, down_ref, *outs
):
    keep_refs, act_ref, (own_grad, give_grad), (normed, upstream) = outs[:8], outs[8], outs[9:11], outs[11:]
    width = own_ref.shape[1]
    cut = FIRST_PART

    @pl.when(pl.program_id(0) == 0)
    def _():
        for first, part, grad in ((0, own_ref, grad_ref), (WINDOW, got_ref, grad_got_ref)):
            rows = part[...] * norms_ref[2:3] + norms_ref[3:4]
            normed[first : first + WINDOW] = rows.astype(jnp.bfloat16)
            upstream[first : first + WINDOW] = grad[...].astype(jnp.bfloat16)

    tile = up_ref.shape[1]
    acts, pres = [], []
    for first in range(0, tile, STRIP):
        strip = slice(first, first + STRIP)
        pre_act = dot(normed[...], up_ref[:, strip])
        share = gelu_parts(pre_act)
        acts.append((pre_act * share).astype(jnp.bfloat16))
        slope = share + pre_act * (root_two_pi * jnp.exp(-0.5 * pre_act * pre_act))
        pres.append((dot(upstream[...], down_ref[strip], 1, 1) * slope).astype(jnp.bfloat16))
    act_ref[...] = jnp.concatenate(acts, axis=1)
    grad_pre = jnp.concatenate(pres, axis=1)
    part = dot(grad_pre, up_ref[...], 1, 1)

    @pl.when(pl.program_id(0) == 0)
    def _():
        own_grad[...], give_grad[...] = part[:WINDOW], part[WINDOW:]

    @pl.when(pl.program_id(0) > 0)
    def _():
        own_grad[...] += part[:WINDOW]
        give_grad[...] += part[WINDOW:]

    for index, (lefts, right) in enumerate(((acts, upstream), (pres, normed))):
        product = jnp.concatenate([dot(left, right[...], 0, 0) for left in lefts], axis=0)
        mine = (at_ref[0] & bits[index]) != 0
        rows = keep_refs[4 * index].shape[1]
        product = product.reshape(-1, 2, rows, width)
        keep = jnp.where(mine, product[:, 1], product[:, 0])
        give = jnp.where(mine, product[:, 0], product[:, 1])
        for place, (low, high) in enumerate(((0, cut), (cut, width))):
            keep_refs[4 * index + 2 * place][...] = keep[:, :, low:high]
            keep_refs[4 * index + 2 * place + 1][...] = give[:, :, low:high]


def units(me, bits, rows, unit_own, unit_got, norms, upstream, upstream_got, w_up, w_down):
    width, hidden = w_up.shape
    half = hidden // 2
    tile = 8 * rows if 8 * rows >= 384 else 384
    tiles = half // tile
    whole = pl.BlockSpec((WINDOW, width), lambda j, at: (0, 0))
    pieces, shapes = [], []
    for index in range(2):
        size = 2 * rows * (index + 1)
        for span in (FIRST_PART, FIRST_PART, width - FIRST_PART, width - FIRST_PART):
            pieces.append(pl.BlockSpec((tile // (2 * size), size, span), lambda j, at: (j, 0, 0)))
            shapes.append(jax.ShapeDtypeStruct((half // (2 * size), size, span), jnp.float32))
    acts = pl.BlockSpec((2 * WINDOW, tile), lambda j, at: (0, j))
    return pl.pallas_call(
        partial(units_kernel, bits),
        grid_spec=pltpu.PrefetchScalarGridSpec(
            num_scalar_prefetch=1,
            grid=(tiles,),
            in_specs=[
                whole,
                whole,
                pl.BlockSpec(norms.shape, lambda j, at: (0, 0)),
                whole,
                whole,
                pl.BlockSpec((width, tile), lambda j, at: (0, (at[0] & 1) * tiles + j)),
                pl.BlockSpec((tile, width), lambda j, at: ((at[0] & 1) * tiles + j, 0)),
            ],
            out_specs=(*pieces, acts, whole, whole),
            scratch_shapes=[
                pltpu.VMEM((2 * WINDOW, width), jnp.bfloat16),
                pltpu.VMEM((2 * WINDOW, width), jnp.bfloat16),
            ],
        ),
        out_shape=(
            *shapes,
            jax.ShapeDtypeStruct((2 * WINDOW, half), jnp.bfloat16),
            jax.ShapeDtypeStruct((WINDOW, width), jnp.float32),
            jax.ShapeDtypeStruct((WINDOW, width), jnp.float32),
        ),
        cost_estimate=cost(
            flops=16 * WINDOW * width * half,
            transcendentals=4 * WINDOW * half,
            bytes_accessed=12 * width * half,
        ),
    )(
        me.reshape(1),
        unit_own,
        unit_got,
        norms,
        upstream,
        upstream_got,
        w_up,
        w_down,
    )


def halves_kernel(right_dim, at_ref, left_ref, right_ref, own_ref, give_ref):
    product = dot(left_ref[...], right_ref[...], 1, right_dim)
    own_ref[...], give_ref[...] = product[:WINDOW], product[WINDOW:]


def halves(me, left, right, right_dim):
    rows, half = left.shape
    width = right.shape[1 - right_dim]
    tile = 256
    if right_dim == 1:
        spec = pl.BlockSpec((tile, half), lambda j, at: (j, at[0] & 1))
    else:
        spec = pl.BlockSpec((half, tile), lambda j, at: (at[0] & 1, j))
    out = pl.BlockSpec((WINDOW, tile), lambda j, at: (0, j))
    return pl.pallas_call(
        partial(halves_kernel, right_dim),
        grid_spec=pltpu.PrefetchScalarGridSpec(
            num_scalar_prefetch=1,
            grid=(width // tile,),
            in_specs=[pl.BlockSpec((rows, half), lambda j, at: (0, 0)), spec],
            out_specs=(out, out),
        ),
        out_shape=(jax.ShapeDtypeStruct((WINDOW, width), jnp.float32),) * 2,
        cost_estimate=cost(
            flops=2 * rows * width * half, transcendentals=0, bytes_accessed=4 * width * half
        ),
    )(me.reshape(1), left, right)


def attend_back_kernel(
    query_ref,
    key_ref,
    value_ref,
    dead_ref,
    row_ref,
    attended_ref,
    log_ref,
    own_ref,
    got_ref,
    unit_ref,
    inverse_ref,
    norms_ref,
    upstream_ref,
    wout_ref,
    dq_ref,
    dk_ref,
    dv_ref,
    grad_hidden_ref,
    low_ref,
    sums_ref,
):
    @pl.when(pl.program_id(0) == 0)
    def _():
        grad_norm = own_ref[...] + got_ref[...]
        unit_rows = unit_ref[...]
        sums_ref[...] = column_sums(grad_norm, unit_rows)
        grad_rows = norm_rows_back(grad_norm, unit_rows, inverse_ref[...], norms_ref[2:3])
        grad_hidden = upstream_ref[...] + grad_rows
        grad_hidden_ref[...] = grad_hidden
        low_ref[...] = grad_hidden.astype(jnp.bfloat16)

    block = query_ref.shape[0]
    key_rows = key_ref[...]
    grad = dot(low_ref[...], wout_ref[...], 1, 1)
    grad = jnp.where(row_ref[...] > 0, grad, 0.0).astype(jnp.bfloat16)
    product = grad.astype(jnp.float32) * attended_ref[...].astype(jnp.float32)
    grads = both_heads(grad)
    grads_wide = jnp.concatenate([grads, both_heads((-product).astype(jnp.bfloat16))], axis=1)
    values_wide = jnp.concatenate([value_ref[...], ones_block(key_rows.shape[0])], axis=1)
    lanes = lax.broadcasted_iota(jnp.int32, (block, 2 * HEAD), 1)
    rest = -log_ref[...]
    extra = jnp.zeros((block, 2 * HEAD), jnp.float32)
    for lane in range(1, 4):
        part = rest.astype(jnp.bfloat16).astype(jnp.float32)
        rest = rest - part
        extra = jnp.where((lanes & (HEAD - 1)) == lane, part, extra)
    extra = both_heads(extra)
    wide_lanes = lax.broadcasted_iota(jnp.int32, (2 * block, 2 * HEAD), 1)
    extra = jnp.where(wide_lanes == 0, 1.0, extra).astype(jnp.bfloat16)
    queries = both_heads(query_ref[...] * jnp.bfloat16(score_factor))
    queries_wide = jnp.concatenate([queries, extra], axis=1)
    keys_wide = jnp.concatenate([key_rows, dead_ref[...]], axis=1)
    pieces = [slice(k, k + PIECE) for k in range(0, 2 * block, PIECE)]
    probs = [jnp.exp(dot(queries_wide[piece], keys_wide, 1, 1)) for piece in pieces]
    grad_scores = [
        (prob * dot(grads_wide[piece], values_wide, 1, 1)).astype(jnp.bfloat16)
        for prob, piece in zip(probs, pieces)
    ]
    probs = jnp.concatenate([prob.astype(jnp.bfloat16) for prob in probs], axis=0)
    grad_scores = jnp.concatenate(grad_scores, axis=0)
    dq_ref[...] = (one_head(dot(grad_scores, key_rows)) * score_factor).astype(jnp.bfloat16)
    dk_ref[...] = dot(grad_scores, queries, 0, 0).astype(jnp.bfloat16)
    dv_ref[...] = dot(probs, grads, 0, 0).astype(jnp.bfloat16)


def attend_back(
    query_rows, packed_keys, key_dead, row_live, attended, logs, own, got, unit, inverse, norms, upstream, w_out
):
    slots, width = query_rows.shape
    keys_len = packed_keys.shape[0]
    pairs = width // (2 * HEAD)
    rows_spec = pl.BlockSpec((slots, 2 * HEAD), lambda p: (0, p))
    keys_spec = pl.BlockSpec((keys_len, 2 * HEAD), lambda p: (0, p))
    whole = pl.BlockSpec((slots, width), lambda p: (0, 0))
    column = pl.BlockSpec((slots, 1), lambda p: (0, 0))
    return pl.pallas_call(
        attend_back_kernel,
        grid=(pairs,),
        in_specs=[
            rows_spec,
            keys_spec,
            pl.BlockSpec((keys_len, 2 * HEAD), lambda p: (0, pairs + p)),
            pl.BlockSpec((keys_len, 2 * HEAD), lambda p: (0, 0)),
            column,
            rows_spec,
            rows_spec,
            whole,
            whole,
            whole,
            column,
            pl.BlockSpec(norms.shape, lambda p: (0, 0)),
            whole,
            pl.BlockSpec((2 * HEAD, width), lambda p: (p, 0)),
        ],
        out_specs=(
            rows_spec,
            keys_spec,
            keys_spec,
            whole,
            whole,
            pl.BlockSpec((2, width), lambda p: (0, 0)),
        ),
        out_shape=(
            jax.ShapeDtypeStruct((slots, width), jnp.bfloat16),
            jax.ShapeDtypeStruct((keys_len, width), jnp.bfloat16),
            jax.ShapeDtypeStruct((keys_len, width), jnp.bfloat16),
            jax.ShapeDtypeStruct((slots, width), jnp.float32),
            jax.ShapeDtypeStruct((slots, width), jnp.bfloat16),
            jax.ShapeDtypeStruct((2, width), jnp.float32),
        ),
        cost_estimate=cost(
            flops=10 * slots * keys_len * width * 4,
            transcendentals=slots * keys_len * HEADS,
            bytes_accessed=6 * slots * width + 8 * keys_len * width,
        ),
    )(
        query_rows,
        packed_keys,
        packed_keys,
        key_dead,
        row_live,
        attended,
        logs,
        own,
        got,
        unit,
        inverse,
        norms,
        upstream,
        w_out,
    )


def weights_kernel(
    at_ref, norm_ref, attended_ref, dq_ref, dk_ref, dv_ref, low_ref, keep_a, keep_b, give_a, give_b
):
    for odd, (even_a, even_b, odd_a, odd_b) in (
        (0, (keep_a, keep_b, give_a, give_b)),
        (1, (give_a, give_b, keep_a, keep_b)),
    ):

        @pl.when((at_ref[0] & 1) == odd)
        def _(even_a=even_a, even_b=even_b, odd_a=odd_a, odd_b=odd_b):
            even_a[...] = dot(norm_ref[:WINDOW], dq_ref[...], 0, 0)
            odd_a[...] = dot(norm_ref[WINDOW:], dk_ref[...], 0, 0)
            odd_b[...] = dot(norm_ref[WINDOW:], dv_ref[...], 0, 0)
            even_b[...] = dot(attended_ref[...], low_ref[...], 0, 0)


def weights(me, normed, attended, dq, dk, dv, low):
    slots, width = normed.shape
    tile = 256

    def full(value):
        return pl.BlockSpec(value.shape, lambda j, at: (0, 0))

    out = pl.BlockSpec((tile, width), lambda j, at: (j, 0))
    return pl.pallas_call(
        weights_kernel,
        grid_spec=pltpu.PrefetchScalarGridSpec(
            num_scalar_prefetch=1,
            grid=(width // tile,),
            in_specs=[
                pl.BlockSpec((slots, tile), lambda j, at: (0, j)),
                pl.BlockSpec((WINDOW, tile), lambda j, at: (0, j)),
                full(dq),
                full(dk),
                full(dv),
                full(low),
            ],
            out_specs=(out,) * 4,
        ),
        out_shape=(jax.ShapeDtypeStruct((width, width), jnp.float32),) * 4,
        cost_estimate=cost(
            flops=4 * slots * width * width, transcendentals=0, bytes_accessed=20 * width * width
        ),
    )(me.reshape(1), normed, attended, dq, dk, dv, low)


def rows_back_kernel(dq_ref, dk_ref, dv_ref, rows_ref, hidden_ref, norms_ref, wq, wk, wv, out_ref, sums_ref):
    step = pl.program_id(0)
    unit_rows, inverse = norm_rows(rows_ref[...].astype(jnp.float32))

    def finish(grad_norm):
        sums = column_sums(grad_norm, unit_rows)
        return (norm_rows_back(grad_norm, unit_rows, inverse, norms_ref[0:1]), sums)

    @pl.when(step == 0)
    def _():
        grad_rows, sums = finish(dot(dq_ref[...], wq[...], 1, 1))
        out_ref[...] = grad_rows + hidden_ref[...]
        sums_ref[...] = sums

    @pl.when(step > 0)
    def _():
        grad_rows, sums = finish(dot(dk_ref[...], wk[...], 1, 1) + dot(dv_ref[...], wv[...], 1, 1))
        out_ref[...] = grad_rows
        sums_ref[...] += sums


def rows_back(dq, dk, dv, rows, grad_hidden, norms, w_qkv):
    slots, width = rows.shape
    fixed = pl.BlockSpec((WINDOW, width), lambda r: (0, 0))
    keys = pl.BlockSpec((WINDOW, width), lambda r: (jnp.maximum(r - 1, 0), 0))
    tile = pl.BlockSpec((WINDOW, width), lambda r: (r, 0))
    return pl.pallas_call(
        rows_back_kernel,
        grid=(slots // WINDOW,),
        in_specs=[
            fixed,
            keys,
            keys,
            tile,
            fixed,
            pl.BlockSpec(norms.shape, lambda r: (0, 0)),
            pl.BlockSpec((width, width), lambda r: (0, 0)),
            pl.BlockSpec((width, width), lambda r: (0, 1)),
            pl.BlockSpec((width, width), lambda r: (0, 2)),
        ],
        out_specs=(tile, pl.BlockSpec((2, width), lambda r: (0, 0))),
        out_shape=(
            jax.ShapeDtypeStruct((slots, width), jnp.float32),
            jax.ShapeDtypeStruct((2, width), jnp.float32),
        ),
        cost_estimate=cost(
            flops=4 * slots * width * width, transcendentals=slots, bytes_accessed=12 * slots * width
        ),
    )(dq, dk, dv, rows, grad_hidden, norms, w_qkv, w_qkv, w_qkv)


def place_kernel(bits, far, got, me_ref, factor_ref, a_ref, b_ref, *refs):
    qkv_ref, out_ref, a_wide, b_wide, semaphores = refs[-5:]
    size, width = a_ref.shape
    me = me_ref[0]
    a_wide[...] = a_ref[...] * factor_ref[0, 0]
    b_wide[...] = b_ref[...] * factor_ref[0, 0]
    odd = (me & 1) != 0
    rows = []
    for bit in bits:
        high = (me & bit) != 0
        rows.append(jnp.where(high, 0 if far else size, size if far else 0))
    rows_a, rows_b = (pl.ds(pl.multiple_of(row, size), size) for row in rows)

    def place(targets):
        copies = [
            pltpu.make_async_copy(source, target, semaphores.at[index])
            for index, (source, target) in enumerate(zip((a_wide, b_wide), targets))
        ]
        for copy in copies:
            copy.start()
        for copy in copies:
            copy.wait()

    @pl.when(odd == got)
    def _():
        place((qkv_ref.at[rows_a, pl.ds(0, width)], out_ref.at[rows_b]))

    @pl.when(odd != got)
    def _():
        place((qkv_ref.at[rows_a, pl.ds(width, width)], qkv_ref.at[rows_b, pl.ds(2 * width, width)]))


def put(me, bits, far, got, factor, pieces, held):
    size, width = pieces[0].shape
    scalar = pl.BlockSpec(memory_space=pltpu.SMEM)
    anywhere = pl.BlockSpec(memory_space=pl.ANY)
    vmem = pl.BlockSpec(memory_space=pltpu.VMEM)
    operands = [*pieces, *(held or ())]
    return pl.pallas_call(
        partial(place_kernel, bits, far, got),
        in_specs=[scalar, scalar, vmem, vmem] + [anywhere] * (2 if held else 0),
        out_specs=(anywhere, anywhere),
        out_shape=(
            jax.ShapeDtypeStruct((2 * size, 3 * width), jnp.float32),
            jax.ShapeDtypeStruct((2 * size, width), jnp.float32),
        ),
        scratch_shapes=[
            pltpu.VMEM((size, width), jnp.float32),
            pltpu.VMEM((size, width), jnp.float32),
            pltpu.SemaphoreType.DMA((2,)),
        ],
        input_output_aliases={4: 0, 5: 1} if held else {},
        cost_estimate=cost(flops=0, transcendentals=0, bytes_accessed=8 * width * width),
    )(me.reshape(1), factor, *operands)


def output_kernel(
    at_ref, *refs
):
    units, hiddens, (own_ref, got_ref, base_ref, norms_ref, up_ref, down_ref) = refs[:3], refs[3:6], refs[6:12]
    out_ref, normed, total, twice = refs[12:]
    step = pl.program_id(0)
    slots, width = out_ref.shape

    @pl.when(step == 0)
    def _():
        for index in range(3):
            rows = slice(index * WINDOW, (index + 1) * WINDOW)
            normed[rows] = (units[index][...] * norms_ref[2:3] + norms_ref[3:4]).astype(jnp.bfloat16)
            total[rows] = hiddens[index][...]

    acts = []
    for first in range(0, up_ref.shape[1], 512):
        pre_act = dot(normed[...], up_ref[:, first : first + 512])
        acts.append((pre_act * gelu_parts(pre_act)).astype(jnp.bfloat16))
    total[...] += dot(jnp.concatenate(acts, axis=1), down_ref[...])

    @pl.when(step == pl.num_programs(0) - 1)
    def _():
        window = (base_ref[...] + (own_ref[...] + got_ref[...])).astype(jnp.bfloat16)
        rest = total[...].astype(jnp.bfloat16)
        for first in (0, slots):
            twice[first : first + WINDOW] = window
            twice[first + WINDOW : first + slots] = rest
        begin = slots - at_ref[0]
        start = pl.multiple_of(begin // 16 * 16, 16)
        shifted = shift_rows(begin - start)
        for first in range(0, slots, WINDOW):
            rows = dot(shifted, twice[pl.ds(start + first, WINDOW + 16), :])
            out_ref[first : first + WINDOW] = rows.astype(jnp.bfloat16)


def output(context, units, hiddens, own, got, base, norms, w_up, w_down):
    width, hidden = w_up.shape
    slots = 4 * WINDOW
    tile = OUTPUT_TILE
    part = pl.BlockSpec((WINDOW, width), lambda j, at: (0, 0))
    return pl.pallas_call(
        output_kernel,
        grid_spec=pltpu.PrefetchScalarGridSpec(
            num_scalar_prefetch=1,
            grid=(hidden // tile,),
            in_specs=[part] * 9
            + [
                pl.BlockSpec(norms.shape, lambda j, at: (0, 0)),
                pl.BlockSpec((width, tile), lambda j, at: (0, j)),
                pl.BlockSpec((tile, width), lambda j, at: (j, 0)),
            ],
            out_specs=pl.BlockSpec((slots, width), lambda j, at: (0, 0)),
            scratch_shapes=[
                pltpu.VMEM((slots - WINDOW, width), jnp.bfloat16),
                pltpu.VMEM((slots - WINDOW, width), jnp.float32),
                pltpu.VMEM((2 * slots + 16, width), jnp.bfloat16),
            ],
        ),
        out_shape=jax.ShapeDtypeStruct((slots, width), jnp.bfloat16),
        cost_estimate=pl.CostEstimate(
            flops=12 * WINDOW * width * hidden,
            transcendentals=3 * WINDOW * hidden,
            bytes_accessed=8 * width * hidden,
        ),
    )(context, *units, *hiddens, own, got, base, norms, w_up, w_down)


def gelu_parts(values):
    share = 0.5 * (1.0 + lax.erf(values * root_half))
    return share


def local(
    devices,
    inputs,
    context_count,
    query_count,
    row_mask,
    ln1_gain,
    ln1_bias,
    w_qkv,
    w_out,
    ln2_gain,
    ln2_bias,
    w_up,
    w_down,
    cotangent,
):
    slots, width = inputs.shape
    hidden = w_up.shape[1]
    half = hidden // 2
    me = lax.axis_index("rows")
    core = me & 1

    def bit_of(bit):
        return ((me & bit) != 0).astype(jnp.int32)

    def swap(value, bit):
        return lax.ppermute(value, "rows", [(i, i ^ bit) for i in range(devices)])

    def pick(value, axis, index):
        return lax.dynamic_index_in_dim(value, index, axis, keepdims=False)

    bits = []
    bit = 2
    while bit < devices:
        bits.append(bit)
        bit *= 2
    top = bits[-1]

    def order_of(list_of_bits, flip):
        if flip and len(list_of_bits) > 1:
            return [list_of_bits[1], list_of_bits[0]] + list_of_bits[2:]
        return list_of_bits

    context = context_count[0]
    queries = query_count[0]
    norms = jnp.concatenate([ln1_gain, ln1_bias, ln2_gain, ln2_bias]).reshape(4, width)
    tie = lax.optimization_barrier
    rows, normed_low, query_window, packed_keys, row_column, key_dead, upstream = project(
        context_count, query_count, inputs, row_mask, cotangent, norms, w_qkv
    )
    upstream_got = swap(upstream, 1)
    attended_q, hidden_q, unit_two, inverse_two, log_sums = attend(
        query_window, packed_keys, key_dead, row_column, rows, w_out, 0, 0, True
    )
    ff_rows = half // (devices // 2)
    ff_bits = bits[:-1]
    pieces = units(
        me,
        bits[:2],
        ff_rows,
        unit_two,
        swap(unit_two, 1),
        norms,
        upstream,
        upstream_got,
        w_up,
        w_down,
    )
    activated, grad_own, grad_give = pieces[8:]
    pieces = pieces[:8]
    first_bits, second_bits = order_of(bits, False), order_of(bits, True)

    class Halving:
        def __init__(self, terms, axes):
            self.terms, self.axes = terms, list(axes)

        def split(self, bit):
            axis = self.axes.index(bit)
            mine = bit_of(bit)
            self.axes.remove(bit)
            self.kept = sum(pick(term, axis, mine) for term in self.terms)
            self.sent = sum(pick(term, axis, 1 - mine) for term in self.terms)

        def go(self, bit):
            self.terms = [self.kept, swap(self.sent, bit)]

        def send(self, bit):
            self.split(bit)
            self.go(bit)

    def got_of(chains):
        return tuple(chain.terms[1] for chain in chains)

    def set_got(chains, values):
        for chain, value in zip(chains, values):
            chain.terms[1] = value

    def feed_forward(index, place):
        keep, give = pieces[4 * index + 2 * place : 4 * index + 2 * place + 2]
        axes = ff_bits[::-1] + [1]
        axes.remove(ff_order[index][0])
        shape = [2] * len(axes) + [ff_rows, keep.shape[-1]]
        got = swap(give, ff_order[index][0])
        return Halving([keep.reshape(shape), got.reshape(shape)], axes)

    def to_top(chain):
        pairs = [(i, i ^ top) for i in range(devices) if ((i & top) != 0) != ((i & 1) != 0)]
        value = chain.terms[0] + chain.terms[1]
        chain.terms = [value, lax.ppermute(value, "rows", pairs)]

    def hand_over(chain):
        mine = sum(pick(term, 1, core) for term in chain.terms)
        other = swap(sum(pick(term, 1, 1 - core) for term in chain.terms), 1)
        return jnp.where(bit_of(top) == core, mine, other)

    ff_order = (order_of(ff_bits, False), order_of(ff_bits, True))

    down_one = feed_forward(0, 0)
    up_one = feed_forward(1, 0)
    ones = (down_one, up_one)

    grad_query, grad_key, grad_value, grad_hidden, grad_low, sums_two = attend_back(
        query_window,
        packed_keys,
        key_dead,
        row_column,
        attended_q,
        log_sums,
        grad_own,
        swap(grad_give, 1),
        unit_two,
        inverse_two,
        norms,
        upstream,
        w_out,
    )
    keep_first, keep_second, *give = weights(
        me, normed_low, attended_q, grad_query, grad_key, grad_value, grad_low
    )

    def unroll(value):
        return lax.dynamic_slice(
            jnp.concatenate([value, value], axis=0), (slots - context, 0), (slots, width)
        )

    def joined(chains):
        terms = [jnp.stack([c.terms[k] for c in chains]) for k in range(2)]
        return Halving(terms, [None] + chains[0].axes)

    ones_got, give = tie((got_of(ones), give))
    set_got(ones, ones_got)
    for chain, order in zip(ones, ff_order):
        chain.send(order[1])
    give_first, give_second = swap(give[0], 1), swap(give[1], 1)
    shape = [2] * len(bits) + [width // (2 ** len(bits)), width]
    first = Halving([keep_first.reshape(shape), give_first.reshape(shape)], first_bits)
    second = Halving([keep_second.reshape(shape), give_second.reshape(shape)], second_bits)
    both = (first, second)

    first.split(first_bits[0])
    second.split(second_bits[0])
    first.sent, second.sent, grad_query, grad_key, grad_value, ones_got = tie(
        (first.sent, second.sent, grad_query, grad_key, grad_value, got_of(ones))
    )
    set_got(ones, ones_got)
    first.go(first_bits[0])
    second.go(second_bits[0])
    ones = joined(ones)
    for bit in ff_bits[2:]:
        ones.send(bit)
    to_top(ones)
    grad_query, _ = tie((grad_query, ones.terms[0]))
    grad_rows, sums_one = rows_back(
        grad_query, grad_key, grad_value, rows, grad_hidden, norms, w_qkv
    )
    context_norms, _ = tie((normed_low[WINDOW:], grad_rows))
    context_queries = dot(context_norms, w_qkv[:, :width]).astype(jnp.bfloat16)

    def context_part(index, queries):
        return attend(
            queries, packed_keys, key_dead, row_column, rows, w_out, index, index + 1, False
        )[1:3]

    out_own, out_give = halves(me, activated, w_down, 0)
    out_give = swap(out_give, 1)
    both_got, ones_got, context_queries, sums_one, out_own, out_give = tie(
        (got_of(both), ones.terms[1], context_queries, sums_one, out_own, out_give)
    )
    set_got(both, both_got)
    ones.terms[1] = ones_got

    first.split(first_bits[1])
    second.split(second_bits[1])
    first.sent, second.sent, ones.terms, sums_one, context_queries = tie(
        (first.sent, second.sent, ones.terms, sums_one, context_queries)
    )
    first.go(first_bits[1])
    second.go(second_bits[1])
    small = jnp.concatenate(
        [sums_one, sums_two, jnp.full((4, width), queries, jnp.float32)], axis=0
    )
    small = small + swap(small, 1)
    part_one = context_part(0, context_queries)
    both_got, small, context_queries, part_one, pieces = tie(
        (got_of(both), small, context_queries, part_one, pieces)
    )
    set_got(both, both_got)
    down_two = feed_forward(0, 1)
    up_two = feed_forward(1, 1)
    twos = (down_two, up_two)

    both = joined(both)
    for bit in bits[2:-1]:
        both.send(bit)
    for bit in bits[2:-1]:
        small = small + swap(small, bit)
    part_two = context_part(1, context_queries)
    both_got, small, part_two, context_queries = tie(
        (both.terms[1], small, part_two, context_queries)
    )
    both.terms[1] = both_got

    value = both.terms[0] + both.terms[1]
    value, context_queries = tie((value, context_queries))
    value_got = swap(value, top)
    part_three = context_part(2, context_queries)
    small, part_three, twos_got = tie((small, part_three, got_of(twos)))
    set_got(twos, twos_got)
    for bit in bits[:2]:
        small = small + swap(small, bit)
    span = (width - FIRST_PART) // 2
    early, late = (
        [
            Halving([term[..., first : first + span] for term in chain.terms], chain.axes)
            for chain in twos
        ]
        for first in (0, span)
    )
    for chain, order in zip(early, ff_order):
        chain.split(order[1])
    early[0].sent, early[1].sent, small = tie((early[0].sent, early[1].sent, small))
    for chain, order in zip(early, ff_order):
        chain.go(order[1])
    for chain, order in zip(late, ff_order):
        chain.split(order[1])
    sent = (late[0].sent, late[1].sent)
    _, early_got, value_got, small, part_two, part_three, ones.terms, grad_rows = tie(
        (sent, got_of(early), value_got, small, part_two, part_three, ones.terms, grad_rows)
    )
    set_got(early, early_got)
    value = value + value_got

    def widen(value, bit, axis):
        got = swap(value, bit)
        high = bit_of(bit) == 1
        return jnp.stack(
            [jnp.where(high, got, value), jnp.where(high, value, got)], axis=axis
        )

    for bit in bits[2:-1][::-1]:
        value = widen(value, bit, 1)
    for chain, order in zip(late, ff_order):
        chain.go(order[1])
    ones = hand_over(ones)
    small = small + swap(small, top)
    value, small, ones, part_one, late_got = tie((value, small, ones, part_one, got_of(late)))
    set_got(late, late_got)
    twos = joined(early + late)
    loss_factor = math.sqrt(devices) * (slots // 4) / small[4, 0]
    factor = loss_factor.reshape(1, 1)

    first_value = widen(value[0], first_bits[1], 0)
    second_value = widen(value[1], second_bits[1], 0)
    for bit in ff_bits[2:]:
        twos.split(bit)
        twos.go(bit)
    grad_inputs = unroll(grad_rows * loss_factor)
    small = small * loss_factor
    first_value, second_value, grad_inputs, small, part_one, twos.terms = tie(
        (first_value, second_value, grad_inputs, small, part_one, twos.terms)
    )

    first_value, second_value = first_value.reshape(-1, width), second_value.reshape(-1, width)
    first_far = swap(first_value, first_bits[0])
    second_far = swap(second_value, second_bits[0])
    first_near = swap(first_value, 1)
    second_near = swap(second_value, 1)
    to_top(twos)
    hiddens, units_c = zip(part_one, part_two, part_three)
    layer_out = output(
        context_count, units_c, hiddens, out_own, out_give, hidden_q, norms, w_up, w_down
    )
    ends = (first_bits[0], second_bits[0])
    held = put(me, ends, False, False, factor, (first_value, second_value), None)
    held = put(me, ends, False, True, factor, (first_near, second_near), held)
    first_far, second_far, twos_got, held, layer_out = tie(
        (first_far, second_far, twos.terms[1], held, layer_out)
    )
    twos.terms[1] = twos_got

    first_got = swap(first_far, 1)
    second_got = swap(second_far, 1)
    twos = hand_over(twos)
    down_share = loss_factor * jnp.concatenate([ones[0], twos[0], twos[2]], axis=1)
    up_share = loss_factor * jnp.concatenate([ones[1], twos[1], twos[3]], axis=1).T
    held = put(me, ends, True, False, factor, (first_far, second_far), held)
    grad_qkv, grad_out = put(me, ends, True, True, factor, (first_got, second_got), held)
    return (
        layer_out,
        grad_inputs,
        small[0],
        small[1],
        grad_qkv,
        grad_out,
        small[2],
        small[3],
        up_share,
        down_share,
    )


def solution(mesh):
    placed = (
        P("rows", None),
        P("rows"),
        P("rows"),
        P("rows"),
        P(),
        P(),
        P(),
        P(),
        P(),
        P(),
        P(),
        P(),
        P("rows", None),
    )
    return jax.shard_map(
        partial(local, mesh.shape["rows"]),
        mesh=mesh,
        in_specs=placed,
        out_specs=(
            P("rows", None),
            P("rows", None),
            P(),
            P(),
            P(),
            P(),
            P(),
            P(),
            P(None, "rows"),
            P("rows", None),
        ),
        check_vma=False,
    )
```

```python
from functools import partial
import math

import jax
import jax.numpy as jnp
from jax import lax
from jax.experimental import pallas as pl
from jax.experimental.pallas import tpu as pltpu
from jax.sharding import PartitionSpec as P

HEADS = 12
HEAD = 64
WINDOW = 256
SHARE = 64
PIECE = 256
STRIP = 768
OUTPUT_TILE = 1024
FIRST_PART = 256

epsilon = 1e-05
score_factor = 1.0 / math.sqrt(HEAD)
masked_score = -3e38
root_half = math.sqrt(0.5)
root_two_pi = math.sqrt(2.0 / math.pi) * 0.5


def dot(left, right, left_dim=1, right_dim=0):
    return lax.dot_general(
        left, right, (((left_dim,), (right_dim,)), ((), ())), preferred_element_type=jnp.float32
    )


def cost(flops, transcendentals, bytes_accessed):
    return pl.CostEstimate(
        flops=flops // SHARE,
        transcendentals=transcendentals // SHARE,
        bytes_accessed=bytes_accessed // SHARE,
    )


def lane_masks(width):
    lanes = lax.broadcasted_iota(jnp.int32, (1, width), 1)
    return (lanes < HEAD, lanes >= HEAD)


def both_heads(rows):
    none = jnp.zeros_like(rows)
    return jnp.concatenate([jnp.where(lanes, rows, none) for lanes in lane_masks(2 * HEAD)], axis=0)


def one_head(rows):
    size = rows.shape[0] // 2
    return jnp.where(lane_masks(2 * HEAD)[0], rows[:size], rows[size:])


def columns(values):
    rows = values[0].shape[0]
    lanes = lax.broadcasted_iota(jnp.int32, (rows, 2 * HEAD), 1)
    block = jnp.zeros((rows, 2 * HEAD), jnp.float32)
    for lane, value in enumerate(values):
        block = jnp.where(lanes == lane, value, block)
    return block.astype(jnp.bfloat16)


def ones_block(rows):
    return jnp.ones((rows, 2 * HEAD), jnp.bfloat16)


def norm_rows(values):
    centre = jnp.mean(values, axis=-1, keepdims=True)
    centred = values - centre
    inverse = lax.rsqrt(jnp.mean(centred * centred, axis=-1, keepdims=True) + epsilon)
    return (centred * inverse, inverse)


def norm_rows_back(grad_norm, unit_rows, inverse, gain):
    grad_unit = grad_norm * gain
    grad_mean = jnp.mean(grad_unit, axis=-1, keepdims=True)
    grad_proj = jnp.mean(grad_unit * unit_rows, axis=-1, keepdims=True)
    return inverse * (grad_unit - grad_mean - unit_rows * grad_proj)


def column_sums(grad_norm, unit_rows):
    return jnp.concatenate(
        [
            jnp.sum(grad_norm * unit_rows, axis=0, keepdims=True),
            jnp.sum(grad_norm, axis=0, keepdims=True),
        ],
        axis=0,
    )


def shift_rows(count):
    taken = lax.broadcasted_iota(jnp.int32, (WINDOW, WINDOW + 16), 1)
    given = lax.broadcasted_iota(jnp.int32, (WINDOW, WINDOW + 16), 0) + count
    return jnp.where(taken == given, 1.0, 0.0).astype(jnp.bfloat16)


def project_kernel(
    context_ref,
    queries_ref,
    rows_ref,
    mask_ref,
    cotangent_ref,
    norms_ref,
    weight_ref,
    rolled_ref,
    norm_ref,
    query_ref,
    packed_ref,
    live_ref,
    dead_ref,
    upstream_ref,
    twice,
    present,
):
    step = pl.program_id(0)
    slots, width = rows_ref.shape

    @pl.when(step == 0)
    def _():
        context, queries = context_ref[0], queries_ref[0]
        start = pl.multiple_of(context // 16 * 16, 16)
        shifted = shift_rows(context - start)
        for half in (slice(0, slots), slice(slots, 2 * slots)):
            twice[half] = rows_ref[...]
        across = lax.broadcasted_iota(jnp.int32, (128, 128), 1)
        down = lax.broadcasted_iota(jnp.int32, (128, 128), 0)
        for group in range(slots // 128):
            kept = (across == down) & (mask_ref[group : group + 1] == 1)
            if group == 0:
                kept = kept | ((across == 0) & (down == 0))
            kept = jnp.where(kept, 1.0, 0.0).astype(jnp.bfloat16)
            marks = dot(kept, jnp.ones((128, 128), jnp.bfloat16)).astype(jnp.bfloat16)
            for first in (0, slots):
                present[first + group * 128 : first + (group + 1) * 128] = marks
        for first in range(0, slots, WINDOW):
            rows = dot(shifted, twice[pl.ds(start + first, WINDOW + 16), :])
            rolled_ref[first : first + WINDOW] = rows.astype(jnp.bfloat16)
            unit_rows = norm_rows(rows)[0]
            norm_ref[first : first + WINDOW] = (
                unit_rows * norms_ref[0:1] + norms_ref[1:2]
            ).astype(jnp.bfloat16)
            here = dot(shifted, present[pl.ds(start + first, WINDOW + 16), :])
            place = lax.broadcasted_iota(jnp.int32, here.shape, 0) + (first + context)
            place = jnp.where(place >= slots, place - slots, place)
            live_ref[first : first + WINDOW] = jnp.where(place < context + queries, here, 0.0)[:, 0:1]
            lanes = lax.broadcasted_iota(jnp.int32, here.shape, 1)
            if first > 0:
                known = (here > 0) & (place < context)
                split = lanes & (HEAD - 1)
                ones = jnp.where((split >= 1) & (split <= 3), 1.0, 0.0)
                dead = jnp.where((lanes == 0) & jnp.logical_not(known), masked_score, ones)
                dead_ref[first - WINDOW : first] = dead.astype(jnp.bfloat16)
            else:
                asked = jnp.where(place < context + queries, here, 0.0)[:, 0:1]
        twice[:slots] = cotangent_ref[...]
        near = jnp.minimum(start, slots - WINDOW - 16)
        near = pl.multiple_of(near, 16)
        upstream_ref[...] = dot(shift_rows(context - near), twice[pl.ds(near, WINDOW + 16), :]) * asked
        query_ref[...] = dot(norm_ref[:WINDOW], weight_ref[...]).astype(jnp.bfloat16)

    @pl.when(step > 0)
    def _():
        packed_ref[...] = dot(norm_ref[WINDOW:], weight_ref[...]).astype(jnp.bfloat16)


def project(context, queries, inputs, row_mask, cotangent, norms, w_qkv):
    slots, width = inputs.shape

    def fixed(shape):
        return pl.BlockSpec(shape, lambda j, at, more: (0, 0))

    whole = fixed((slots, width))
    outs = (
        ((slots, width), jnp.bfloat16),
        ((slots, width), jnp.bfloat16),
        ((WINDOW, width), jnp.bfloat16),
        ((slots - WINDOW, 2 * width), jnp.bfloat16),
        ((slots, 1), jnp.float32),
        ((slots - WINDOW, 128), jnp.bfloat16),
        ((WINDOW, width), jnp.float32),
    )
    specs = [fixed(shape) for shape, _ in outs]
    specs[3] = pl.BlockSpec((slots - WINDOW, width), lambda j, at, more: (0, jnp.maximum(j - 1, 0)))
    return pl.pallas_call(
        project_kernel,
        grid_spec=pltpu.PrefetchScalarGridSpec(
            num_scalar_prefetch=2,
            grid=(3,),
            in_specs=[
                whole,
                fixed((slots // 128, 128)),
                whole,
                fixed(norms.shape),
                pl.BlockSpec((width, width), lambda j, at, more: (0, j)),
            ],
            out_specs=specs,
            scratch_shapes=[
                pltpu.VMEM((2 * slots, width), jnp.bfloat16),
                pltpu.VMEM((2 * slots, 128), jnp.bfloat16),
            ],
        ),
        out_shape=[jax.ShapeDtypeStruct(shape, dtype) for shape, dtype in outs],
        cost_estimate=cost(
            flops=2 * slots * width * 2 * width,
            transcendentals=slots,
            bytes_accessed=14 * slots * width,
        ),
    )(context, queries, inputs, row_mask.reshape(slots // 128, 128), cotangent, norms, w_qkv)


def attend_kernel(
    keep_logs, query_ref, key_ref, value_ref, dead_ref, row_ref, rows_ref, wout_ref, *outs
):
    attended_ref, hidden_ref, unit_ref, inverse_ref = outs[:4]
    log_ref, attended = outs[-2:]
    step = pl.program_id(1)
    block = query_ref.shape[0]
    first_lane = columns([jnp.ones((2 * block, 1), jnp.float32)])
    queries = both_heads(query_ref[...] * jnp.bfloat16(score_factor))
    queries = jnp.concatenate([queries, first_lane], axis=1)
    keys = jnp.concatenate([key_ref[...], dead_ref[...]], axis=1)
    values = jnp.concatenate([value_ref[...], ones_block(key_ref.shape[0])], axis=1)
    scores = [dot(queries[k : k + PIECE], keys, 1, 1) for k in range(0, 2 * block, PIECE)]
    exponents = [
        jnp.exp(part - jnp.max(part, axis=-1, keepdims=True)).astype(jnp.bfloat16) for part in scores
    ]
    parts, totals = [], []
    for exponent in exponents:
        summed = dot(exponent, values)
        totals.append(summed[:, 2 * HEAD :])
        parts.append(summed[:, : 2 * HEAD] / summed[:, 2 * HEAD :])
    if keep_logs:
        logs = [
            jnp.max(part, axis=-1, keepdims=True) + jnp.log(total) for part, total in zip(scores, totals)
        ]
        log_ref[...] = one_head(jnp.concatenate(logs, axis=0))
    both = one_head(jnp.concatenate(parts, axis=0))
    both = jnp.where(row_ref[...] > 0, both, 0.0).astype(jnp.bfloat16)
    attended_ref[...] = both
    attended[:, pl.ds(pl.multiple_of(step * 2 * HEAD, 2 * HEAD), 2 * HEAD)] = both

    @pl.when(step == pl.num_programs(1) - 1)
    def _():
        hidden = rows_ref[...].astype(jnp.float32) + dot(attended[...], wout_ref[...])
        hidden_ref[...] = hidden
        unit_ref[...], inverse_ref[...] = norm_rows(hidden)


def attend(query_rows, packed_keys, key_dead, row_live, rows, w_out, from_query, from_row, keep_logs):
    slots, block, width = WINDOW, WINDOW, query_rows.shape[1]
    keys_len = packed_keys.shape[0]
    pairs = width // (2 * HEAD)
    whole = pl.BlockSpec((block, width), lambda r, p: (r, 0))
    return pl.pallas_call(
        partial(attend_kernel, keep_logs),
        grid=(slots // block, pairs),
        in_specs=[
            pl.BlockSpec((block, 2 * HEAD), lambda r, p: (from_query, p)),
            pl.BlockSpec((keys_len, 2 * HEAD), lambda r, p: (0, p)),
            pl.BlockSpec((keys_len, 2 * HEAD), lambda r, p: (0, pairs + p)),
            pl.BlockSpec((keys_len, 2 * HEAD), lambda r, p: (0, 0)),
            pl.BlockSpec((block, 1), lambda r, p: (from_row, 0)),
            pl.BlockSpec((block, width), lambda r, p: (from_row, 0)),
            pl.BlockSpec((width, width), lambda r, p: (0, 0)),
        ],
        out_specs=(
            pl.BlockSpec((block, 2 * HEAD), lambda r, p: (r, p)),
            whole,
            whole,
            pl.BlockSpec((block, 1), lambda r, p: (r, 0)),
            *([pl.BlockSpec((block, 2 * HEAD), lambda r, p: (r, p))] if keep_logs else ()),
        ),
        scratch_shapes=[pltpu.VMEM((block, width), jnp.bfloat16)],
        out_shape=(
            jax.ShapeDtypeStruct((slots, width), jnp.bfloat16),
            jax.ShapeDtypeStruct((slots, width), jnp.float32),
            jax.ShapeDtypeStruct((slots, width), jnp.float32),
            jax.ShapeDtypeStruct((slots, 1), jnp.float32),
            *([jax.ShapeDtypeStruct((slots, width), jnp.float32)] if keep_logs else ()),
        ),
        cost_estimate=cost(
            flops=4 * slots * keys_len * width * 4,
            transcendentals=slots * keys_len * HEADS,
            bytes_accessed=12 * slots * width + 4 * keys_len * width,
        ),
    )(query_rows, packed_keys, packed_keys, key_dead, row_live, rows, w_out)


def units_kernel(
    bits, at_ref, own_ref, got_ref, norms_ref, grad_ref, grad_got_ref, up_ref, down_ref, *outs
):
    keep_refs, act_ref, (own_grad, give_grad), (normed, upstream) = outs[:8], outs[8], outs[9:11], outs[11:]
    width = own_ref.shape[1]
    cut = FIRST_PART

    @pl.when(pl.program_id(0) == 0)
    def _():
        for first, part, grad in ((0, own_ref, grad_ref), (WINDOW, got_ref, grad_got_ref)):
            rows = part[...] * norms_ref[2:3] + norms_ref[3:4]
            normed[first : first + WINDOW] = rows.astype(jnp.bfloat16)
            upstream[first : first + WINDOW] = grad[...].astype(jnp.bfloat16)

    tile = up_ref.shape[1]
    acts, pres = [], []
    for first in range(0, tile, STRIP):
        strip = slice(first, first + STRIP)
        pre_act = dot(normed[...], up_ref[:, strip])
        share = gelu_parts(pre_act)
        acts.append((pre_act * share).astype(jnp.bfloat16))
        slope = share + pre_act * (root_two_pi * jnp.exp(-0.5 * pre_act * pre_act))
        pres.append((dot(upstream[...], down_ref[strip], 1, 1) * slope).astype(jnp.bfloat16))
    act_ref[...] = jnp.concatenate(acts, axis=1)
    grad_pre = jnp.concatenate(pres, axis=1)
    part = dot(grad_pre, up_ref[...], 1, 1)

    @pl.when(pl.program_id(0) == 0)
    def _():
        own_grad[...], give_grad[...] = part[:WINDOW], part[WINDOW:]

    @pl.when(pl.program_id(0) > 0)
    def _():
        own_grad[...] += part[:WINDOW]
        give_grad[...] += part[WINDOW:]

    for index, (lefts, right) in enumerate(((acts, upstream), (pres, normed))):
        product = jnp.concatenate([dot(left, right[...], 0, 0) for left in lefts], axis=0)
        mine = (at_ref[0] & bits[index]) != 0
        rows = keep_refs[4 * index].shape[1]
        product = product.reshape(-1, 2, rows, width)
        keep = jnp.where(mine, product[:, 1], product[:, 0])
        give = jnp.where(mine, product[:, 0], product[:, 1])
        for place, (low, high) in enumerate(((0, cut), (cut, width))):
            keep_refs[4 * index + 2 * place][...] = keep[:, :, low:high]
            keep_refs[4 * index + 2 * place + 1][...] = give[:, :, low:high]


def units(me, bits, rows, unit_own, unit_got, norms, upstream, upstream_got, w_up, w_down):
    width, hidden = w_up.shape
    half = hidden // 2
    tile = 8 * rows if 8 * rows >= 384 else 384
    tiles = half // tile
    whole = pl.BlockSpec((WINDOW, width), lambda j, at: (0, 0))
    pieces, shapes = [], []
    for index in range(2):
        size = 2 * rows * (index + 1)
        for span in (FIRST_PART, FIRST_PART, width - FIRST_PART, width - FIRST_PART):
            pieces.append(pl.BlockSpec((tile // (2 * size), size, span), lambda j, at: (j, 0, 0)))
            shapes.append(jax.ShapeDtypeStruct((half // (2 * size), size, span), jnp.float32))
    acts = pl.BlockSpec((2 * WINDOW, tile), lambda j, at: (0, j))
    return pl.pallas_call(
        partial(units_kernel, bits),
        grid_spec=pltpu.PrefetchScalarGridSpec(
            num_scalar_prefetch=1,
            grid=(tiles,),
            in_specs=[
                whole,
                whole,
                pl.BlockSpec(norms.shape, lambda j, at: (0, 0)),
                whole,
                whole,
                pl.BlockSpec((width, tile), lambda j, at: (0, (at[0] & 1) * tiles + j)),
                pl.BlockSpec((tile, width), lambda j, at: ((at[0] & 1) * tiles + j, 0)),
            ],
            out_specs=(*pieces, acts, whole, whole),
            scratch_shapes=[
                pltpu.VMEM((2 * WINDOW, width), jnp.bfloat16),
                pltpu.VMEM((2 * WINDOW, width), jnp.bfloat16),
            ],
        ),
        out_shape=(
            *shapes,
            jax.ShapeDtypeStruct((2 * WINDOW, half), jnp.bfloat16),
            jax.ShapeDtypeStruct((WINDOW, width), jnp.float32),
            jax.ShapeDtypeStruct((WINDOW, width), jnp.float32),
        ),
        cost_estimate=cost(
            flops=16 * WINDOW * width * half,
            transcendentals=4 * WINDOW * half,
            bytes_accessed=12 * width * half,
        ),
    )(
        me.reshape(1),
        unit_own,
        unit_got,
        norms,
        upstream,
        upstream_got,
        w_up,
        w_down,
    )


def halves_kernel(right_dim, at_ref, left_ref, right_ref, own_ref, give_ref):
    product = dot(left_ref[...], right_ref[...], 1, right_dim)
    own_ref[...], give_ref[...] = product[:WINDOW], product[WINDOW:]


def halves(me, left, right, right_dim):
    rows, half = left.shape
    width = right.shape[1 - right_dim]
    tile = 256
    if right_dim == 1:
        spec = pl.BlockSpec((tile, half), lambda j, at: (j, at[0] & 1))
    else:
        spec = pl.BlockSpec((half, tile), lambda j, at: (at[0] & 1, j))
    out = pl.BlockSpec((WINDOW, tile), lambda j, at: (0, j))
    return pl.pallas_call(
        partial(halves_kernel, right_dim),
        grid_spec=pltpu.PrefetchScalarGridSpec(
            num_scalar_prefetch=1,
            grid=(width // tile,),
            in_specs=[pl.BlockSpec((rows, half), lambda j, at: (0, 0)), spec],
            out_specs=(out, out),
        ),
        out_shape=(jax.ShapeDtypeStruct((WINDOW, width), jnp.float32),) * 2,
        cost_estimate=cost(
            flops=2 * rows * width * half, transcendentals=0, bytes_accessed=4 * width * half
        ),
    )(me.reshape(1), left, right)


def attend_back_kernel(
    query_ref,
    key_ref,
    value_ref,
    dead_ref,
    row_ref,
    attended_ref,
    log_ref,
    own_ref,
    got_ref,
    unit_ref,
    inverse_ref,
    norms_ref,
    upstream_ref,
    wout_ref,
    dq_ref,
    dk_ref,
    dv_ref,
    grad_hidden_ref,
    low_ref,
    sums_ref,
):
    @pl.when(pl.program_id(0) == 0)
    def _():
        grad_norm = own_ref[...] + got_ref[...]
        unit_rows = unit_ref[...]
        sums_ref[...] = column_sums(grad_norm, unit_rows)
        grad_rows = norm_rows_back(grad_norm, unit_rows, inverse_ref[...], norms_ref[2:3])
        grad_hidden = upstream_ref[...] + grad_rows
        grad_hidden_ref[...] = grad_hidden
        low_ref[...] = grad_hidden.astype(jnp.bfloat16)

    block = query_ref.shape[0]
    key_rows = key_ref[...]
    grad = dot(low_ref[...], wout_ref[...], 1, 1)
    grad = jnp.where(row_ref[...] > 0, grad, 0.0).astype(jnp.bfloat16)
    product = grad.astype(jnp.float32) * attended_ref[...].astype(jnp.float32)
    grads = both_heads(grad)
    grads_wide = jnp.concatenate([grads, both_heads((-product).astype(jnp.bfloat16))], axis=1)
    values_wide = jnp.concatenate([value_ref[...], ones_block(key_rows.shape[0])], axis=1)
    lanes = lax.broadcasted_iota(jnp.int32, (block, 2 * HEAD), 1)
    rest = -log_ref[...]
    extra = jnp.zeros((block, 2 * HEAD), jnp.float32)
    for lane in range(1, 4):
        part = rest.astype(jnp.bfloat16).astype(jnp.float32)
        rest = rest - part
        extra = jnp.where((lanes & (HEAD - 1)) == lane, part, extra)
    extra = both_heads(extra)
    wide_lanes = lax.broadcasted_iota(jnp.int32, (2 * block, 2 * HEAD), 1)
    extra = jnp.where(wide_lanes == 0, 1.0, extra).astype(jnp.bfloat16)
    queries = both_heads(query_ref[...] * jnp.bfloat16(score_factor))
    queries_wide = jnp.concatenate([queries, extra], axis=1)
    keys_wide = jnp.concatenate([key_rows, dead_ref[...]], axis=1)
    pieces = [slice(k, k + PIECE) for k in range(0, 2 * block, PIECE)]
    probs = [jnp.exp(dot(queries_wide[piece], keys_wide, 1, 1)) for piece in pieces]
    grad_scores = [
        (prob * dot(grads_wide[piece], values_wide, 1, 1)).astype(jnp.bfloat16)
        for prob, piece in zip(probs, pieces)
    ]
    probs = jnp.concatenate([prob.astype(jnp.bfloat16) for prob in probs], axis=0)
    grad_scores = jnp.concatenate(grad_scores, axis=0)
    dq_ref[...] = (one_head(dot(grad_scores, key_rows)) * score_factor).astype(jnp.bfloat16)
    dk_ref[...] = dot(grad_scores, queries, 0, 0).astype(jnp.bfloat16)
    dv_ref[...] = dot(probs, grads, 0, 0).astype(jnp.bfloat16)


def attend_back(
    query_rows, packed_keys, key_dead, row_live, attended, logs, own, got, unit, inverse, norms, upstream, w_out
):
    slots, width = query_rows.shape
    keys_len = packed_keys.shape[0]
    pairs = width // (2 * HEAD)
    rows_spec = pl.BlockSpec((slots, 2 * HEAD), lambda p: (0, p))
    keys_spec = pl.BlockSpec((keys_len, 2 * HEAD), lambda p: (0, p))
    whole = pl.BlockSpec((slots, width), lambda p: (0, 0))
    column = pl.BlockSpec((slots, 1), lambda p: (0, 0))
    return pl.pallas_call(
        attend_back_kernel,
        grid=(pairs,),
        in_specs=[
            rows_spec,
            keys_spec,
            pl.BlockSpec((keys_len, 2 * HEAD), lambda p: (0, pairs + p)),
            pl.BlockSpec((keys_len, 2 * HEAD), lambda p: (0, 0)),
            column,
            rows_spec,
            rows_spec,
            whole,
            whole,
            whole,
            column,
            pl.BlockSpec(norms.shape, lambda p: (0, 0)),
            whole,
            pl.BlockSpec((2 * HEAD, width), lambda p: (p, 0)),
        ],
        out_specs=(
            rows_spec,
            keys_spec,
            keys_spec,
            whole,
            whole,
            pl.BlockSpec((2, width), lambda p: (0, 0)),
        ),
        out_shape=(
            jax.ShapeDtypeStruct((slots, width), jnp.bfloat16),
            jax.ShapeDtypeStruct((keys_len, width), jnp.bfloat16),
            jax.ShapeDtypeStruct((keys_len, width), jnp.bfloat16),
            jax.ShapeDtypeStruct((slots, width), jnp.float32),
            jax.ShapeDtypeStruct((slots, width), jnp.bfloat16),
            jax.ShapeDtypeStruct((2, width), jnp.float32),
        ),
        cost_estimate=cost(
            flops=10 * slots * keys_len * width * 4,
            transcendentals=slots * keys_len * HEADS,
            bytes_accessed=6 * slots * width + 8 * keys_len * width,
        ),
    )(
        query_rows,
        packed_keys,
        packed_keys,
        key_dead,
        row_live,
        attended,
        logs,
        own,
        got,
        unit,
        inverse,
        norms,
        upstream,
        w_out,
    )


def weights_kernel(
    at_ref, norm_ref, attended_ref, dq_ref, dk_ref, dv_ref, low_ref, keep_a, keep_b, give_a, give_b
):
    for odd, (even_a, even_b, odd_a, odd_b) in (
        (0, (keep_a, keep_b, give_a, give_b)),
        (1, (give_a, give_b, keep_a, keep_b)),
    ):

        @pl.when((at_ref[0] & 1) == odd)
        def _(even_a=even_a, even_b=even_b, odd_a=odd_a, odd_b=odd_b):
            even_a[...] = dot(norm_ref[:WINDOW], dq_ref[...], 0, 0)
            odd_a[...] = dot(norm_ref[WINDOW:], dk_ref[...], 0, 0)
            odd_b[...] = dot(norm_ref[WINDOW:], dv_ref[...], 0, 0)
            even_b[...] = dot(attended_ref[...], low_ref[...], 0, 0)


def weights(me, normed, attended, dq, dk, dv, low):
    slots, width = normed.shape
    tile = 256

    def full(value):
        return pl.BlockSpec(value.shape, lambda j, at: (0, 0))

    out = pl.BlockSpec((tile, width), lambda j, at: (j, 0))
    return pl.pallas_call(
        weights_kernel,
        grid_spec=pltpu.PrefetchScalarGridSpec(
            num_scalar_prefetch=1,
            grid=(width // tile,),
            in_specs=[
                pl.BlockSpec((slots, tile), lambda j, at: (0, j)),
                pl.BlockSpec((WINDOW, tile), lambda j, at: (0, j)),
                full(dq),
                full(dk),
                full(dv),
                full(low),
            ],
            out_specs=(out,) * 4,
        ),
        out_shape=(jax.ShapeDtypeStruct((width, width), jnp.float32),) * 4,
        cost_estimate=cost(
            flops=4 * slots * width * width, transcendentals=0, bytes_accessed=20 * width * width
        ),
    )(me.reshape(1), normed, attended, dq, dk, dv, low)


def rows_back_kernel(dq_ref, dk_ref, dv_ref, rows_ref, hidden_ref, norms_ref, wq, wk, wv, out_ref, sums_ref):
    step = pl.program_id(0)
    unit_rows, inverse = norm_rows(rows_ref[...].astype(jnp.float32))

    def finish(grad_norm):
        sums = column_sums(grad_norm, unit_rows)
        return (norm_rows_back(grad_norm, unit_rows, inverse, norms_ref[0:1]), sums)

    @pl.when(step == 0)
    def _():
        grad_rows, sums = finish(dot(dq_ref[...], wq[...], 1, 1))
        out_ref[...] = grad_rows + hidden_ref[...]
        sums_ref[...] = sums

    @pl.when(step > 0)
    def _():
        grad_rows, sums = finish(dot(dk_ref[...], wk[...], 1, 1) + dot(dv_ref[...], wv[...], 1, 1))
        out_ref[...] = grad_rows
        sums_ref[...] += sums


def rows_back(dq, dk, dv, rows, grad_hidden, norms, w_qkv):
    slots, width = rows.shape
    fixed = pl.BlockSpec((WINDOW, width), lambda r: (0, 0))
    keys = pl.BlockSpec((WINDOW, width), lambda r: (jnp.maximum(r - 1, 0), 0))
    tile = pl.BlockSpec((WINDOW, width), lambda r: (r, 0))
    return pl.pallas_call(
        rows_back_kernel,
        grid=(slots // WINDOW,),
        in_specs=[
            fixed,
            keys,
            keys,
            tile,
            fixed,
            pl.BlockSpec(norms.shape, lambda r: (0, 0)),
            pl.BlockSpec((width, width), lambda r: (0, 0)),
            pl.BlockSpec((width, width), lambda r: (0, 1)),
            pl.BlockSpec((width, width), lambda r: (0, 2)),
        ],
        out_specs=(tile, pl.BlockSpec((2, width), lambda r: (0, 0))),
        out_shape=(
            jax.ShapeDtypeStruct((slots, width), jnp.float32),
            jax.ShapeDtypeStruct((2, width), jnp.float32),
        ),
        cost_estimate=cost(
            flops=4 * slots * width * width, transcendentals=slots, bytes_accessed=12 * slots * width
        ),
    )(dq, dk, dv, rows, grad_hidden, norms, w_qkv, w_qkv, w_qkv)


def place_kernel(bits, far, got, me_ref, factor_ref, a_ref, b_ref, *refs):
    qkv_ref, out_ref, a_wide, b_wide, semaphores = refs[-5:]
    size, width = a_ref.shape
    me = me_ref[0]
    a_wide[...] = a_ref[...] * factor_ref[0, 0]
    b_wide[...] = b_ref[...] * factor_ref[0, 0]
    odd = (me & 1) != 0
    rows = []
    for bit in bits:
        high = (me & bit) != 0
        rows.append(jnp.where(high, 0 if far else size, size if far else 0))
    rows_a, rows_b = (pl.ds(pl.multiple_of(row, size), size) for row in rows)

    def place(targets):
        copies = [
            pltpu.make_async_copy(source, target, semaphores.at[index])
            for index, (source, target) in enumerate(zip((a_wide, b_wide), targets))
        ]
        for copy in copies:
            copy.start()
        for copy in copies:
            copy.wait()

    @pl.when(odd == got)
    def _():
        place((qkv_ref.at[rows_a, pl.ds(0, width)], out_ref.at[rows_b]))

    @pl.when(odd != got)
    def _():
        place((qkv_ref.at[rows_a, pl.ds(width, width)], qkv_ref.at[rows_b, pl.ds(2 * width, width)]))


def put(me, bits, far, got, factor, pieces, held):
    size, width = pieces[0].shape
    scalar = pl.BlockSpec(memory_space=pltpu.SMEM)
    anywhere = pl.BlockSpec(memory_space=pl.ANY)
    vmem = pl.BlockSpec(memory_space=pltpu.VMEM)
    operands = [*pieces, *(held or ())]
    return pl.pallas_call(
        partial(place_kernel, bits, far, got),
        in_specs=[scalar, scalar, vmem, vmem] + [anywhere] * (2 if held else 0),
        out_specs=(anywhere, anywhere),
        out_shape=(
            jax.ShapeDtypeStruct((2 * size, 3 * width), jnp.float32),
            jax.ShapeDtypeStruct((2 * size, width), jnp.float32),
        ),
        scratch_shapes=[
            pltpu.VMEM((size, width), jnp.float32),
            pltpu.VMEM((size, width), jnp.float32),
            pltpu.SemaphoreType.DMA((2,)),
        ],
        input_output_aliases={4: 0, 5: 1} if held else {},
        cost_estimate=cost(flops=0, transcendentals=0, bytes_accessed=8 * width * width),
    )(me.reshape(1), factor, *operands)


def output_kernel(
    at_ref, *refs
):
    units, hiddens, (own_ref, got_ref, base_ref, norms_ref, up_ref, down_ref) = refs[:3], refs[3:6], refs[6:12]
    out_ref, normed, total, twice = refs[12:]
    step = pl.program_id(0)
    slots, width = out_ref.shape

    @pl.when(step == 0)
    def _():
        for index in range(3):
            rows = slice(index * WINDOW, (index + 1) * WINDOW)
            normed[rows] = (units[index][...] * norms_ref[2:3] + norms_ref[3:4]).astype(jnp.bfloat16)
            total[rows] = hiddens[index][...]

    acts = []
    for first in range(0, up_ref.shape[1], 512):
        pre_act = dot(normed[...], up_ref[:, first : first + 512])
        acts.append((pre_act * gelu_parts(pre_act)).astype(jnp.bfloat16))
    total[...] += dot(jnp.concatenate(acts, axis=1), down_ref[...])

    @pl.when(step == pl.num_programs(0) - 1)
    def _():
        window = (base_ref[...] + (own_ref[...] + got_ref[...])).astype(jnp.bfloat16)
        rest = total[...].astype(jnp.bfloat16)
        for first in (0, slots):
            twice[first : first + WINDOW] = window
            twice[first + WINDOW : first + slots] = rest
        begin = slots - at_ref[0]
        start = pl.multiple_of(begin // 16 * 16, 16)
        shifted = shift_rows(begin - start)
        for first in range(0, slots, WINDOW):
            rows = dot(shifted, twice[pl.ds(start + first, WINDOW + 16), :])
            out_ref[first : first + WINDOW] = rows.astype(jnp.bfloat16)


def output(context, units, hiddens, own, got, base, norms, w_up, w_down):
    width, hidden = w_up.shape
    slots = 4 * WINDOW
    tile = OUTPUT_TILE
    part = pl.BlockSpec((WINDOW, width), lambda j, at: (0, 0))
    return pl.pallas_call(
        output_kernel,
        grid_spec=pltpu.PrefetchScalarGridSpec(
            num_scalar_prefetch=1,
            grid=(hidden // tile,),
            in_specs=[part] * 9
            + [
                pl.BlockSpec(norms.shape, lambda j, at: (0, 0)),
                pl.BlockSpec((width, tile), lambda j, at: (0, j)),
                pl.BlockSpec((tile, width), lambda j, at: (j, 0)),
            ],
            out_specs=pl.BlockSpec((slots, width), lambda j, at: (0, 0)),
            scratch_shapes=[
                pltpu.VMEM((slots - WINDOW, width), jnp.bfloat16),
                pltpu.VMEM((slots - WINDOW, width), jnp.float32),
                pltpu.VMEM((2 * slots + 16, width), jnp.bfloat16),
            ],
        ),
        out_shape=jax.ShapeDtypeStruct((slots, width), jnp.bfloat16),
        cost_estimate=pl.CostEstimate(
            flops=12 * WINDOW * width * hidden,
            transcendentals=3 * WINDOW * hidden,
            bytes_accessed=8 * width * hidden,
        ),
    )(context, *units, *hiddens, own, got, base, norms, w_up, w_down)


def gelu_parts(values):
    share = 0.5 * (1.0 + lax.erf(values * root_half))
    return share


def local(
    devices,
    inputs,
    context_count,
    query_count,
    row_mask,
    ln1_gain,
    ln1_bias,
    w_qkv,
    w_out,
    ln2_gain,
    ln2_bias,
    w_up,
    w_down,
    cotangent,
):
    slots, width = inputs.shape
    hidden = w_up.shape[1]
    half = hidden // 2
    me = lax.axis_index("rows")
    core = me & 1

    def bit_of(bit):
        return ((me & bit) != 0).astype(jnp.int32)

    def swap(value, bit):
        return lax.ppermute(value, "rows", [(i, i ^ bit) for i in range(devices)])

    def pick(value, axis, index):
        return lax.dynamic_index_in_dim(value, index, axis, keepdims=False)

    bits = []
    bit = 2
    while bit < devices:
        bits.append(bit)
        bit *= 2
    top = bits[-1]

    def order_of(list_of_bits, flip):
        if flip and len(list_of_bits) > 1:
            return [list_of_bits[1], list_of_bits[0]] + list_of_bits[2:]
        return list_of_bits

    context = context_count[0]
    queries = query_count[0]
    norms = jnp.concatenate([ln1_gain, ln1_bias, ln2_gain, ln2_bias]).reshape(4, width)
    tie = lax.optimization_barrier
    rows, normed_low, query_window, packed_keys, row_column, key_dead, upstream = project(
        context_count, query_count, inputs, row_mask, cotangent, norms, w_qkv
    )
    upstream_got = swap(upstream, 1)
    attended_q, hidden_q, unit_two, inverse_two, log_sums = attend(
        query_window, packed_keys, key_dead, row_column, rows, w_out, 0, 0, True
    )
    ff_rows = half // (devices // 2)
    ff_bits = bits[:-1]
    pieces = units(
        me,
        bits[:2],
        ff_rows,
        unit_two,
        swap(unit_two, 1),
        norms,
        upstream,
        upstream_got,
        w_up,
        w_down,
    )
    activated, grad_own, grad_give = pieces[8:]
    pieces = pieces[:8]
    first_bits, second_bits = order_of(bits, False), order_of(bits, True)

    class Halving:
        def __init__(self, terms, axes):
            self.terms, self.axes = terms, list(axes)

        def split(self, bit):
            axis = self.axes.index(bit)
            mine = bit_of(bit)
            self.axes.remove(bit)
            self.kept = sum(pick(term, axis, mine) for term in self.terms)
            self.sent = sum(pick(term, axis, 1 - mine) for term in self.terms)

        def go(self, bit):
            self.terms = [self.kept, swap(self.sent, bit)]

        def send(self, bit):
            self.split(bit)
            self.go(bit)

    def got_of(chains):
        return tuple(chain.terms[1] for chain in chains)

    def set_got(chains, values):
        for chain, value in zip(chains, values):
            chain.terms[1] = value

    def feed_forward(index, place):
        keep, give = pieces[4 * index + 2 * place : 4 * index + 2 * place + 2]
        axes = ff_bits[::-1] + [1]
        axes.remove(ff_order[index][0])
        shape = [2] * len(axes) + [ff_rows, keep.shape[-1]]
        got = swap(give, ff_order[index][0])
        return Halving([keep.reshape(shape), got.reshape(shape)], axes)

    def to_top(chain):
        pairs = [(i, i ^ top) for i in range(devices) if ((i & top) != 0) != ((i & 1) != 0)]
        value = chain.terms[0] + chain.terms[1]
        chain.terms = [value, lax.ppermute(value, "rows", pairs)]

    def hand_over(chain):
        mine = sum(pick(term, 1, core) for term in chain.terms)
        other = swap(sum(pick(term, 1, 1 - core) for term in chain.terms), 1)
        return jnp.where(bit_of(top) == core, mine, other)

    ff_order = (order_of(ff_bits, False), order_of(ff_bits, True))

    down_one = feed_forward(0, 0)
    up_one = feed_forward(1, 0)
    ones = (down_one, up_one)

    grad_query, grad_key, grad_value, grad_hidden, grad_low, sums_two = attend_back(
        query_window,
        packed_keys,
        key_dead,
        row_column,
        attended_q,
        log_sums,
        grad_own,
        swap(grad_give, 1),
        unit_two,
        inverse_two,
        norms,
        upstream,
        w_out,
    )
    keep_first, keep_second, *give = weights(
        me, normed_low, attended_q, grad_query, grad_key, grad_value, grad_low
    )

    def unroll(value):
        return lax.dynamic_slice(
            jnp.concatenate([value, value], axis=0), (slots - context, 0), (slots, width)
        )

    def joined(chains):
        terms = [jnp.stack([c.terms[k] for c in chains]) for k in range(2)]
        return Halving(terms, [None] + chains[0].axes)

    ones_got, give = tie((got_of(ones), give))
    set_got(ones, ones_got)
    for chain, order in zip(ones, ff_order):
        chain.send(order[1])
    give_first, give_second = swap(give[0], 1), swap(give[1], 1)
    shape = [2] * len(bits) + [width // (2 ** len(bits)), width]
    first = Halving([keep_first.reshape(shape), give_first.reshape(shape)], first_bits)
    second = Halving([keep_second.reshape(shape), give_second.reshape(shape)], second_bits)
    both = (first, second)

    first.split(first_bits[0])
    second.split(second_bits[0])
    first.sent, second.sent, grad_query, grad_key, grad_value, ones_got = tie(
        (first.sent, second.sent, grad_query, grad_key, grad_value, got_of(ones))
    )
    set_got(ones, ones_got)
    first.go(first_bits[0])
    second.go(second_bits[0])
    ones = joined(ones)
    for bit in ff_bits[2:]:
        ones.send(bit)
    to_top(ones)
    grad_query, _ = tie((grad_query, ones.terms[0]))
    grad_rows, sums_one = rows_back(
        grad_query, grad_key, grad_value, rows, grad_hidden, norms, w_qkv
    )
    context_norms, _ = tie((normed_low[WINDOW:], grad_rows))
    context_queries = dot(context_norms, w_qkv[:, :width]).astype(jnp.bfloat16)

    def context_part(index, queries):
        return attend(
            queries, packed_keys, key_dead, row_column, rows, w_out, index, index + 1, False
        )[1:3]

    out_own, out_give = halves(me, activated, w_down, 0)
    out_give = swap(out_give, 1)
    both_got, ones_got, context_queries, sums_one, out_own, out_give = tie(
        (got_of(both), ones.terms[1], context_queries, sums_one, out_own, out_give)
    )
    set_got(both, both_got)
    ones.terms[1] = ones_got

    first.split(first_bits[1])
    second.split(second_bits[1])
    first.sent, second.sent, ones.terms, sums_one, context_queries = tie(
        (first.sent, second.sent, ones.terms, sums_one, context_queries)
    )
    first.go(first_bits[1])
    second.go(second_bits[1])
    small = jnp.concatenate(
        [sums_one, sums_two, jnp.full((4, width), queries, jnp.float32)], axis=0
    )
    small = small + swap(small, 1)
    part_one = context_part(0, context_queries)
    both_got, small, context_queries, part_one, pieces = tie(
        (got_of(both), small, context_queries, part_one, pieces)
    )
    set_got(both, both_got)
    down_two = feed_forward(0, 1)
    up_two = feed_forward(1, 1)
    twos = (down_two, up_two)

    both = joined(both)
    for bit in bits[2:-1]:
        both.send(bit)
    for bit in bits[2:-1]:
        small = small + swap(small, bit)
    part_two = context_part(1, context_queries)
    both_got, small, part_two, context_queries = tie(
        (both.terms[1], small, part_two, context_queries)
    )
    both.terms[1] = both_got

    value = both.terms[0] + both.terms[1]
    value, context_queries = tie((value, context_queries))
    value_got = swap(value, top)
    part_three = context_part(2, context_queries)
    small, part_three, twos_got = tie((small, part_three, got_of(twos)))
    set_got(twos, twos_got)
    for bit in bits[:2]:
        small = small + swap(small, bit)
    span = (width - FIRST_PART) // 2
    early, late = (
        [
            Halving([term[..., first : first + span] for term in chain.terms], chain.axes)
            for chain in twos
        ]
        for first in (0, span)
    )
    for chain, order in zip(early, ff_order):
        chain.split(order[1])
    early[0].sent, early[1].sent, small = tie((early[0].sent, early[1].sent, small))
    for chain, order in zip(early, ff_order):
        chain.go(order[1])
    for chain, order in zip(late, ff_order):
        chain.split(order[1])
    sent = (late[0].sent, late[1].sent)
    _, early_got, value_got, small, part_two, part_three, ones.terms, grad_rows = tie(
        (sent, got_of(early), value_got, small, part_two, part_three, ones.terms, grad_rows)
    )
    set_got(early, early_got)
    value = value + value_got

    def widen(value, bit, axis):
        got = swap(value, bit)
        high = bit_of(bit) == 1
        return jnp.stack(
            [jnp.where(high, got, value), jnp.where(high, value, got)], axis=axis
        )

    for bit in bits[2:-1][::-1]:
        value = widen(value, bit, 1)
    for chain, order in zip(late, ff_order):
        chain.go(order[1])
    ones = hand_over(ones)
    small = small + swap(small, top)
    early = joined(early)
    for bit in ff_bits[2:3]:
        early.split(bit)
        early.sent, small = tie((early.sent, small))
        early.go(bit)
    value, small, ones, part_one, late_got = tie((value, small, ones, part_one, got_of(late)))
    set_got(late, late_got)
    late = joined(late)
    loss_factor = math.sqrt(devices) * (slots // 4) / small[4, 0]
    factor = loss_factor.reshape(1, 1)

    first_value = widen(value[0], first_bits[1], 0)
    second_value = widen(value[1], second_bits[1], 0)
    for bit in ff_bits[2:3]:
        late.send(bit)
    for bit in ff_bits[3:]:
        early.send(bit)
        late.send(bit)
    grad_inputs = unroll(grad_rows * loss_factor)
    small = small * loss_factor
    first_value, second_value, grad_inputs, small, part_one, early.terms, late.terms = tie(
        (first_value, second_value, grad_inputs, small, part_one, early.terms, late.terms)
    )
    terms = [jnp.concatenate(pair, axis=0) for pair in zip(early.terms, late.terms)]
    twos = Halving(terms, early.axes)

    first_value, second_value = first_value.reshape(-1, width), second_value.reshape(-1, width)
    first_far = swap(first_value, first_bits[0])
    second_far = swap(second_value, second_bits[0])
    first_near = swap(first_value, 1)
    second_near = swap(second_value, 1)
    to_top(twos)
    hiddens, units_c = zip(part_one, part_two, part_three)
    layer_out = output(
        context_count, units_c, hiddens, out_own, out_give, hidden_q, norms, w_up, w_down
    )
    ends = (first_bits[0], second_bits[0])
    held = put(me, ends, False, False, factor, (first_value, second_value), None)
    held = put(me, ends, False, True, factor, (first_near, second_near), held)
    first_far, second_far, twos_got, held, layer_out = tie(
        (first_far, second_far, twos.terms[1], held, layer_out)
    )
    twos.terms[1] = twos_got

    first_got = swap(first_far, 1)
    second_got = swap(second_far, 1)
    twos = hand_over(twos)
    down_share = loss_factor * jnp.concatenate([ones[0], twos[0], twos[2]], axis=1)
    up_share = loss_factor * jnp.concatenate([ones[1], twos[1], twos[3]], axis=1).T
    held = put(me, ends, True, False, factor, (first_far, second_far), held)
    grad_qkv, grad_out = put(me, ends, True, True, factor, (first_got, second_got), held)
    return (
        layer_out,
        grad_inputs,
        small[0],
        small[1],
        grad_qkv,
        grad_out,
        small[2],
        small[3],
        up_share,
        down_share,
    )


def solution(mesh):
    placed = (
        P("rows", None),
        P("rows"),
        P("rows"),
        P("rows"),
        P(),
        P(),
        P(),
        P(),
        P(),
        P(),
        P(),
        P(),
        P("rows", None),
    )
    return jax.shard_map(
        partial(local, mesh.shape["rows"]),
        mesh=mesh,
        in_specs=placed,
        out_specs=(
            P("rows", None),
            P("rows", None),
            P(),
            P(),
            P(),
            P(),
            P(),
            P(),
            P(None, "rows"),
            P("rows", None),
        ),
        check_vma=False,
    )
```

```python
from functools import partial
import math

import jax
import jax.numpy as jnp
from jax import lax
from jax.experimental import pallas as pl
from jax.experimental.pallas import tpu as pltpu
from jax.sharding import PartitionSpec as P

HEADS = 12
HEAD = 64
WINDOW = 256
SHARE = 64
PIECE = 256
STRIP = 768
OUTPUT_TILE = 1024
FIRST_PART = 256

epsilon = 1e-05
score_factor = 1.0 / math.sqrt(HEAD)
masked_score = -3e38
root_half = math.sqrt(0.5)
root_two_pi = math.sqrt(2.0 / math.pi) * 0.5


def dot(left, right, left_dim=1, right_dim=0):
    return lax.dot_general(
        left, right, (((left_dim,), (right_dim,)), ((), ())), preferred_element_type=jnp.float32
    )


def cost(flops, transcendentals, bytes_accessed):
    return pl.CostEstimate(
        flops=flops // SHARE,
        transcendentals=transcendentals // SHARE,
        bytes_accessed=bytes_accessed // SHARE,
    )


def lane_masks(width):
    lanes = lax.broadcasted_iota(jnp.int32, (1, width), 1)
    return (lanes < HEAD, lanes >= HEAD)


def both_heads(rows):
    none = jnp.zeros_like(rows)
    return jnp.concatenate([jnp.where(lanes, rows, none) for lanes in lane_masks(2 * HEAD)], axis=0)


def one_head(rows):
    size = rows.shape[0] // 2
    return jnp.where(lane_masks(2 * HEAD)[0], rows[:size], rows[size:])


def columns(values):
    rows = values[0].shape[0]
    lanes = lax.broadcasted_iota(jnp.int32, (rows, 2 * HEAD), 1)
    block = jnp.zeros((rows, 2 * HEAD), jnp.float32)
    for lane, value in enumerate(values):
        block = jnp.where(lanes == lane, value, block)
    return block.astype(jnp.bfloat16)


def ones_block(rows):
    return jnp.ones((rows, 2 * HEAD), jnp.bfloat16)


def norm_rows(values):
    centre = jnp.mean(values, axis=-1, keepdims=True)
    centred = values - centre
    inverse = lax.rsqrt(jnp.mean(centred * centred, axis=-1, keepdims=True) + epsilon)
    return (centred * inverse, inverse)


def norm_rows_back(grad_norm, unit_rows, inverse, gain):
    grad_unit = grad_norm * gain
    grad_mean = jnp.mean(grad_unit, axis=-1, keepdims=True)
    grad_proj = jnp.mean(grad_unit * unit_rows, axis=-1, keepdims=True)
    return inverse * (grad_unit - grad_mean - unit_rows * grad_proj)


def column_sums(grad_norm, unit_rows):
    return jnp.concatenate(
        [
            jnp.sum(grad_norm * unit_rows, axis=0, keepdims=True),
            jnp.sum(grad_norm, axis=0, keepdims=True),
        ],
        axis=0,
    )


def shift_rows(count):
    taken = lax.broadcasted_iota(jnp.int32, (WINDOW, WINDOW + 16), 1)
    given = lax.broadcasted_iota(jnp.int32, (WINDOW, WINDOW + 16), 0) + count
    return jnp.where(taken == given, 1.0, 0.0).astype(jnp.bfloat16)


def project_kernel(
    context_ref,
    queries_ref,
    rows_ref,
    mask_ref,
    cotangent_ref,
    norms_ref,
    weight_ref,
    rolled_ref,
    norm_ref,
    query_ref,
    packed_ref,
    live_ref,
    dead_ref,
    upstream_ref,
    twice,
    present,
):
    step = pl.program_id(0)
    slots, width = rows_ref.shape

    @pl.when(step == 0)
    def _():
        context, queries = context_ref[0], queries_ref[0]
        start = pl.multiple_of(context // 16 * 16, 16)
        shifted = shift_rows(context - start)
        for half in (slice(0, slots), slice(slots, 2 * slots)):
            twice[half] = rows_ref[...]
        across = lax.broadcasted_iota(jnp.int32, (128, 128), 1)
        down = lax.broadcasted_iota(jnp.int32, (128, 128), 0)
        for group in range(slots // 128):
            kept = (across == down) & (mask_ref[group : group + 1] == 1)
            if group == 0:
                kept = kept | ((across == 0) & (down == 0))
            kept = jnp.where(kept, 1.0, 0.0).astype(jnp.bfloat16)
            marks = dot(kept, jnp.ones((128, 128), jnp.bfloat16)).astype(jnp.bfloat16)
            for first in (0, slots):
                present[first + group * 128 : first + (group + 1) * 128] = marks
        for first in range(0, slots, WINDOW):
            rows = dot(shifted, twice[pl.ds(start + first, WINDOW + 16), :])
            rolled_ref[first : first + WINDOW] = rows.astype(jnp.bfloat16)
            unit_rows = norm_rows(rows)[0]
            norm_ref[first : first + WINDOW] = (
                unit_rows * norms_ref[0:1] + norms_ref[1:2]
            ).astype(jnp.bfloat16)
            here = dot(shifted, present[pl.ds(start + first, WINDOW + 16), :])
            place = lax.broadcasted_iota(jnp.int32, here.shape, 0) + (first + context)
            place = jnp.where(place >= slots, place - slots, place)
            live_ref[first : first + WINDOW] = jnp.where(place < context + queries, here, 0.0)[:, 0:1]
            lanes = lax.broadcasted_iota(jnp.int32, here.shape, 1)
            if first > 0:
                known = (here > 0) & (place < context)
                split = lanes & (HEAD - 1)
                ones = jnp.where((split >= 1) & (split <= 3), 1.0, 0.0)
                dead = jnp.where((lanes == 0) & jnp.logical_not(known), masked_score, ones)
                dead_ref[first - WINDOW : first] = dead.astype(jnp.bfloat16)
            else:
                asked = jnp.where(place < context + queries, here, 0.0)[:, 0:1]
        twice[:slots] = cotangent_ref[...]
        near = jnp.minimum(start, slots - WINDOW - 16)
        near = pl.multiple_of(near, 16)
        upstream_ref[...] = dot(shift_rows(context - near), twice[pl.ds(near, WINDOW + 16), :]) * asked
        query_ref[...] = dot(norm_ref[:WINDOW], weight_ref[...]).astype(jnp.bfloat16)

    @pl.when(step > 0)
    def _():
        packed_ref[...] = dot(norm_ref[WINDOW:], weight_ref[...]).astype(jnp.bfloat16)


def project(context, queries, inputs, row_mask, cotangent, norms, w_qkv):
    slots, width = inputs.shape

    def fixed(shape):
        return pl.BlockSpec(shape, lambda j, at, more: (0, 0))

    whole = fixed((slots, width))
    outs = (
        ((slots, width), jnp.bfloat16),
        ((slots, width), jnp.bfloat16),
        ((WINDOW, width), jnp.bfloat16),
        ((slots - WINDOW, 2 * width), jnp.bfloat16),
        ((slots, 1), jnp.float32),
        ((slots - WINDOW, 128), jnp.bfloat16),
        ((WINDOW, width), jnp.float32),
    )
    specs = [fixed(shape) for shape, _ in outs]
    specs[3] = pl.BlockSpec((slots - WINDOW, width), lambda j, at, more: (0, jnp.maximum(j - 1, 0)))
    return pl.pallas_call(
        project_kernel,
        grid_spec=pltpu.PrefetchScalarGridSpec(
            num_scalar_prefetch=2,
            grid=(3,),
            in_specs=[
                whole,
                fixed((slots // 128, 128)),
                whole,
                fixed(norms.shape),
                pl.BlockSpec((width, width), lambda j, at, more: (0, j)),
            ],
            out_specs=specs,
            scratch_shapes=[
                pltpu.VMEM((2 * slots, width), jnp.bfloat16),
                pltpu.VMEM((2 * slots, 128), jnp.bfloat16),
            ],
        ),
        out_shape=[jax.ShapeDtypeStruct(shape, dtype) for shape, dtype in outs],
        cost_estimate=cost(
            flops=2 * slots * width * 2 * width,
            transcendentals=slots,
            bytes_accessed=14 * slots * width,
        ),
    )(context, queries, inputs, row_mask.reshape(slots // 128, 128), cotangent, norms, w_qkv)


def attend_kernel(
    keep_logs, query_ref, key_ref, value_ref, dead_ref, row_ref, rows_ref, wout_ref, *outs
):
    attended_ref, hidden_ref, unit_ref, inverse_ref = outs[:4]
    log_ref, attended = outs[-2:]
    step = pl.program_id(1)
    block = query_ref.shape[0]
    first_lane = columns([jnp.ones((2 * block, 1), jnp.float32)])
    queries = both_heads(query_ref[...] * jnp.bfloat16(score_factor))
    queries = jnp.concatenate([queries, first_lane], axis=1)
    keys = jnp.concatenate([key_ref[...], dead_ref[...]], axis=1)
    values = jnp.concatenate([value_ref[...], ones_block(key_ref.shape[0])], axis=1)
    scores = [dot(queries[k : k + PIECE], keys, 1, 1) for k in range(0, 2 * block, PIECE)]
    exponents = [
        jnp.exp(part - jnp.max(part, axis=-1, keepdims=True)).astype(jnp.bfloat16) for part in scores
    ]
    parts, totals = [], []
    for exponent in exponents:
        summed = dot(exponent, values)
        totals.append(summed[:, 2 * HEAD :])
        parts.append(summed[:, : 2 * HEAD] / summed[:, 2 * HEAD :])
    if keep_logs:
        logs = [
            jnp.max(part, axis=-1, keepdims=True) + jnp.log(total) for part, total in zip(scores, totals)
        ]
        log_ref[...] = one_head(jnp.concatenate(logs, axis=0))
    both = one_head(jnp.concatenate(parts, axis=0))
    both = jnp.where(row_ref[...] > 0, both, 0.0).astype(jnp.bfloat16)
    attended_ref[...] = both
    attended[:, pl.ds(pl.multiple_of(step * 2 * HEAD, 2 * HEAD), 2 * HEAD)] = both

    @pl.when(step == pl.num_programs(1) - 1)
    def _():
        hidden = rows_ref[...].astype(jnp.float32) + dot(attended[...], wout_ref[...])
        hidden_ref[...] = hidden
        unit_ref[...], inverse_ref[...] = norm_rows(hidden)


def attend(query_rows, packed_keys, key_dead, row_live, rows, w_out, from_query, from_row, keep_logs):
    slots, block, width = WINDOW, WINDOW, query_rows.shape[1]
    keys_len = packed_keys.shape[0]
    pairs = width // (2 * HEAD)
    whole = pl.BlockSpec((block, width), lambda r, p: (r, 0))
    return pl.pallas_call(
        partial(attend_kernel, keep_logs),
        grid=(slots // block, pairs),
        in_specs=[
            pl.BlockSpec((block, 2 * HEAD), lambda r, p: (from_query, p)),
            pl.BlockSpec((keys_len, 2 * HEAD), lambda r, p: (0, p)),
            pl.BlockSpec((keys_len, 2 * HEAD), lambda r, p: (0, pairs + p)),
            pl.BlockSpec((keys_len, 2 * HEAD), lambda r, p: (0, 0)),
            pl.BlockSpec((block, 1), lambda r, p: (from_row, 0)),
            pl.BlockSpec((block, width), lambda r, p: (from_row, 0)),
            pl.BlockSpec((width, width), lambda r, p: (0, 0)),
        ],
        out_specs=(
            pl.BlockSpec((block, 2 * HEAD), lambda r, p: (r, p)),
            whole,
            whole,
            pl.BlockSpec((block, 1), lambda r, p: (r, 0)),
            *([pl.BlockSpec((block, 2 * HEAD), lambda r, p: (r, p))] if keep_logs else ()),
        ),
        scratch_shapes=[pltpu.VMEM((block, width), jnp.bfloat16)],
        out_shape=(
            jax.ShapeDtypeStruct((slots, width), jnp.bfloat16),
            jax.ShapeDtypeStruct((slots, width), jnp.float32),
            jax.ShapeDtypeStruct((slots, width), jnp.float32),
            jax.ShapeDtypeStruct((slots, 1), jnp.float32),
            *([jax.ShapeDtypeStruct((slots, width), jnp.float32)] if keep_logs else ()),
        ),
        cost_estimate=cost(
            flops=4 * slots * keys_len * width * 4,
            transcendentals=slots * keys_len * HEADS,
            bytes_accessed=12 * slots * width + 4 * keys_len * width,
        ),
    )(query_rows, packed_keys, packed_keys, key_dead, row_live, rows, w_out)


def units_kernel(
    bits, at_ref, own_ref, got_ref, norms_ref, grad_ref, grad_got_ref, up_ref, down_ref, *outs
):
    keep_refs, act_ref, (own_grad, give_grad), (normed, upstream) = outs[:8], outs[8], outs[9:11], outs[11:]
    width = own_ref.shape[1]
    cut = FIRST_PART

    @pl.when(pl.program_id(0) == 0)
    def _():
        for first, part, grad in ((0, own_ref, grad_ref), (WINDOW, got_ref, grad_got_ref)):
            rows = part[...] * norms_ref[2:3] + norms_ref[3:4]
            normed[first : first + WINDOW] = rows.astype(jnp.bfloat16)
            upstream[first : first + WINDOW] = grad[...].astype(jnp.bfloat16)

    tile = up_ref.shape[1]
    acts, pres = [], []
    for first in range(0, tile, STRIP):
        strip = slice(first, first + STRIP)
        pre_act = dot(normed[...], up_ref[:, strip])
        share = gelu_parts(pre_act)
        acts.append((pre_act * share).astype(jnp.bfloat16))
        slope = share + pre_act * (root_two_pi * jnp.exp(-0.5 * pre_act * pre_act))
        pres.append((dot(upstream[...], down_ref[strip], 1, 1) * slope).astype(jnp.bfloat16))
    act_ref[...] = jnp.concatenate(acts, axis=1)
    grad_pre = jnp.concatenate(pres, axis=1)
    part = dot(grad_pre, up_ref[...], 1, 1)

    @pl.when(pl.program_id(0) == 0)
    def _():
        own_grad[...], give_grad[...] = part[:WINDOW], part[WINDOW:]

    @pl.when(pl.program_id(0) > 0)
    def _():
        own_grad[...] += part[:WINDOW]
        give_grad[...] += part[WINDOW:]

    for index, (lefts, right) in enumerate(((acts, upstream), (pres, normed))):
        product = jnp.concatenate([dot(left, right[...], 0, 0) for left in lefts], axis=0)
        mine = (at_ref[0] & bits[index]) != 0
        rows = keep_refs[4 * index].shape[1]
        product = product.reshape(-1, 2, rows, width)
        keep = jnp.where(mine, product[:, 1], product[:, 0])
        give = jnp.where(mine, product[:, 0], product[:, 1])
        for place, (low, high) in enumerate(((0, cut), (cut, width))):
            keep_refs[4 * index + 2 * place][...] = keep[:, :, low:high]
            keep_refs[4 * index + 2 * place + 1][...] = give[:, :, low:high]


def units(me, bits, rows, unit_own, unit_got, norms, upstream, upstream_got, w_up, w_down):
    width, hidden = w_up.shape
    half = hidden // 2
    tile = 8 * rows if 8 * rows >= 384 else 384
    tiles = half // tile
    whole = pl.BlockSpec((WINDOW, width), lambda j, at: (0, 0))
    pieces, shapes = [], []
    for index in range(2):
        size = 2 * rows * (index + 1)
        for span in (FIRST_PART, FIRST_PART, width - FIRST_PART, width - FIRST_PART):
            pieces.append(pl.BlockSpec((tile // (2 * size), size, span), lambda j, at: (j, 0, 0)))
            shapes.append(jax.ShapeDtypeStruct((half // (2 * size), size, span), jnp.float32))
    acts = pl.BlockSpec((2 * WINDOW, tile), lambda j, at: (0, j))
    return pl.pallas_call(
        partial(units_kernel, bits),
        grid_spec=pltpu.PrefetchScalarGridSpec(
            num_scalar_prefetch=1,
            grid=(tiles,),
            in_specs=[
                whole,
                whole,
                pl.BlockSpec(norms.shape, lambda j, at: (0, 0)),
                whole,
                whole,
                pl.BlockSpec((width, tile), lambda j, at: (0, (at[0] & 1) * tiles + j)),
                pl.BlockSpec((tile, width), lambda j, at: ((at[0] & 1) * tiles + j, 0)),
            ],
            out_specs=(*pieces, acts, whole, whole),
            scratch_shapes=[
                pltpu.VMEM((2 * WINDOW, width), jnp.bfloat16),
                pltpu.VMEM((2 * WINDOW, width), jnp.bfloat16),
            ],
        ),
        out_shape=(
            *shapes,
            jax.ShapeDtypeStruct((2 * WINDOW, half), jnp.bfloat16),
            jax.ShapeDtypeStruct((WINDOW, width), jnp.float32),
            jax.ShapeDtypeStruct((WINDOW, width), jnp.float32),
        ),
        cost_estimate=cost(
            flops=16 * WINDOW * width * half,
            transcendentals=4 * WINDOW * half,
            bytes_accessed=12 * width * half,
        ),
    )(
        me.reshape(1),
        unit_own,
        unit_got,
        norms,
        upstream,
        upstream_got,
        w_up,
        w_down,
    )


def halves_kernel(right_dim, at_ref, left_ref, right_ref, own_ref, give_ref):
    product = dot(left_ref[...], right_ref[...], 1, right_dim)
    own_ref[...], give_ref[...] = product[:WINDOW], product[WINDOW:]


def halves(me, left, right, right_dim):
    rows, half = left.shape
    width = right.shape[1 - right_dim]
    tile = 256
    if right_dim == 1:
        spec = pl.BlockSpec((tile, half), lambda j, at: (j, at[0] & 1))
    else:
        spec = pl.BlockSpec((half, tile), lambda j, at: (at[0] & 1, j))
    out = pl.BlockSpec((WINDOW, tile), lambda j, at: (0, j))
    return pl.pallas_call(
        partial(halves_kernel, right_dim),
        grid_spec=pltpu.PrefetchScalarGridSpec(
            num_scalar_prefetch=1,
            grid=(width // tile,),
            in_specs=[pl.BlockSpec((rows, half), lambda j, at: (0, 0)), spec],
            out_specs=(out, out),
        ),
        out_shape=(jax.ShapeDtypeStruct((WINDOW, width), jnp.float32),) * 2,
        cost_estimate=cost(
            flops=2 * rows * width * half, transcendentals=0, bytes_accessed=4 * width * half
        ),
    )(me.reshape(1), left, right)


def attend_back_kernel(
    query_ref,
    key_ref,
    value_ref,
    dead_ref,
    row_ref,
    attended_ref,
    log_ref,
    own_ref,
    got_ref,
    unit_ref,
    inverse_ref,
    norms_ref,
    upstream_ref,
    wout_ref,
    dq_ref,
    dk_ref,
    dv_ref,
    grad_hidden_ref,
    low_ref,
    sums_ref,
):
    @pl.when(pl.program_id(0) == 0)
    def _():
        grad_norm = own_ref[...] + got_ref[...]
        unit_rows = unit_ref[...]
        sums_ref[...] = column_sums(grad_norm, unit_rows)
        grad_rows = norm_rows_back(grad_norm, unit_rows, inverse_ref[...], norms_ref[2:3])
        grad_hidden = upstream_ref[...] + grad_rows
        grad_hidden_ref[...] = grad_hidden
        low_ref[...] = grad_hidden.astype(jnp.bfloat16)

    block = query_ref.shape[0]
    key_rows = key_ref[...]
    grad = dot(low_ref[...], wout_ref[...], 1, 1)
    grad = jnp.where(row_ref[...] > 0, grad, 0.0).astype(jnp.bfloat16)
    product = grad.astype(jnp.float32) * attended_ref[...].astype(jnp.float32)
    grads = both_heads(grad)
    grads_wide = jnp.concatenate([grads, both_heads((-product).astype(jnp.bfloat16))], axis=1)
    values_wide = jnp.concatenate([value_ref[...], ones_block(key_rows.shape[0])], axis=1)
    lanes = lax.broadcasted_iota(jnp.int32, (block, 2 * HEAD), 1)
    rest = -log_ref[...]
    extra = jnp.zeros((block, 2 * HEAD), jnp.float32)
    for lane in range(1, 4):
        part = rest.astype(jnp.bfloat16).astype(jnp.float32)
        rest = rest - part
        extra = jnp.where((lanes & (HEAD - 1)) == lane, part, extra)
    extra = both_heads(extra)
    wide_lanes = lax.broadcasted_iota(jnp.int32, (2 * block, 2 * HEAD), 1)
    extra = jnp.where(wide_lanes == 0, 1.0, extra).astype(jnp.bfloat16)
    queries = both_heads(query_ref[...] * jnp.bfloat16(score_factor))
    queries_wide = jnp.concatenate([queries, extra], axis=1)
    keys_wide = jnp.concatenate([key_rows, dead_ref[...]], axis=1)
    pieces = [slice(k, k + PIECE) for k in range(0, 2 * block, PIECE)]
    probs = [jnp.exp(dot(queries_wide[piece], keys_wide, 1, 1)) for piece in pieces]
    grad_scores = [
        (prob * dot(grads_wide[piece], values_wide, 1, 1)).astype(jnp.bfloat16)
        for prob, piece in zip(probs, pieces)
    ]
    probs = jnp.concatenate([prob.astype(jnp.bfloat16) for prob in probs], axis=0)
    grad_scores = jnp.concatenate(grad_scores, axis=0)
    dq_ref[...] = (one_head(dot(grad_scores, key_rows)) * score_factor).astype(jnp.bfloat16)
    dk_ref[...] = dot(grad_scores, queries, 0, 0).astype(jnp.bfloat16)
    dv_ref[...] = dot(probs, grads, 0, 0).astype(jnp.bfloat16)


def attend_back(
    query_rows, packed_keys, key_dead, row_live, attended, logs, own, got, unit, inverse, norms, upstream, w_out
):
    slots, width = query_rows.shape
    keys_len = packed_keys.shape[0]
    pairs = width // (2 * HEAD)
    rows_spec = pl.BlockSpec((slots, 2 * HEAD), lambda p: (0, p))
    keys_spec = pl.BlockSpec((keys_len, 2 * HEAD), lambda p: (0, p))
    whole = pl.BlockSpec((slots, width), lambda p: (0, 0))
    column = pl.BlockSpec((slots, 1), lambda p: (0, 0))
    return pl.pallas_call(
        attend_back_kernel,
        grid=(pairs,),
        in_specs=[
            rows_spec,
            keys_spec,
            pl.BlockSpec((keys_len, 2 * HEAD), lambda p: (0, pairs + p)),
            pl.BlockSpec((keys_len, 2 * HEAD), lambda p: (0, 0)),
            column,
            rows_spec,
            rows_spec,
            whole,
            whole,
            whole,
            column,
            pl.BlockSpec(norms.shape, lambda p: (0, 0)),
            whole,
            pl.BlockSpec((2 * HEAD, width), lambda p: (p, 0)),
        ],
        out_specs=(
            rows_spec,
            keys_spec,
            keys_spec,
            whole,
            whole,
            pl.BlockSpec((2, width), lambda p: (0, 0)),
        ),
        out_shape=(
            jax.ShapeDtypeStruct((slots, width), jnp.bfloat16),
            jax.ShapeDtypeStruct((keys_len, width), jnp.bfloat16),
            jax.ShapeDtypeStruct((keys_len, width), jnp.bfloat16),
            jax.ShapeDtypeStruct((slots, width), jnp.float32),
            jax.ShapeDtypeStruct((slots, width), jnp.bfloat16),
            jax.ShapeDtypeStruct((2, width), jnp.float32),
        ),
        cost_estimate=cost(
            flops=10 * slots * keys_len * width * 4,
            transcendentals=slots * keys_len * HEADS,
            bytes_accessed=6 * slots * width + 8 * keys_len * width,
        ),
    )(
        query_rows,
        packed_keys,
        packed_keys,
        key_dead,
        row_live,
        attended,
        logs,
        own,
        got,
        unit,
        inverse,
        norms,
        upstream,
        w_out,
    )


def weights_kernel(
    at_ref, norm_ref, attended_ref, dq_ref, dk_ref, dv_ref, low_ref, keep_a, keep_b, give_a, give_b
):
    for odd, (even_a, even_b, odd_a, odd_b) in (
        (0, (keep_a, keep_b, give_a, give_b)),
        (1, (give_a, give_b, keep_a, keep_b)),
    ):

        @pl.when((at_ref[0] & 1) == odd)
        def _(even_a=even_a, even_b=even_b, odd_a=odd_a, odd_b=odd_b):
            even_a[...] = dot(norm_ref[:WINDOW], dq_ref[...], 0, 0)
            odd_a[...] = dot(norm_ref[WINDOW:], dk_ref[...], 0, 0)
            odd_b[...] = dot(norm_ref[WINDOW:], dv_ref[...], 0, 0)
            even_b[...] = dot(attended_ref[...], low_ref[...], 0, 0)


def weights(me, normed, attended, dq, dk, dv, low):
    slots, width = normed.shape
    tile = 256

    def full(value):
        return pl.BlockSpec(value.shape, lambda j, at: (0, 0))

    out = pl.BlockSpec((tile, width), lambda j, at: (j, 0))
    return pl.pallas_call(
        weights_kernel,
        grid_spec=pltpu.PrefetchScalarGridSpec(
            num_scalar_prefetch=1,
            grid=(width // tile,),
            in_specs=[
                pl.BlockSpec((slots, tile), lambda j, at: (0, j)),
                pl.BlockSpec((WINDOW, tile), lambda j, at: (0, j)),
                full(dq),
                full(dk),
                full(dv),
                full(low),
            ],
            out_specs=(out,) * 4,
        ),
        out_shape=(jax.ShapeDtypeStruct((width, width), jnp.float32),) * 4,
        cost_estimate=cost(
            flops=4 * slots * width * width, transcendentals=0, bytes_accessed=20 * width * width
        ),
    )(me.reshape(1), normed, attended, dq, dk, dv, low)


def rows_back_kernel(dq_ref, dk_ref, dv_ref, rows_ref, hidden_ref, norms_ref, wq, wk, wv, out_ref, sums_ref):
    step = pl.program_id(0)
    unit_rows, inverse = norm_rows(rows_ref[...].astype(jnp.float32))

    def finish(grad_norm):
        sums = column_sums(grad_norm, unit_rows)
        return (norm_rows_back(grad_norm, unit_rows, inverse, norms_ref[0:1]), sums)

    @pl.when(step == 0)
    def _():
        grad_rows, sums = finish(dot(dq_ref[...], wq[...], 1, 1))
        out_ref[...] = grad_rows + hidden_ref[...]
        sums_ref[...] = sums

    @pl.when(step > 0)
    def _():
        grad_rows, sums = finish(dot(dk_ref[...], wk[...], 1, 1) + dot(dv_ref[...], wv[...], 1, 1))
        out_ref[...] = grad_rows
        sums_ref[...] += sums


def rows_back(dq, dk, dv, rows, grad_hidden, norms, w_qkv):
    slots, width = rows.shape
    fixed = pl.BlockSpec((WINDOW, width), lambda r: (0, 0))
    keys = pl.BlockSpec((WINDOW, width), lambda r: (jnp.maximum(r - 1, 0), 0))
    tile = pl.BlockSpec((WINDOW, width), lambda r: (r, 0))
    return pl.pallas_call(
        rows_back_kernel,
        grid=(slots // WINDOW,),
        in_specs=[
            fixed,
            keys,
            keys,
            tile,
            fixed,
            pl.BlockSpec(norms.shape, lambda r: (0, 0)),
            pl.BlockSpec((width, width), lambda r: (0, 0)),
            pl.BlockSpec((width, width), lambda r: (0, 1)),
            pl.BlockSpec((width, width), lambda r: (0, 2)),
        ],
        out_specs=(tile, pl.BlockSpec((2, width), lambda r: (0, 0))),
        out_shape=(
            jax.ShapeDtypeStruct((slots, width), jnp.float32),
            jax.ShapeDtypeStruct((2, width), jnp.float32),
        ),
        cost_estimate=cost(
            flops=4 * slots * width * width, transcendentals=slots, bytes_accessed=12 * slots * width
        ),
    )(dq, dk, dv, rows, grad_hidden, norms, w_qkv, w_qkv, w_qkv)


def place_kernel(bits, far, got, me_ref, factor_ref, a_ref, b_ref, *refs):
    qkv_ref, out_ref, a_wide, b_wide, semaphores = refs[-5:]
    size, width = a_ref.shape
    me = me_ref[0]
    a_wide[...] = a_ref[...] * factor_ref[0, 0]
    b_wide[...] = b_ref[...] * factor_ref[0, 0]
    odd = (me & 1) != 0
    rows = []
    for bit in bits:
        high = (me & bit) != 0
        rows.append(jnp.where(high, 0 if far else size, size if far else 0))
    rows_a, rows_b = (pl.ds(pl.multiple_of(row, size), size) for row in rows)

    def place(targets):
        copies = [
            pltpu.make_async_copy(source, target, semaphores.at[index])
            for index, (source, target) in enumerate(zip((a_wide, b_wide), targets))
        ]
        for copy in copies:
            copy.start()
        for copy in copies:
            copy.wait()

    @pl.when(odd == got)
    def _():
        place((qkv_ref.at[rows_a, pl.ds(0, width)], out_ref.at[rows_b]))

    @pl.when(odd != got)
    def _():
        place((qkv_ref.at[rows_a, pl.ds(width, width)], qkv_ref.at[rows_b, pl.ds(2 * width, width)]))


def put(me, bits, far, got, factor, pieces, held):
    size, width = pieces[0].shape
    scalar = pl.BlockSpec(memory_space=pltpu.SMEM)
    anywhere = pl.BlockSpec(memory_space=pl.ANY)
    vmem = pl.BlockSpec(memory_space=pltpu.VMEM)
    operands = [*pieces, *(held or ())]
    return pl.pallas_call(
        partial(place_kernel, bits, far, got),
        in_specs=[scalar, scalar, vmem, vmem] + [anywhere] * (2 if held else 0),
        out_specs=(anywhere, anywhere),
        out_shape=(
            jax.ShapeDtypeStruct((2 * size, 3 * width), jnp.float32),
            jax.ShapeDtypeStruct((2 * size, width), jnp.float32),
        ),
        scratch_shapes=[
            pltpu.VMEM((size, width), jnp.float32),
            pltpu.VMEM((size, width), jnp.float32),
            pltpu.SemaphoreType.DMA((2,)),
        ],
        input_output_aliases={4: 0, 5: 1} if held else {},
        cost_estimate=cost(flops=0, transcendentals=0, bytes_accessed=8 * width * width),
    )(me.reshape(1), factor, *operands)


def output_kernel(
    at_ref, *refs
):
    units, hiddens, (own_ref, got_ref, base_ref, norms_ref, up_ref, down_ref) = refs[:3], refs[3:6], refs[6:12]
    out_ref, normed, total, twice = refs[12:]
    step = pl.program_id(0)
    slots, width = out_ref.shape

    @pl.when(step == 0)
    def _():
        for index in range(3):
            rows = slice(index * WINDOW, (index + 1) * WINDOW)
            normed[rows] = (units[index][...] * norms_ref[2:3] + norms_ref[3:4]).astype(jnp.bfloat16)
            total[rows] = hiddens[index][...]

    acts = []
    for first in range(0, up_ref.shape[1], 512):
        pre_act = dot(normed[...], up_ref[:, first : first + 512])
        acts.append((pre_act * gelu_parts(pre_act)).astype(jnp.bfloat16))
    total[...] += dot(jnp.concatenate(acts, axis=1), down_ref[...])

    @pl.when(step == pl.num_programs(0) - 1)
    def _():
        window = (base_ref[...] + (own_ref[...] + got_ref[...])).astype(jnp.bfloat16)
        rest = total[...].astype(jnp.bfloat16)
        for first in (0, slots):
            twice[first : first + WINDOW] = window
            twice[first + WINDOW : first + slots] = rest
        begin = slots - at_ref[0]
        start = pl.multiple_of(begin // 16 * 16, 16)
        shifted = shift_rows(begin - start)
        for first in range(0, slots, WINDOW):
            rows = dot(shifted, twice[pl.ds(start + first, WINDOW + 16), :])
            out_ref[first : first + WINDOW] = rows.astype(jnp.bfloat16)


def output(context, units, hiddens, own, got, base, norms, w_up, w_down):
    width, hidden = w_up.shape
    slots = 4 * WINDOW
    tile = OUTPUT_TILE
    part = pl.BlockSpec((WINDOW, width), lambda j, at: (0, 0))
    return pl.pallas_call(
        output_kernel,
        grid_spec=pltpu.PrefetchScalarGridSpec(
            num_scalar_prefetch=1,
            grid=(hidden // tile,),
            in_specs=[part] * 9
            + [
                pl.BlockSpec(norms.shape, lambda j, at: (0, 0)),
                pl.BlockSpec((width, tile), lambda j, at: (0, j)),
                pl.BlockSpec((tile, width), lambda j, at: (j, 0)),
            ],
            out_specs=pl.BlockSpec((slots, width), lambda j, at: (0, 0)),
            scratch_shapes=[
                pltpu.VMEM((slots - WINDOW, width), jnp.bfloat16),
                pltpu.VMEM((slots - WINDOW, width), jnp.float32),
                pltpu.VMEM((2 * slots + 16, width), jnp.bfloat16),
            ],
        ),
        out_shape=jax.ShapeDtypeStruct((slots, width), jnp.bfloat16),
        cost_estimate=pl.CostEstimate(
            flops=12 * WINDOW * width * hidden,
            transcendentals=3 * WINDOW * hidden,
            bytes_accessed=8 * width * hidden,
        ),
    )(context, *units, *hiddens, own, got, base, norms, w_up, w_down)


def gelu_parts(values):
    share = 0.5 * (1.0 + lax.erf(values * root_half))
    return share


def local(
    devices,
    inputs,
    context_count,
    query_count,
    row_mask,
    ln1_gain,
    ln1_bias,
    w_qkv,
    w_out,
    ln2_gain,
    ln2_bias,
    w_up,
    w_down,
    cotangent,
):
    slots, width = inputs.shape
    hidden = w_up.shape[1]
    half = hidden // 2
    me = lax.axis_index("rows")
    core = me & 1

    def bit_of(bit):
        return ((me & bit) != 0).astype(jnp.int32)

    def swap(value, bit):
        return lax.ppermute(value, "rows", [(i, i ^ bit) for i in range(devices)])

    def pick(value, axis, index):
        return lax.dynamic_index_in_dim(value, index, axis, keepdims=False)

    bits = []
    bit = 2
    while bit < devices:
        bits.append(bit)
        bit *= 2
    top = bits[-1]

    def order_of(list_of_bits, flip):
        if flip and len(list_of_bits) > 1:
            return [list_of_bits[1], list_of_bits[0]] + list_of_bits[2:]
        return list_of_bits

    context = context_count[0]
    queries = query_count[0]
    norms = jnp.concatenate([ln1_gain, ln1_bias, ln2_gain, ln2_bias]).reshape(4, width)
    tie = lax.optimization_barrier
    rows, normed_low, query_window, packed_keys, row_column, key_dead, upstream = project(
        context_count, query_count, inputs, row_mask, cotangent, norms, w_qkv
    )
    upstream_got = swap(upstream, 1)
    attended_q, hidden_q, unit_two, inverse_two, log_sums = attend(
        query_window, packed_keys, key_dead, row_column, rows, w_out, 0, 0, True
    )
    ff_rows = half // (devices // 2)
    ff_bits = bits[:-1]
    pieces = units(
        me,
        bits[:2],
        ff_rows,
        unit_two,
        swap(unit_two, 1),
        norms,
        upstream,
        upstream_got,
        w_up,
        w_down,
    )
    activated, grad_own, grad_give = pieces[8:]
    pieces = pieces[:8]
    first_bits, second_bits = order_of(bits, False), order_of(bits, True)

    class Halving:
        def __init__(self, terms, axes):
            self.terms, self.axes = terms, list(axes)

        def split(self, bit):
            axis = self.axes.index(bit)
            mine = bit_of(bit)
            self.axes.remove(bit)
            self.kept = sum(pick(term, axis, mine) for term in self.terms)
            self.sent = sum(pick(term, axis, 1 - mine) for term in self.terms)

        def go(self, bit):
            self.terms = [self.kept, swap(self.sent, bit)]

        def send(self, bit):
            self.split(bit)
            self.go(bit)

    def got_of(chains):
        return tuple(chain.terms[1] for chain in chains)

    def set_got(chains, values):
        for chain, value in zip(chains, values):
            chain.terms[1] = value

    def feed_forward(index, place):
        keep, give = pieces[4 * index + 2 * place : 4 * index + 2 * place + 2]
        axes = ff_bits[::-1] + [1]
        axes.remove(ff_order[index][0])
        shape = [2] * len(axes) + [ff_rows, keep.shape[-1]]
        got = swap(give, ff_order[index][0])
        return Halving([keep.reshape(shape), got.reshape(shape)], axes)

    def to_top(chain):
        pairs = [(i, i ^ top) for i in range(devices) if ((i & top) != 0) != ((i & 1) != 0)]
        value = chain.terms[0] + chain.terms[1]
        chain.terms = [value, lax.ppermute(value, "rows", pairs)]

    def hand_over(chain):
        mine = sum(pick(term, 1, core) for term in chain.terms)
        other = swap(sum(pick(term, 1, 1 - core) for term in chain.terms), 1)
        return jnp.where(bit_of(top) == core, mine, other)

    ff_order = (order_of(ff_bits, False), order_of(ff_bits, True))

    down_one = feed_forward(0, 0)
    up_one = feed_forward(1, 0)
    ones = (down_one, up_one)

    grad_query, grad_key, grad_value, grad_hidden, grad_low, sums_two = attend_back(
        query_window,
        packed_keys,
        key_dead,
        row_column,
        attended_q,
        log_sums,
        grad_own,
        swap(grad_give, 1),
        unit_two,
        inverse_two,
        norms,
        upstream,
        w_out,
    )
    keep_first, keep_second, *give = weights(
        me, normed_low, attended_q, grad_query, grad_key, grad_value, grad_low
    )

    def unroll(value):
        return lax.dynamic_slice(
            jnp.concatenate([value, value], axis=0), (slots - context, 0), (slots, width)
        )

    def joined(chains):
        terms = [jnp.stack([c.terms[k] for c in chains]) for k in range(2)]
        return Halving(terms, [None] + chains[0].axes)

    ones_got, give = tie((got_of(ones), give))
    set_got(ones, ones_got)
    for chain, order in zip(ones, ff_order):
        chain.send(order[1])
    give_first, give_second = swap(give[0], 1), swap(give[1], 1)
    shape = [2] * len(bits) + [width // (2 ** len(bits)), width]
    first = Halving([keep_first.reshape(shape), give_first.reshape(shape)], first_bits)
    second = Halving([keep_second.reshape(shape), give_second.reshape(shape)], second_bits)
    both = (first, second)

    first.split(first_bits[0])
    second.split(second_bits[0])
    first.sent, second.sent, grad_query, grad_key, grad_value, ones_got = tie(
        (first.sent, second.sent, grad_query, grad_key, grad_value, got_of(ones))
    )
    set_got(ones, ones_got)
    first.go(first_bits[0])
    second.go(second_bits[0])
    ones = joined(ones)
    for bit in ff_bits[2:]:
        ones.send(bit)
    to_top(ones)
    grad_query, _ = tie((grad_query, ones.terms[0]))
    grad_rows, sums_one = rows_back(
        grad_query, grad_key, grad_value, rows, grad_hidden, norms, w_qkv
    )
    context_norms, _ = tie((normed_low[WINDOW:], grad_rows))
    context_queries = dot(context_norms, w_qkv[:, :width]).astype(jnp.bfloat16)

    def context_part(index, queries):
        return attend(
            queries, packed_keys, key_dead, row_column, rows, w_out, index, index + 1, False
        )[1:3]

    out_own, out_give = halves(me, activated, w_down, 0)
    out_give = swap(out_give, 1)
    both_got, ones_got, context_queries, sums_one, out_own, out_give = tie(
        (got_of(both), ones.terms[1], context_queries, sums_one, out_own, out_give)
    )
    set_got(both, both_got)
    ones.terms[1] = ones_got

    first.split(first_bits[1])
    second.split(second_bits[1])
    first.sent, second.sent, ones.terms, sums_one, context_queries = tie(
        (first.sent, second.sent, ones.terms, sums_one, context_queries)
    )
    first.go(first_bits[1])
    second.go(second_bits[1])
    small = jnp.concatenate(
        [sums_one, sums_two, jnp.full((4, width), queries, jnp.float32)], axis=0
    )
    small = small + swap(small, 1)
    small = small + swap(small, bits[0])
    part_one = context_part(0, context_queries)
    both_got, small, context_queries, part_one, pieces = tie(
        (got_of(both), small, context_queries, part_one, pieces)
    )
    set_got(both, both_got)
    down_two = feed_forward(0, 1)
    up_two = feed_forward(1, 1)
    twos = (down_two, up_two)

    both = joined(both)
    for bit in bits[2:-1]:
        both.send(bit)
    for bit in bits[2:-1]:
        small = small + swap(small, bit)
    part_two = context_part(1, context_queries)
    both_got, small, part_two, context_queries = tie(
        (both.terms[1], small, part_two, context_queries)
    )
    both.terms[1] = both_got

    value = both.terms[0] + both.terms[1]
    value, context_queries = tie((value, context_queries))
    value_got = swap(value, top)
    part_three = context_part(2, context_queries)
    small, part_three, twos_got = tie((small, part_three, got_of(twos)))
    set_got(twos, twos_got)
    small = small + swap(small, bits[1])
    span = (width - FIRST_PART) // 2
    early, late = (
        [
            Halving([term[..., first : first + span] for term in chain.terms], chain.axes)
            for chain in twos
        ]
        for first in (0, span)
    )
    for chain, order in zip(early, ff_order):
        chain.split(order[1])
    early[0].sent, early[1].sent, small = tie((early[0].sent, early[1].sent, small))
    for chain, order in zip(early, ff_order):
        chain.go(order[1])
    for chain, order in zip(late, ff_order):
        chain.split(order[1])
    sent = (late[0].sent, late[1].sent)
    _, early_got, value_got, small, part_two, part_three, ones.terms, grad_rows = tie(
        (sent, got_of(early), value_got, small, part_two, part_three, ones.terms, grad_rows)
    )
    set_got(early, early_got)
    value = value + value_got

    def widen(value, bit, axis):
        got = swap(value, bit)
        high = bit_of(bit) == 1
        return jnp.stack(
            [jnp.where(high, got, value), jnp.where(high, value, got)], axis=axis
        )

    for bit in bits[2:-1][::-1]:
        value = widen(value, bit, 1)
    for chain, order in zip(late, ff_order):
        chain.go(order[1])
    ones = hand_over(ones)
    small = small + swap(small, top)
    early = joined(early)
    for bit in ff_bits[2:3]:
        early.split(bit)
        early.sent, small = tie((early.sent, small))
        early.go(bit)
    value, small, ones, part_one, late_got = tie((value, small, ones, part_one, got_of(late)))
    set_got(late, late_got)
    late = joined(late)
    loss_factor = math.sqrt(devices) * (slots // 4) / small[4, 0]
    factor = loss_factor.reshape(1, 1)

    first_value = widen(value[0], first_bits[1], 0)
    second_value = widen(value[1], second_bits[1], 0)
    for bit in ff_bits[2:3]:
        late.send(bit)
    for bit in ff_bits[3:]:
        early.send(bit)
        late.send(bit)
    grad_inputs = unroll(grad_rows * loss_factor)
    small = small * loss_factor
    first_value, second_value, grad_inputs, small, part_one, early.terms, late.terms = tie(
        (first_value, second_value, grad_inputs, small, part_one, early.terms, late.terms)
    )
    terms = [jnp.concatenate(pair, axis=0) for pair in zip(early.terms, late.terms)]
    twos = Halving(terms, early.axes)

    first_value, second_value = first_value.reshape(-1, width), second_value.reshape(-1, width)
    first_far = swap(first_value, first_bits[0])
    second_far = swap(second_value, second_bits[0])
    first_near = swap(first_value, 1)
    second_near = swap(second_value, 1)
    to_top(twos)
    hiddens, units_c = zip(part_one, part_two, part_three)
    layer_out = output(
        context_count, units_c, hiddens, out_own, out_give, hidden_q, norms, w_up, w_down
    )
    ends = (first_bits[0], second_bits[0])
    held = put(me, ends, False, False, factor, (first_value, second_value), None)
    held = put(me, ends, False, True, factor, (first_near, second_near), held)
    first_far, second_far, twos_got, held, layer_out = tie(
        (first_far, second_far, twos.terms[1], held, layer_out)
    )
    twos.terms[1] = twos_got

    first_got = swap(first_far, 1)
    second_got = swap(second_far, 1)
    twos = hand_over(twos)
    down_share = loss_factor * jnp.concatenate([ones[0], twos[0], twos[2]], axis=1)
    up_share = loss_factor * jnp.concatenate([ones[1], twos[1], twos[3]], axis=1).T
    held = put(me, ends, True, False, factor, (first_far, second_far), held)
    grad_qkv, grad_out = put(me, ends, True, True, factor, (first_got, second_got), held)
    return (
        layer_out,
        grad_inputs,
        small[0],
        small[1],
        grad_qkv,
        grad_out,
        small[2],
        small[3],
        up_share,
        down_share,
    )


def solution(mesh):
    placed = (
        P("rows", None),
        P("rows"),
        P("rows"),
        P("rows"),
        P(),
        P(),
        P(),
        P(),
        P(),
        P(),
        P(),
        P(),
        P("rows", None),
    )
    return jax.shard_map(
        partial(local, mesh.shape["rows"]),
        mesh=mesh,
        in_specs=placed,
        out_specs=(
            P("rows", None),
            P("rows", None),
            P(),
            P(),
            P(),
            P(),
            P(),
            P(),
            P(None, "rows"),
            P("rows", None),
        ),
        check_vma=False,
    )
```
